32 devices in a mesh: context: 4 (over x, core), tensor: 4 (over z), dp: 2 (over y).
Axes of the slice: x: 2, y: 2, z: 4, core: 2. Of those that a mesh axis runs over, the one named last changes fastest.
Arguments:
- queries: bfloat16 [1024, 64, 128], P(('dp', 'context'), 'tensor'), parts along dimension 0, may hold values from -160 to 160
- key_heads: bfloat16 [1024, 4, 128], P(('dp', 'context'), 'tensor'), parts along dimension 0, may hold values from -6 to 6
- value_heads: bfloat16 [1024, 4, 128], P(('dp', 'context'), 'tensor'), parts along dimension 0, may hold values from -6 to 6
- out_grad: bfloat16 [1024, 64, 128], P(('dp', 'context'), 'tensor'), parts along dimension 0, may hold values from -6 to 6
- layout: int32 [1024], P('dp'), parts along dimension 0, may hold values from 0 to 511, as said below
- documents: int32 [1024], P('dp'), parts along dimension 0, may hold values from 0 to 3, never falling along the last dimension, each value on 1 to 384 neighbouring positions
Outputs:
- output: bfloat16 [1024, 64, 128], P(('dp', 'context'), 'tensor'), parts along dimension 0
- query_grad: bfloat16 [1024, 64, 128], P(('dp', 'context'), 'tensor'), parts along dimension 0
- key_grad: float32 [1024, 512], P(('dp', 'context'), 'tensor'), parts along dimension 0
- value_grad: float32 [1024, 512], P(('dp', 'context'), 'tensor'), parts along dimension 0
The draws below stay inside these ranges and needn't reach their ends.
There are 2 independent parts, one for each index of `dp`. The reference program is written for one: setup_inputs(seed, part) draws one part's arguments, and reference() takes and returns one part's arrays. A program takes and returns all parts, laid end to end along the dimension named above; each array names one. Nothing has to cross between parts.
Inputs may be any that keep to these rules, and one draw needn't show every extreme that they name: `layout`: a permutation of the tokens made of aligned runs of 64 consecutive tokens; every device's rows are two such runs, in an order drawn from the seed.
All inputs are finite; a program needn't handle non-finite values.
Results may differ from the reference program's by a relative error of at most 0.0064.
Values may be sent and summed in bfloat16 or wider, within the bound.
A program may use at most 128 MiB of HBM per device.

```python
import math
import jax
import jax.numpy as jnp
import numpy as np
from jax import lax

HD = 128
GROUP = 16
KV_GROUPS = 4
TOK_DEV = 128
H = 64
SEQ = 512
DOCS = 4
DOC_MOST = 384
N_CONTEXT = 4


def paired_draw(key):
    key_seed = jax.random.fold_in(key, 101)
    query_seed = jax.random.fold_in(key, 202)
    key_vals = jnp.clip(jax.random.normal(key_seed, (SEQ, KV_GROUPS, HD), jnp.float32), -6.0, 6.0)
    query_vals = jnp.clip(jax.random.normal(query_seed, (SEQ, H, HD), jnp.float32), -6.0, 6.0)
    return (query_vals, key_vals)


def draw_queries(key, part):
    return paired_draw(key)[0].astype(jnp.bfloat16)


def draw_key_heads(key, part):
    return paired_draw(key)[1].astype(jnp.bfloat16)


def draw_layout(key, part):
    half_run = TOK_DEV // 2
    runs = jax.random.permutation(key, 2 * N_CONTEXT)
    return (runs[:, None] * half_run + jnp.arange(half_run, dtype=jnp.int32)[None, :]).reshape(-1).astype(jnp.int32)


def level_of(own_key, shape, cuts, low, high):
    def one(axis_at, shards_of):
        steps = jax.random.uniform(jax.random.fold_in(jax.random.fold_in(own_key, 6), axis_at), (shards_of,), jnp.float32, low / len(cuts), high / len(cuts))
        return jnp.repeat(jnp.exp(steps), shape[axis_at] // shards_of).reshape((-1,) + (1,) * (len(shape) - axis_at - 1))

    factor_of = one(*cuts[0])
    for cut in cuts[1:]:
        factor_of = factor_of * one(*cut)
    return factor_of


def length_profile(amount, total, bound, skew):
    weights = [(1 << 20) // math.isqrt(standing ** skew) + 1 for standing in range(2, amount + 1)]
    spare, given = total - bound - (amount - 1), [1] * (amount - 1)
    while spare > 0:
        free = [i for i in range(amount - 1) if given[i] < bound]
        pool, budget = sum([weights[i] for i in free]), spare
        for i in free:
            more = min(bound - given[i], max(1, budget * weights[i] // pool), spare)
            given[i] = given[i] + more
            spare = spare - more
    return np.array([bound] + given)


def ragged_sizes(key, count, total, limit, lean):
    if count == 2:
        one = jax.random.randint(key, (), max(1, total - limit), min(limit, total - 1) + 1)
        return jnp.stack([one, total - one])
    tallies = jnp.asarray(length_profile(count, total, limit, lean), jnp.int32)
    pairs = (count - 1) // 2
    donor, sink = tallies[1:1 + 2 * pairs:2], tallies[2:2 + 2 * pairs:2]
    margin = jnp.minimum(donor - 1, limit - sink)
    passed = jax.random.randint(jax.random.fold_in(key, 1), (pairs,), 0, 1 << 20) % (margin + 1)
    tallies = tallies.at[1:1 + 2 * pairs:2].set(donor - passed).at[2:2 + 2 * pairs:2].set(sink + passed)
    return tallies[jax.random.permutation(jax.random.fold_in(key, 2), count)]


def gaussian(stream_key, shape, scale, bound, cuts=(), kind=jnp.bfloat16):
    drawn = jax.random.normal(stream_key, shape, jnp.float32) * scale
    if len(cuts) > 0:
        drawn = level_of(stream_key, shape, cuts, -0.22, 0.18) * drawn
    return jnp.clip(drawn, min=-bound, max=bound).astype(kind)


def setup_inputs(seed: int = 0, part: int = 0) -> dict:
    streams_of = jax.random.split(jax.random.key(seed), 7)
    part_keys = jax.random.split(jax.random.fold_in(streams_of[6], part), 7)
    return {
        "queries": draw_queries(jax.random.fold_in(jax.random.fold_in(streams_of[6], part), 71), part),
        "key_heads": draw_key_heads(jax.random.fold_in(jax.random.fold_in(streams_of[6], part), 71), part),
        "value_heads": gaussian(part_keys[2], (SEQ, KV_GROUPS, HD), 1.0, 6.0, ((0, 4), (1, 4))),
        "out_grad": gaussian(part_keys[3], (SEQ, H, HD), 1.0, 6.0, ((0, 4), (1, 4))),
        "layout": draw_layout(jax.random.fold_in(jax.random.fold_in(streams_of[6], part), 71), part),
        "documents": jnp.searchsorted(jnp.cumsum(ragged_sizes(part_keys[5], DOCS, SEQ, DOC_MOST, 2)), jnp.arange(SEQ), side="right").astype(jnp.int32),
    }


THETA = 8000000.0

def rotary(source, places, direction):
    half_dim = source.shape[-1] // 2
    frequency = jnp.exp(-(2.0 * jnp.arange(half_dim, dtype=jnp.float32) / source.shape[-1]) * math.log(THETA))
    angles = places.astype(jnp.float32)[:, None] * frequency[None, :]
    cosine = jnp.cos(angles)[:, None, :]
    sine_part = direction * jnp.sin(angles)[:, None, :]
    first_half = source[..., :half_dim]
    second = source[..., half_dim:]
    return jnp.concatenate([first_half * cosine - second * sine_part, second * cosine + first_half * sine_part], axis=-1)

def doc_positions(documents):
    length = documents.shape[0]
    indices = jnp.arange(length, dtype=jnp.int32)
    starts_here = jnp.concatenate([jnp.ones((1,), dtype=bool), documents[1:] != documents[:-1]])
    firsts = lax.cummax(jnp.where(starts_here, indices, jnp.zeros_like(indices)), axis=0)
    return indices - firsts

def reference(queries, key_heads, value_heads, out_grad, layout, documents):
    positions = doc_positions(documents)
    places = jnp.take(positions, layout)
    doc_rows = jnp.take(documents, layout)
    scaling = 1.0 / math.sqrt(HD)
    query_rot = rotary(queries.astype(jnp.float32), places, 1.0).astype(jnp.bfloat16)
    key_rot = rotary(key_heads.astype(jnp.float32), places, 1.0).astype(jnp.bfloat16)
    allowed = (doc_rows[:, None] == doc_rows[None, :]) & (layout[None, :] <= layout[:, None])
    owners = np.arange(H) // GROUP
    query_heads = jnp.transpose(query_rot, (1, 0, 2))
    key_per_head = jnp.transpose(key_rot, (1, 0, 2))[owners]
    value_per_head = jnp.transpose(value_heads, (1, 0, 2))[owners]
    grad_heads = jnp.transpose(out_grad, (1, 0, 2))

    def one_head(operands):
        query_one, key_one, value_one, grad_one = operands
        scores = jnp.dot(query_one, key_one.T, preferred_element_type=jnp.float32) * scaling
        scores = jnp.where(allowed, scores, -1e+30)
        largest = lax.optimization_barrier(jnp.max(scores, axis=1, keepdims=True))
        weights = jnp.exp(scores - largest)
        attention = weights / lax.optimization_barrier(jnp.sum(weights, axis=1, keepdims=True))
        attention_b = attention.astype(jnp.bfloat16)
        result = jnp.dot(attention_b, value_one, preferred_element_type=jnp.float32).astype(jnp.bfloat16)
        dprobs = jnp.dot(grad_one, value_one.T, preferred_element_type=jnp.float32)
        row_delta = lax.optimization_barrier(jnp.sum(grad_one.astype(jnp.float32) * result.astype(jnp.float32), axis=1, keepdims=True))
        dscores = (attention * (dprobs - row_delta) * scaling).astype(jnp.bfloat16)
        return (result, jnp.dot(dscores, key_one, preferred_element_type=jnp.float32), jnp.dot(dscores.T, query_one, preferred_element_type=jnp.float32), jnp.dot(attention_b.T, grad_one, preferred_element_type=jnp.float32))
    results, query_rot_grad, key_rot_grad, value_terms = lax.map(one_head, (query_heads, key_per_head, value_per_head, grad_heads))
    output = jnp.transpose(results, (1, 0, 2))
    query_grad = rotary(jnp.transpose(query_rot_grad, (1, 0, 2)), places, -1.0).astype(jnp.bfloat16)
    key_sum = jnp.transpose(key_rot_grad.reshape(KV_GROUPS, GROUP, SEQ, HD).sum(axis=1), (1, 0, 2))
    key_grad = rotary(key_sum, places, -1.0).reshape(SEQ, KV_GROUPS * HD)
    value_grad = jnp.transpose(value_terms.reshape(KV_GROUPS, GROUP, SEQ, HD).sum(axis=1), (1, 0, 2)).reshape(SEQ, KV_GROUPS * HD)
    return (output, query_grad, key_grad, value_grad)
```

```python
import functools
import math

import jax
import jax.numpy as jnp
from jax import lax
from jax.experimental import pallas as pl
from jax.experimental.pallas import tpu as pltpu
from jax.sharding import PartitionSpec as P

THETA = 8000000.0
RUN = 64
MASKED = -1e30
MESH = pl.DeviceIdType.MESH
F32 = jnp.float32
BF16 = jnp.bfloat16


def dot(lhs, rhs, rhs_dim=0):
    return lax.dot_general(lhs, rhs, (((1,), (rhs_dim,)), ((), ())), preferred_element_type=F32)


def sine_cosine(x):
    turns = jnp.floor(x * (2.0 / math.pi) + 0.5)
    r = ((x - turns * 1.5703125) - turns * 4.837512969970703125e-4) - turns * 7.54978995489188216e-8
    z = r * r
    s = r + r * z * (-1.6666654611e-1 + z * (8.3321608736e-3 - z * 1.9515295891e-4))
    c = 1.0 - 0.5 * z + z * z * (4.166664568298827e-2 + z * (-1.388731625493765e-3 + z * 2.443315711809948e-5))
    quarter = turns.astype(jnp.int32)
    odd = (quarter & 1) == 1
    sine = jnp.where(odd, c, s)
    cosine = jnp.where(odd, s, c)
    return (jnp.where((quarter & 2) == 2, -sine, sine), jnp.where(((quarter + 1) & 2) == 2, -cosine, cosine))


def per_token(ref, first, tokens, heads):
    return jnp.concatenate([
        jnp.broadcast_to(ref[first + t:first + t + 1, :], (heads, ref.shape[-1])) for t in range(tokens)], axis=0)


def pair_kernel(heads, chunk, layout_h, layout_row_h, docs_h, q_h, k_h, v_h, g_h,
                o_ref, dq_ref, dk_ref, dv_ref,
                layout_s, layout_v, docs_v, q_in, g_in, kraw, vall, kb, qe, cos_ref, sin_ref, cos_mine, sin_mine,
                w_all, dp_all, p_t, ds_t, stats, k_t, v_t, send_buf, recv_buf, own,
                local_sem, send_sem, recv_sem):
    n = 4
    me = lax.axis_index("context")
    seq, hd = kraw.shape
    rows = seq // n
    half = hd // 2
    tokens = chunk // heads
    steps = rows // tokens
    scale = 1.0 / math.sqrt(hd)
    factor = scale * math.log2(math.e)
    chip, core = me // 2, lax.rem(me, 2)
    partner = chip * 2 + (1 - core)
    across = (1 - chip) * 2 + core
    diagonal = (1 - chip) * 2 + (1 - core)

    def block(at, count=1):
        return pl.ds(pl.multiple_of(at * rows, rows), count * rows)

    barrier = pltpu.get_barrier_semaphore()
    for peer in (across, diagonal, partner):
        pl.semaphore_signal(barrier, inc=1, device_id={"context": peer}, device_id_type=MESH)

    mine = block(me)
    near, far = block(2 * chip, 2), block(2 * (1 - chip), 2)
    k_copy = pltpu.make_async_copy(k_h, kraw.at[mine], local_sem.at[2])
    v_copy = pltpu.make_async_copy(v_h, vall.at[mine], local_sem.at[4])
    layout_copy = pltpu.make_async_copy(layout_h, layout_s, local_sem.at[0])
    docs_copy = pltpu.make_async_copy(docs_h, docs_v, local_sem.at[1])
    row_copy = pltpu.make_async_copy(layout_row_h, layout_v, local_sem.at[3])
    q_copy = pltpu.make_async_copy(q_h, q_in, local_sem.at[5])
    g_copy = pltpu.make_async_copy(g_h, g_in, local_sem.at[6])
    for copy in (k_copy, v_copy, layout_copy, docs_copy, row_copy, q_copy, g_copy):
        copy.start()

    def transfer(at, source, target, to):
        return pltpu.make_async_remote_copy(
            src_ref=source, dst_ref=target, send_sem=send_sem.at[at], recv_sem=recv_sem.at[at],
            device_id={"context": to}, device_id_type=MESH)

    k_across = transfer(0, kraw.at[mine], kraw.at[mine], across)
    k_near = transfer(1, kraw.at[mine], kraw.at[mine], partner)
    k_pass = transfer(2, kraw.at[block(across)], kraw.at[block(across)], partner)
    v_across = transfer(3, vall.at[mine], vall.at[mine], across)
    v_near = transfer(4, vall.at[mine], vall.at[mine], partner)
    v_diagonal = transfer(5, vall.at[mine], vall.at[mine], diagonal)
    grads = {(kind, to): transfer(6 + 3 * kind + to, send_buf.at[kind, to], recv_buf.at[kind, to],
                                  (across, diagonal, partner)[to]) for kind in (0, 1) for to in (0, 1, 2)}

    for at in range(steps):
        row = lax.broadcasted_iota(jnp.int32, (chunk, hd), 0) // heads + at * tokens
        col = lax.broadcasted_iota(jnp.int32, (chunk, hd), 1)
        qe[at * chunk:(at + 1) * chunk, hd:] = jnp.where(row == col, 1.0, 0.0).astype(BF16)

    k_copy.wait()
    v_copy.wait()
    pl.semaphore_wait(barrier, n - 1)
    for copy in (k_across, k_near, v_across, v_near, v_diagonal):
        copy.start()

    lane = lax.broadcasted_iota(jnp.int32, (1, hd), 1)
    low = lane < half
    freq = jnp.exp(-(2.0 * lax.rem(lane, half).astype(F32) / hd) * math.log(THETA))
    within = lax.broadcasted_iota(jnp.int32, (RUN, 1), 0).astype(F32)
    docs_copy.wait()
    docs = jnp.broadcast_to(docs_v[...], (8, seq))
    lane_at = lax.broadcasted_iota(jnp.int32, (8, seq), 1)
    starts = jnp.where(docs != pltpu.roll(docs, 1, 1), lane_at, 0).astype(F32)[:1]
    layout_copy.wait()

    def places(owner):
        found = []
        for run in range(rows // RUN):
            token = within + layout_s[owner * rows + run * RUN].astype(F32)
            start = jnp.max(jnp.where(starts <= token, starts, 0.0), axis=1, keepdims=True)
            found.append((token, start))
        return found

    def tables(owner, found):
        (token_a, start_a), (token_b, start_b) = found
        sine, cosine = sine_cosine(jnp.where(low, token_a - start_a, token_b - start_b) * freq)
        sine_r, cosine_r = pltpu.roll(sine, half, 1), pltpu.roll(cosine, half, 1)
        here = block(owner)
        c = jnp.concatenate([jnp.where(low, cosine, cosine_r), jnp.where(low, cosine_r, cosine)], axis=0)
        s = jnp.concatenate([jnp.where(low, -sine, sine_r), jnp.where(low, -sine_r, sine)], axis=0)
        cos_ref[here, :] = c
        sin_ref[here, :] = s
        return c, s

    def rotate(x, c, s):
        return x * c + pltpu.roll(x, half, 1) * s

    def rotate_keys(owner):
        here = block(owner)
        kb[here, :hd] = rotate(kraw[here, :].astype(F32), cos_ref[here, :], sin_ref[here, :]).astype(BF16)

    found = places(me)
    c, s = tables(me, found)
    cos_mine[...] = c
    sin_mine[...] = s
    token = jnp.concatenate([t for t, _ in found], axis=0)
    start = jnp.concatenate([t for _, t in found], axis=0)
    row_copy.wait()
    keys = layout_v[...].astype(F32)
    kb[:, hd:] = jnp.where((keys >= start) & (keys <= token), 0.0, MASKED).T.astype(BF16)
    rotate_keys(me)
    q_copy.wait()
    for at in range(steps):
        here = slice(at * chunk, (at + 1) * chunk)
        cosines = per_token(cos_mine, at * tokens, tokens, heads)
        sines = per_token(sin_mine, at * tokens, tokens, heads)
        qe[here, :hd] = rotate(q_in[here, :].astype(F32), cosines, sines).astype(BF16)
    for owner in (partner, across, diagonal):
        tables(owner, places(owner))

    def score(where, at, chunk_at):
        here = slice(chunk_at * chunk, (chunk_at + 1) * chunk)
        scores = dot(kb[where, :], qe[here, :], 1)
        largest = jnp.max(scores, axis=0, keepdims=True)
        weights = jnp.exp2((scores - largest) * factor)
        w_all[where, here] = weights
        stats[3 * at:3 * at + 1, here] = largest
        stats[3 * at + 1:3 * at + 2, here] = jnp.sum(weights, axis=0, keepdims=True)

    def back(where, at, chunk_at):
        here = slice(chunk_at * chunk, (chunk_at + 1) * chunk)
        dprobs = dot(vall[where, :], g_in[here, :], 1)
        dp_all[where, here] = dprobs
        stats[3 * at + 2:3 * at + 3, here] = jnp.sum(w_all[where, here] * dprobs, axis=0, keepdims=True)

    k_near.wait_recv()
    rotate_keys(partner)
    g_copy.wait()
    v_near.wait_recv()
    for at in range(steps):
        score(near, 0, at)
        back(near, 0, at)

    k_across.wait_recv()
    k_pass.start()
    rotate_keys(across)
    for at in range(steps):
        score(block(across), 1, at)
    v_across.wait_recv()
    for at in range(steps):
        back(block(across), 1, at)
    k_pass.wait_recv()
    rotate_keys(diagonal)
    for at in range(steps):
        score(block(diagonal), 2, at)

    maxima = [stats[3 * at:3 * at + 1, :] for at in range(3)]
    largest = jnp.maximum(jnp.maximum(maxima[0], maxima[1]), maxima[2])
    shrink = [jnp.exp2((m - largest) * factor) for m in maxima]
    inverse = 1.0 / sum(shrink[at] * stats[3 * at + 1:3 * at + 2, :] for at in range(3))
    for at in range(3):
        stats[9 + at:10 + at, :] = shrink[at] * inverse

    def make_p(where, at, chunk_at):
        here = slice(chunk_at * chunk, (chunk_at + 1) * chunk)
        p = w_all[where, here] * stats[9 + at:10 + at, here]
        w_all[where, here] = p
        p_t[where, here] = p.astype(BF16)

    def make_ds(where, chunk_at):
        here = slice(chunk_at * chunk, (chunk_at + 1) * chunk)
        ds_t[where, here] = (w_all[where, here] * (dp_all[where, here] - stats[12:13, here])).astype(BF16)

    for at in range(steps):
        make_p(block(across), 1, at)
        make_p(block(diagonal), 2, at)

    def far_send(kind, left, right):
        for to, owner in ((0, across), (1, diagonal)):
            send_buf[kind, to] = dot(left[block(owner), :], right).astype(BF16)
            grads[kind, to].start()

    far_send(0, p_t, g_in[...])
    v_diagonal.wait_recv()
    for at in range(steps):
        back(block(diagonal), 2, at)
    stats[12:13, :] = stats[9:10, :] * stats[2:3, :] + stats[10:11, :] * stats[5:6, :] + stats[8:9, :]
    for at in range(steps):
        make_ds(block(across), at)
        make_ds(block(diagonal), at)
    far_send(1, ds_t, qe[:, :hd])

    for at in range(steps):
        make_p(near, 0, at)
        make_ds(near, at)
    for kind, left, right in ((0, p_t, g_in[...]), (1, ds_t, qe[:, :hd])):
        send_buf[kind, 2] = dot(left[block(partner), :], right).astype(BF16)
        grads[kind, 2].start()
        own[kind] = dot(left[mine, :], right)

    k_t[...] = kb[:, :hd].astype(F32).T.astype(BF16)
    v_t[...] = vall[...].astype(F32).T.astype(BF16)
    for at in range(steps):
        here = slice(at * chunk, (at + 1) * chunk)
        o_ref[here, :] = dot(v_t[...], p_t[:, here]).T.astype(BF16)
    cos_mine[...] = cos_mine[...] * scale
    sin_mine[...] = sin_mine[...] * -scale
    for at in range(steps):
        here = slice(at * chunk, (at + 1) * chunk)
        cosines = per_token(cos_mine, at * tokens, tokens, heads)
        sines = per_token(sin_mine, at * tokens, tokens, heads)
        dq_ref[here, :] = rotate(dot(k_t[...], ds_t[:, here]).T, cosines, sines).astype(BF16)

    def collect(kind):
        for to in (2, 0, 1):
            grads[kind, to].wait_recv()
        return own[kind] + jnp.sum(recv_buf[kind].astype(F32), axis=0)

    dv_ref[...] = collect(0)
    dk_ref[...] = rotate(collect(1), cos_mine[...], sin_mine[...])
    for copy in (k_across, k_near, k_pass, v_across, v_near, v_diagonal, *grads.values()):
        copy.wait_send()


def loop(count, step):
    if count <= 8:
        for index in range(count):
            step(index)
    else:
        lax.fori_loop(0, count, lambda index, _: (step(index), None)[1], None)


def span(at, size):
    start = at * size
    return pl.ds(start if isinstance(at, int) else pl.multiple_of(start, size), size)


def rotate(x, cosine, sine):
    return x * cosine + pltpu.roll(x, x.shape[-1] // 2, 1) * sine


def spread(ref, at, chunk, heads):
    part = ref[span(at, chunk // heads), :]
    return jnp.broadcast_to(part[:, None, :], (chunk // heads, heads, part.shape[-1])).reshape(chunk, -1)


def ring_kernel(n, heads, chunk, layout_h, layout_row_h, docs_h, q_h, k_h, v_h, g_h,
                o_ref, dq_ref, dk_ref, dv_ref,
                layout_s, layout_v, docs_v, q_in, g_in, k_in, probs, k_t, cos_ref, sin_ref, qe, kall, vall, v_t, p_t, bias_t,
                send_buf, recv_buf, own_dv, local_sem, send_sem, recv_sem):
    me = lax.axis_index("context")
    rows, hd = k_in.shape
    seq = rows * n
    flat = rows * heads
    tokens = chunk // heads
    steps = flat // chunk
    scale = 1.0 / math.sqrt(hd)

    factor = scale * math.log2(math.e)

    def peer(k):
        pair = lax.rem(me // 2 + (k + 1) // 2, n // 2)
        return pair * 2 + lax.rem(me + k + 1, 2)

    barrier = pltpu.get_barrier_semaphore()
    for k in range(n - 1):
        pl.semaphore_signal(barrier, inc=1, device_id={"context": peer(k)}, device_id_type=MESH)

    mine = span(me, rows)
    layout_copy = pltpu.make_async_copy(layout_h, layout_s, local_sem.at[0])
    docs_copy = pltpu.make_async_copy(docs_h, docs_v, local_sem.at[1])
    k_copy = pltpu.make_async_copy(k_h, k_in, local_sem.at[2])
    row_copy = pltpu.make_async_copy(layout_row_h, layout_v, local_sem.at[3])
    v_copy = pltpu.make_async_copy(v_h, vall.at[mine], local_sem.at[4])
    q_copy = pltpu.make_async_copy(q_h, q_in, local_sem.at[5])
    g_copy = pltpu.make_async_copy(g_h, g_in, local_sem.at[6])
    for copy in (layout_copy, docs_copy, k_copy, v_copy, row_copy, q_copy, g_copy):
        copy.start()

    half = hd // 2
    lane = lax.broadcasted_iota(jnp.int32, (1, hd), 1)
    freq = jnp.exp(-(2.0 * lax.rem(lane, half).astype(F32) / hd) * math.log(THETA))
    row_at = lax.broadcasted_iota(jnp.int32, (rows, hd), 0)
    layout_copy.wait()
    first = layout_s[me * rows].astype(F32)
    second = layout_s[me * rows + RUN].astype(F32)
    token = jnp.where(row_at < RUN, row_at.astype(F32) + first, (row_at - RUN).astype(F32) + second)
    token = token[:, :1]
    docs_copy.wait()
    docs = jnp.broadcast_to(docs_v[...], (8, seq))
    lane_at = lax.broadcasted_iota(jnp.int32, (8, seq), 1)
    starts = jnp.where(docs != pltpu.roll(docs, 1, 1), lane_at, 0).astype(F32)[:1]
    start = jnp.max(jnp.where(starts <= token, starts, 0.0), axis=1, keepdims=True)
    angles = (token - start) * freq
    cosine = jnp.cos(angles)
    sine = jnp.where(lane < half, -1.0, 1.0) * jnp.sin(angles)
    cos_ref[...] = cosine
    sin_ref[...] = sine
    k_copy.wait()
    kall[mine] = rotate(k_in[...].astype(F32), cosine, sine).astype(BF16)
    v_copy.wait()

    pl.semaphore_wait(barrier, n - 1)

    def transfer(kind, k, source, target):
        return pltpu.make_async_remote_copy(
            src_ref=source, dst_ref=target,
            send_sem=send_sem.at[kind, k], recv_sem=recv_sem.at[kind, k],
            device_id={"context": peer(k)}, device_id_type=MESH)

    def k_send(k):
        return transfer(0, k, kall.at[mine], kall.at[mine])

    def v_send(k):
        return transfer(1, k, vall.at[mine], vall.at[mine])

    def g_send(kind, k):
        return transfer(2 + kind, k, send_buf.at[kind, k], recv_buf.at[kind, k])

    loop(n - 1, lambda k: k_send(n - 2 - k).start())

    row_copy.wait()
    keys = layout_v[...].astype(F32)
    bias_t[...] = jnp.where((keys >= start) & (keys <= token), 0.0, MASKED).T.astype(BF16)
    q_copy.wait()

    def make_q(at):
        here = span(at, chunk)
        cosines, sines = spread(cos_ref, at, chunk, heads), spread(sin_ref, at, chunk, heads)
        qe[here, :hd] = rotate(q_in[here, :].astype(F32), cosines, sines).astype(BF16)
        row = lax.broadcasted_iota(jnp.int32, (chunk, hd), 0) // heads + at * tokens
        col = lax.broadcasted_iota(jnp.int32, (chunk, hd), 1)
        qe[here, hd:] = (row == col).astype(F32).astype(BF16)

    loop(steps, make_q)

    def make_probs(at):
        here = span(at, chunk)
        scores = dot(jnp.concatenate([kall[...], bias_t[...]], axis=1), qe[here, :], 1)
        largest = jnp.max(scores, axis=0, keepdims=True)
        weights = jnp.exp2((scores - largest) * factor)
        total = jnp.sum(weights, axis=0, keepdims=True)
        p_t[:, here] = (weights * (1.0 / total)).astype(BF16)

    loop(n - 1, lambda k: k_send(k).wait_recv())
    loop(n - 1, lambda k: v_send(k).start())
    loop(steps, make_probs)
    g_copy.wait()

    def v_grads(k):
        send_buf[0, k] = dot(p_t[span(peer(k), rows), :], g_in[...]).astype(BF16)
        g_send(0, k).start()

    loop(n - 1, lambda k: v_grads(n - 2 - k))
    loop(n - 1, lambda k: v_send(k).wait_recv())

    def make_ds(at):
        here = span(at, chunk)
        dprobs = dot(vall[...], g_in[here, :], 1)
        p = p_t[:, here].astype(F32)
        delta = jnp.sum(p * dprobs, axis=0, keepdims=True)
        probs[:, here] = (p * (dprobs - delta)).astype(BF16)

    loop(steps, make_ds)

    def k_grads(k):
        send_buf[1, k] = (dot(probs[span(peer(k), rows), :], qe[:, :hd]) * scale).astype(BF16)
        g_send(1, k).start()

    loop(n - 1, lambda k: k_grads(n - 2 - k))
    own_dk = dot(probs[mine, :], qe[:, :hd]) * scale
    own_dv[...] = dot(p_t[mine, :], g_in[...])
    k_t[...] = kall[...].astype(F32).T.astype(BF16)
    v_t[...] = vall[...].astype(F32).T.astype(BF16)

    def make_o(at):
        here = span(at, chunk)
        o_ref[here, :] = dot(v_t[...], p_t[:, here]).T.astype(BF16)

    def make_dq(at):
        here = span(at, chunk)
        grad = dot(k_t[...], probs[:, here]).T * scale
        cosines, sines = spread(cos_ref, at, chunk, heads), spread(sin_ref, at, chunk, heads)
        dq_ref[here, :] = rotate(grad, cosines, -sines).astype(BF16)

    loop(steps, make_o)
    loop(steps, make_dq)

    def collect(kind, own):
        loop(n - 1, lambda k: g_send(kind, k).wait_recv())
        return own + jnp.sum(recv_buf[kind].astype(F32), axis=0)

    dv_ref[...] = collect(0, own_dv[...])
    dk_ref[...] = rotate(collect(1, own_dk), cos_ref[...], -sin_ref[...])

    def finish(k):
        k_send(k).wait_send()
        v_send(k).wait_send()
        g_send(0, k).wait_send()
        g_send(1, k).wait_send()

    loop(n - 1, finish)


def last_kernel(*refs):
    count = len(refs) // 2
    sem = refs[-1]
    copies = [pltpu.make_async_copy(refs[at], refs[count + at], sem.at[at]) for at in range(count)]
    for copy in copies:
        copy.start()
    for copy in copies:
        copy.wait()


def body(n, queries, key_heads, value_heads, out_grad, layout, documents):
    rows, heads, hd = queries.shape
    seq = layout.shape[0]
    flat = rows * heads
    hbm = pl.BlockSpec(memory_space=pltpu.HBM)
    vmem = pl.BlockSpec(memory_space=pltpu.VMEM)
    shapes = (
        jax.ShapeDtypeStruct((flat, hd), BF16),
        jax.ShapeDtypeStruct((flat, hd), BF16),
        jax.ShapeDtypeStruct((rows, hd), F32),
        jax.ShapeDtypeStruct((rows, hd), F32),
    )
    operands = [
        pltpu.SMEM((seq,), jnp.int32),
        pltpu.VMEM((1, seq), jnp.int32),
        pltpu.VMEM((1, seq), jnp.int32),
        pltpu.VMEM((flat, hd), BF16),
        pltpu.VMEM((flat, hd), BF16),
    ]
    if n == 4:
        kernel = functools.partial(pair_kernel, heads, 256)
        scratch = operands + [
            pltpu.VMEM((seq, hd), BF16),
            pltpu.VMEM((seq, hd), BF16),
            pltpu.VMEM((seq, 2 * hd), BF16),
            pltpu.VMEM((flat, 2 * hd), BF16),
            pltpu.VMEM((seq, hd), F32),
            pltpu.VMEM((seq, hd), F32),
            pltpu.VMEM((rows, hd), F32),
            pltpu.VMEM((rows, hd), F32),
            pltpu.VMEM((seq, flat), F32),
            pltpu.VMEM((seq, flat), F32),
            pltpu.VMEM((seq, flat), BF16),
            pltpu.VMEM((seq, flat), BF16),
            pltpu.VMEM((16, flat), F32),
            pltpu.VMEM((hd, seq), BF16),
            pltpu.VMEM((hd, seq), BF16),
            pltpu.VMEM((2, 3, rows, hd), BF16),
            pltpu.VMEM((2, 3, rows, hd), BF16),
            pltpu.VMEM((2, rows, hd), F32),
            pltpu.SemaphoreType.DMA((7,)),
            pltpu.SemaphoreType.DMA((12,)),
            pltpu.SemaphoreType.DMA((12,)),
        ]
    else:
        kernel = functools.partial(ring_kernel, n, heads, 128)
        scratch = operands + [
            pltpu.VMEM((rows, hd), BF16),
            pltpu.VMEM((seq, flat), BF16),
            pltpu.VMEM((hd, seq), BF16),
            pltpu.VMEM((rows, hd), F32),
            pltpu.VMEM((rows, hd), F32),
            pltpu.VMEM((flat, 2 * hd), BF16),
            pltpu.VMEM((seq, hd), BF16),
            pltpu.VMEM((seq, hd), BF16),
            pltpu.VMEM((hd, seq), BF16),
            pltpu.VMEM((seq, flat), BF16),
            pltpu.VMEM((seq, rows), BF16),
            pltpu.VMEM((2, n - 1, rows, hd), BF16),
            pltpu.VMEM((2, n - 1, rows, hd), BF16),
            pltpu.VMEM((rows, hd), F32),
            pltpu.SemaphoreType.DMA((7,)),
            pltpu.SemaphoreType.DMA((4, n - 1)),
            pltpu.SemaphoreType.DMA((4, n - 1)),
        ]
    carried = pl.pallas_call(
        kernel,
        out_shape=shapes,
        in_specs=[hbm] * 7,
        out_specs=(vmem,) * 4,
        scratch_shapes=scratch,
        compiler_params=pltpu.CompilerParams(
            collective_id=0, has_side_effects=True, vmem_limit_bytes=(40 if n == 4 else 58) * 1024 * 1024),
    )(*[pltpu.with_memory_space_constraint(operand, pltpu.HBM) for operand in (
        layout, layout.reshape(1, seq), documents.reshape(1, seq),
        queries.reshape(flat, hd), key_heads.reshape(rows, hd), value_heads.reshape(rows, hd),
        out_grad.reshape(flat, hd),
    )])
    out, dq, dk, dv = pl.pallas_call(
        last_kernel,
        out_shape=shapes,
        in_specs=[vmem] * 4,
        out_specs=(hbm,) * 4,
        scratch_shapes=[pltpu.SemaphoreType.DMA((4,))],
        compiler_params=pltpu.CompilerParams(vmem_limit_bytes=8 * 1024 * 1024),
    )(*carried)
    return (out.reshape(rows, heads, hd), dq.reshape(rows, heads, hd), dk, dv)


def solution(mesh):
    return jax.shard_map(
        functools.partial(body, mesh.shape["context"]),
        mesh=mesh,
        in_specs=(
            P(("dp", "context"), "tensor", None),
            P(("dp", "context"), "tensor", None),
            P(("dp", "context"), "tensor", None),
            P(("dp", "context"), "tensor", None),
            P("dp"),
            P("dp"),
        ),
        out_specs=(
            P(("dp", "context"), "tensor", None),
            P(("dp", "context"), "tensor", None),
            P(("dp", "context"), "tensor"),
            P(("dp", "context"), "tensor"),
        ),
        check_vma=False,
    )
```

```python
import functools
import math

import jax
import jax.numpy as jnp
from jax import lax
from jax.experimental import pallas as pl
from jax.experimental.pallas import tpu as pltpu
from jax.sharding import PartitionSpec as P

THETA = 8000000.0
RUN = 64
MASKED = -1e30
MESH = pl.DeviceIdType.MESH
F32 = jnp.float32
BF16 = jnp.bfloat16


def dot(lhs, rhs, rhs_dim=0):
    return lax.dot_general(lhs, rhs, (((1,), (rhs_dim,)), ((), ())), preferred_element_type=F32)


def sine_cosine(x):
    turns = jnp.floor(x * (2.0 / math.pi) + 0.5)
    r = ((x - turns * 1.5703125) - turns * 4.837512969970703125e-4) - turns * 7.54978995489188216e-8
    z = r * r
    s = r + r * z * (-1.6666654611e-1 + z * (8.3321608736e-3 - z * 1.9515295891e-4))
    c = 1.0 - 0.5 * z + z * z * (4.166664568298827e-2 + z * (-1.388731625493765e-3 + z * 2.443315711809948e-5))
    quarter = turns.astype(jnp.int32)
    odd = (quarter & 1) == 1
    sine = jnp.where(odd, c, s)
    cosine = jnp.where(odd, s, c)
    return (jnp.where((quarter & 2) == 2, -sine, sine), jnp.where(((quarter + 1) & 2) == 2, -cosine, cosine))


def per_token(ref, first, tokens, heads):
    return jnp.concatenate([
        jnp.broadcast_to(ref[first + t:first + t + 1, :], (heads, ref.shape[-1])) for t in range(tokens)], axis=0)


def pair_kernel(heads, chunk, layout_h, layout_row_h, docs_h, q_h, k_h, v_h, g_h,
                o_ref, dq_ref, dk_ref, dv_ref,
                layout_s, layout_v, docs_v, q_in, g_in, kraw, vall, kb, qe, q_t, g_t, cos_ref, sin_ref, cos_mine, sin_mine,
                w_near, w_across, w_diagonal, dp_near, dp_across, dp_diagonal, p_t, ds_t, stats, k_t, v_t,
                grad_near, send_buf, recv_buf,
                local_sem, send_sem, recv_sem):
    n = 4
    me = lax.axis_index("context")
    rows, hd = cos_mine.shape
    seq = n * rows
    half = hd // 2
    tokens = chunk // heads
    steps = rows // tokens
    scale = 1.0 / math.sqrt(hd)
    factor = scale * math.log2(math.e)
    chip, core = me // 2, lax.rem(me, 2)
    partner = chip * 2 + (1 - core)
    across = (1 - chip) * 2 + core
    diagonal = (1 - chip) * 2 + (1 - core)
    owners = (me, partner, across, diagonal)

    def block(role, count=1):
        return slice(role * rows, (role + count) * rows)

    def part(at):
        return slice(at * chunk, (at + 1) * chunk)

    near, far = block(0, 2), block(2, 2)

    barrier = pltpu.get_barrier_semaphore()
    for peer in (across, diagonal, partner):
        pl.semaphore_signal(barrier, inc=1, device_id={"context": peer}, device_id_type=MESH)

    k_copy = pltpu.make_async_copy(k_h, kraw.at[block(0)], local_sem.at[2])
    v_copy = pltpu.make_async_copy(v_h, vall.at[block(0)], local_sem.at[4])
    layout_copy = pltpu.make_async_copy(layout_h, layout_s, local_sem.at[0])
    docs_copy = pltpu.make_async_copy(docs_h, docs_v, local_sem.at[1])
    row_copy = pltpu.make_async_copy(layout_row_h, layout_v, local_sem.at[3])
    q_copy = pltpu.make_async_copy(q_h, q_in, local_sem.at[5])
    g_copy = pltpu.make_async_copy(g_h, g_in, local_sem.at[6])
    for copy in (k_copy, v_copy, layout_copy, docs_copy, row_copy, q_copy, g_copy):
        copy.start()

    def transfer(at, source, target, to):
        return pltpu.make_async_remote_copy(
            src_ref=source, dst_ref=target, send_sem=send_sem.at[at], recv_sem=recv_sem.at[at],
            device_id={"context": to}, device_id_type=MESH)

    k_across = transfer(0, kraw.at[block(0)], kraw.at[block(2)], across)
    k_near = transfer(1, kraw.at[block(0)], kraw.at[block(1)], partner)
    k_diagonal = transfer(2, kraw.at[block(0)], kraw.at[block(3)], diagonal)
    v_across = transfer(3, vall.at[block(0)], vall.at[block(2)], across)
    v_near = transfer(4, vall.at[block(0)], vall.at[block(1)], partner)
    v_diagonal = transfer(5, vall.at[block(0)], vall.at[block(3)], diagonal)
    dv_near = transfer(6, send_buf.at[0], recv_buf.at[0], partner)
    dv_across = transfer(7, send_buf.at[1], recv_buf.at[1], across)
    dv_diagonal = transfer(8, send_buf.at[2], recv_buf.at[2], diagonal)
    dk_near = transfer(9, send_buf.at[3], recv_buf.at[3], partner)
    dk_across = transfer(10, send_buf.at[4], recv_buf.at[4], across)
    dk_diagonal = transfer(11, send_buf.at[5], recv_buf.at[5], diagonal)

    for at in range(steps):
        row = lax.broadcasted_iota(jnp.int32, (chunk, hd), 0) // heads + at * tokens
        col = lax.broadcasted_iota(jnp.int32, (chunk, hd), 1)
        qe[part(at), hd:] = jnp.where(row == col, 1.0, 0.0).astype(BF16)

    k_copy.wait()
    v_copy.wait()
    pl.semaphore_wait(barrier, n - 1)
    for copy in (k_across, k_near, k_diagonal, v_near, v_across, v_diagonal):
        copy.start()

    lane = lax.broadcasted_iota(jnp.int32, (1, hd), 1)
    low = lane < half
    freq = jnp.exp(-(2.0 * lax.rem(lane, half).astype(F32) / hd) * math.log(THETA))
    within = lax.broadcasted_iota(jnp.int32, (RUN, 1), 0).astype(F32)
    docs_copy.wait()
    docs = jnp.broadcast_to(docs_v[...], (8, seq))
    lane_at = lax.broadcasted_iota(jnp.int32, (8, seq), 1)
    starts = jnp.where(docs != pltpu.roll(docs, 1, 1), lane_at, 0).astype(F32)[:1]
    layout_copy.wait()

    def places(owner):
        found = []
        for run in range(rows // RUN):
            token = within + layout_s[owner * rows + run * RUN].astype(F32)
            start = jnp.max(jnp.where(starts <= token, starts, 0.0), axis=1, keepdims=True)
            found.append((token, start))
        return found

    def tables(found):
        (token_a, start_a), (token_b, start_b) = found
        sine, cosine = sine_cosine(jnp.where(low, token_a - start_a, token_b - start_b) * freq)
        sine_r, cosine_r = pltpu.roll(sine, half, 1), pltpu.roll(cosine, half, 1)
        c = jnp.concatenate([jnp.where(low, cosine, cosine_r), jnp.where(low, cosine_r, cosine)], axis=0)
        s = jnp.concatenate([jnp.where(low, -sine, sine_r), jnp.where(low, -sine_r, sine)], axis=0)
        return c, s

    def rotate(x, c, s):
        return x * c + pltpu.roll(x, half, 1) * s

    def rotate_keys(role, c, s):
        kb[block(role), :hd] = rotate(kraw[block(role), :].astype(F32), c, s).astype(BF16)

    found = places(me)
    c, s = tables(found)
    cos_mine[...] = c
    sin_mine[...] = s
    rotate_keys(0, c, s)
    token = jnp.concatenate([t for t, _ in found], axis=0)
    start = jnp.concatenate([t for _, t in found], axis=0)
    row_copy.wait()
    for role in range(n):
        keys = layout_v[:, pl.ds(pl.multiple_of(owners[role] * rows, rows), rows)].astype(F32)
        kb[block(role), hd:] = jnp.where((keys >= start) & (keys <= token), 0.0, MASKED).T.astype(BF16)
    q_copy.wait()
    for at in range(steps):
        cosines = per_token(cos_mine, at * tokens, tokens, heads)
        sines = per_token(sin_mine, at * tokens, tokens, heads)
        rotated = rotate(q_in[part(at), :].astype(F32), cosines, sines)
        qe[part(at), :hd] = rotated.astype(BF16)
        q_t[:, part(at)] = rotated.T.astype(BF16)
    g_copy.wait()
    for at in range(steps):
        g_t[:, part(at)] = g_in[part(at), :].astype(F32).T.astype(BF16)
    for role in (1, 2, 3):
        c, s = tables(places(owners[role]))
        cos_ref[block(role), :] = c
        sin_ref[block(role), :] = s

    def score(role, count, w_ref, at, chunk_at):
        here = part(chunk_at)
        scores = dot(kb[block(role, count), :], qe[here, :], 1)
        largest = jnp.max(scores, axis=0, keepdims=True)
        weights = jnp.exp2((scores - largest) * factor)
        w_ref[:, here] = weights
        stats[3 * at:3 * at + 1, here] = largest
        stats[3 * at + 1:3 * at + 2, here] = jnp.sum(weights, axis=0, keepdims=True)

    def back(role, count, w_ref, dp_ref, at, chunk_at):
        here = part(chunk_at)
        dprobs = dot(vall[block(role, count), :], g_in[here, :], 1)
        dp_ref[:, here] = dprobs
        stats[3 * at + 2:3 * at + 3, here] = jnp.sum(w_ref[:, here] * dprobs, axis=0, keepdims=True)

    def arrived(role):
        rotate_keys(role, cos_ref[block(role), :], sin_ref[block(role), :])

    k_near.wait_recv()
    arrived(1)
    v_near.wait_recv()
    for at in range(steps):
        score(0, 2, w_near, 0, at)
        back(0, 2, w_near, dp_near, 0, at)

    k_across.wait_recv()
    arrived(2)
    for at in range(steps):
        score(2, 1, w_across, 1, at)
    k_diagonal.wait_recv()
    arrived(3)
    for at in range(steps):
        here = part(at)
        score(3, 1, w_diagonal, 2, at)
        maxima = [stats[3 * b:3 * b + 1, here] for b in range(3)]
        largest = jnp.maximum(jnp.maximum(maxima[0], maxima[1]), maxima[2])
        shrink = [jnp.exp2((m - largest) * factor) for m in maxima]
        inverse = 1.0 / sum(shrink[b] * stats[3 * b + 1:3 * b + 2, here] for b in range(3))
        weight = [shrink[b] * inverse for b in range(3)]
        stats[9:10, here] = weight[0]
        stats[10:11, here] = weight[0] * stats[2:3, here]
        for b, w_ref, role in ((1, w_across, 2), (2, w_diagonal, 3)):
            p = w_ref[:, here] * weight[b]
            w_ref[:, here] = p
            p_t[block(role), here] = p.astype(BF16)
    dv = dot(g_t[...], p_t[far, :], 1).astype(BF16)
    send_buf[1] = dv[:, :rows]
    send_buf[2] = dv[:, rows:]
    dv_across.start()
    dv_diagonal.start()

    v_across.wait_recv()
    for at in range(steps):
        back(2, 1, w_across, dp_across, 1, at)
    v_diagonal.wait_recv()
    for at in range(steps):
        here = part(at)
        back(3, 1, w_diagonal, dp_diagonal, 2, at)
        delta = stats[10:11, here] + stats[5:6, here] + stats[8:9, here]
        stats[11:12, here] = delta
        for w_ref, dp_ref, role in ((w_across, dp_across, 2), (w_diagonal, dp_diagonal, 3)):
            ds_t[block(role), here] = (w_ref[:, here] * (dp_ref[:, here] - delta)).astype(BF16)
    dk = dot(q_t[...], ds_t[far, :], 1).astype(BF16)
    send_buf[4] = dk[:, :rows]
    send_buf[5] = dk[:, rows:]
    dk_across.start()
    dk_diagonal.start()

    for at in range(steps):
        here = part(at)
        p = w_near[:, here] * stats[9:10, here]
        p_t[near, here] = p.astype(BF16)
        ds_t[near, here] = (p * (dp_near[:, here] - stats[11:12, here])).astype(BF16)
    for kind, left, right in ((0, g_t, p_t), (1, q_t, ds_t)):
        grad = dot(left[...], right[near, :], 1)
        send_buf[3 * kind] = grad[:, rows:].astype(BF16)
        (dv_near, dk_near)[kind].start()
        grad_near[kind] = grad[:, :rows]

    k_t[...] = kb[:, :hd].astype(F32).T.astype(BF16)
    v_t[...] = vall[...].astype(F32).T.astype(BF16)
    for at in range(steps):
        o_ref[part(at), :] = dot(v_t[...], p_t[:, part(at)]).T.astype(BF16)
    cos_mine[...] = cos_mine[...] * scale
    sin_mine[...] = sin_mine[...] * -scale
    for at in range(steps):
        cosines = per_token(cos_mine, at * tokens, tokens, heads)
        sines = per_token(sin_mine, at * tokens, tokens, heads)
        dq_ref[part(at), :] = rotate(dot(k_t[...], ds_t[:, part(at)]).T, cosines, sines).astype(BF16)

    dv_near.wait_recv()
    dk_near.wait_recv()
    dv_across.wait_recv()
    dv_diagonal.wait_recv()
    dv_ref[...] = (grad_near[0] + recv_buf[0].astype(F32) + recv_buf[1].astype(F32) + recv_buf[2].astype(F32)).T
    dk_across.wait_recv()
    dk_diagonal.wait_recv()
    dk_ref[...] = rotate((grad_near[1] + recv_buf[3].astype(F32) + recv_buf[4].astype(F32) + recv_buf[5].astype(F32)).T, cos_mine[...], sin_mine[...])
    for copy in (k_across, k_near, k_diagonal, v_across, v_near, v_diagonal,
                 dv_near, dv_across, dv_diagonal, dk_near, dk_across, dk_diagonal):
        copy.wait_send()


def loop(count, step):
    if count <= 8:
        for index in range(count):
            step(index)
    else:
        lax.fori_loop(0, count, lambda index, _: (step(index), None)[1], None)


def span(at, size):
    start = at * size
    return pl.ds(start if isinstance(at, int) else pl.multiple_of(start, size), size)


def rotate(x, cosine, sine):
    return x * cosine + pltpu.roll(x, x.shape[-1] // 2, 1) * sine


def spread(ref, at, chunk, heads):
    part = ref[span(at, chunk // heads), :]
    return jnp.broadcast_to(part[:, None, :], (chunk // heads, heads, part.shape[-1])).reshape(chunk, -1)


def ring_kernel(n, heads, chunk, layout_h, layout_row_h, docs_h, q_h, k_h, v_h, g_h,
                o_ref, dq_ref, dk_ref, dv_ref,
                layout_s, layout_v, docs_v, q_in, g_in, k_in, probs, k_t, cos_ref, sin_ref, qe, kall, vall, v_t, p_t, bias_t,
                send_buf, recv_buf, own_dv, local_sem, send_sem, recv_sem):
    me = lax.axis_index("context")
    rows, hd = k_in.shape
    seq = rows * n
    flat = rows * heads
    tokens = chunk // heads
    steps = flat // chunk
    scale = 1.0 / math.sqrt(hd)

    factor = scale * math.log2(math.e)

    def peer(k):
        pair = lax.rem(me // 2 + (k + 1) // 2, n // 2)
        return pair * 2 + lax.rem(me + k + 1, 2)

    barrier = pltpu.get_barrier_semaphore()
    for k in range(n - 1):
        pl.semaphore_signal(barrier, inc=1, device_id={"context": peer(k)}, device_id_type=MESH)

    mine = span(me, rows)
    layout_copy = pltpu.make_async_copy(layout_h, layout_s, local_sem.at[0])
    docs_copy = pltpu.make_async_copy(docs_h, docs_v, local_sem.at[1])
    k_copy = pltpu.make_async_copy(k_h, k_in, local_sem.at[2])
    row_copy = pltpu.make_async_copy(layout_row_h, layout_v, local_sem.at[3])
    v_copy = pltpu.make_async_copy(v_h, vall.at[mine], local_sem.at[4])
    q_copy = pltpu.make_async_copy(q_h, q_in, local_sem.at[5])
    g_copy = pltpu.make_async_copy(g_h, g_in, local_sem.at[6])
    for copy in (layout_copy, docs_copy, k_copy, v_copy, row_copy, q_copy, g_copy):
        copy.start()

    half = hd // 2
    lane = lax.broadcasted_iota(jnp.int32, (1, hd), 1)
    freq = jnp.exp(-(2.0 * lax.rem(lane, half).astype(F32) / hd) * math.log(THETA))
    row_at = lax.broadcasted_iota(jnp.int32, (rows, hd), 0)
    layout_copy.wait()
    first = layout_s[me * rows].astype(F32)
    second = layout_s[me * rows + RUN].astype(F32)
    token = jnp.where(row_at < RUN, row_at.astype(F32) + first, (row_at - RUN).astype(F32) + second)
    token = token[:, :1]
    docs_copy.wait()
    docs = jnp.broadcast_to(docs_v[...], (8, seq))
    lane_at = lax.broadcasted_iota(jnp.int32, (8, seq), 1)
    starts = jnp.where(docs != pltpu.roll(docs, 1, 1), lane_at, 0).astype(F32)[:1]
    start = jnp.max(jnp.where(starts <= token, starts, 0.0), axis=1, keepdims=True)
    angles = (token - start) * freq
    cosine = jnp.cos(angles)
    sine = jnp.where(lane < half, -1.0, 1.0) * jnp.sin(angles)
    cos_ref[...] = cosine
    sin_ref[...] = sine
    k_copy.wait()
    kall[mine] = rotate(k_in[...].astype(F32), cosine, sine).astype(BF16)
    v_copy.wait()

    pl.semaphore_wait(barrier, n - 1)

    def transfer(kind, k, source, target):
        return pltpu.make_async_remote_copy(
            src_ref=source, dst_ref=target,
            send_sem=send_sem.at[kind, k], recv_sem=recv_sem.at[kind, k],
            device_id={"context": peer(k)}, device_id_type=MESH)

    def k_send(k):
        return transfer(0, k, kall.at[mine], kall.at[mine])

    def v_send(k):
        return transfer(1, k, vall.at[mine], vall.at[mine])

    def g_send(kind, k):
        return transfer(2 + kind, k, send_buf.at[kind, k], recv_buf.at[kind, k])

    loop(n - 1, lambda k: k_send(n - 2 - k).start())

    row_copy.wait()
    keys = layout_v[...].astype(F32)
    bias_t[...] = jnp.where((keys >= start) & (keys <= token), 0.0, MASKED).T.astype(BF16)
    q_copy.wait()

    def make_q(at):
        here = span(at, chunk)
        cosines, sines = spread(cos_ref, at, chunk, heads), spread(sin_ref, at, chunk, heads)
        qe[here, :hd] = rotate(q_in[here, :].astype(F32), cosines, sines).astype(BF16)
        row = lax.broadcasted_iota(jnp.int32, (chunk, hd), 0) // heads + at * tokens
        col = lax.broadcasted_iota(jnp.int32, (chunk, hd), 1)
        qe[here, hd:] = (row == col).astype(F32).astype(BF16)

    loop(steps, make_q)

    def make_probs(at):
        here = span(at, chunk)
        scores = dot(jnp.concatenate([kall[...], bias_t[...]], axis=1), qe[here, :], 1)
        largest = jnp.max(scores, axis=0, keepdims=True)
        weights = jnp.exp2((scores - largest) * factor)
        total = jnp.sum(weights, axis=0, keepdims=True)
        p_t[:, here] = (weights * (1.0 / total)).astype(BF16)

    loop(n - 1, lambda k: k_send(k).wait_recv())
    loop(n - 1, lambda k: v_send(k).start())
    loop(steps, make_probs)
    g_copy.wait()

    def v_grads(k):
        send_buf[0, k] = dot(p_t[span(peer(k), rows), :], g_in[...]).astype(BF16)
        g_send(0, k).start()

    loop(n - 1, lambda k: v_grads(n - 2 - k))
    loop(n - 1, lambda k: v_send(k).wait_recv())

    def make_ds(at):
        here = span(at, chunk)
        dprobs = dot(vall[...], g_in[here, :], 1)
        p = p_t[:, here].astype(F32)
        delta = jnp.sum(p * dprobs, axis=0, keepdims=True)
        probs[:, here] = (p * (dprobs - delta)).astype(BF16)

    loop(steps, make_ds)

    def k_grads(k):
        send_buf[1, k] = (dot(probs[span(peer(k), rows), :], qe[:, :hd]) * scale).astype(BF16)
        g_send(1, k).start()

    loop(n - 1, lambda k: k_grads(n - 2 - k))
    own_dk = dot(probs[mine, :], qe[:, :hd]) * scale
    own_dv[...] = dot(p_t[mine, :], g_in[...])
    k_t[...] = kall[...].astype(F32).T.astype(BF16)
    v_t[...] = vall[...].astype(F32).T.astype(BF16)

    def make_o(at):
        here = span(at, chunk)
        o_ref[here, :] = dot(v_t[...], p_t[:, here]).T.astype(BF16)

    def make_dq(at):
        here = span(at, chunk)
        grad = dot(k_t[...], probs[:, here]).T * scale
        cosines, sines = spread(cos_ref, at, chunk, heads), spread(sin_ref, at, chunk, heads)
        dq_ref[here, :] = rotate(grad, cosines, -sines).astype(BF16)

    loop(steps, make_o)
    loop(steps, make_dq)

    def collect(kind, own):
        loop(n - 1, lambda k: g_send(kind, k).wait_recv())
        return own + jnp.sum(recv_buf[kind].astype(F32), axis=0)

    dv_ref[...] = collect(0, own_dv[...])
    dk_ref[...] = rotate(collect(1, own_dk), cos_ref[...], -sin_ref[...])

    def finish(k):
        k_send(k).wait_send()
        v_send(k).wait_send()
        g_send(0, k).wait_send()
        g_send(1, k).wait_send()

    loop(n - 1, finish)


def last_kernel(*refs):
    count = len(refs) // 2
    sem = refs[-1]
    copies = [pltpu.make_async_copy(refs[at], refs[count + at], sem.at[at]) for at in range(count)]
    for copy in copies:
        copy.start()
    for copy in copies:
        copy.wait()


def body(n, queries, key_heads, value_heads, out_grad, layout, documents):
    rows, heads, hd = queries.shape
    seq = layout.shape[0]
    flat = rows * heads
    hbm = pl.BlockSpec(memory_space=pltpu.HBM)
    vmem = pl.BlockSpec(memory_space=pltpu.VMEM)
    shapes = (
        jax.ShapeDtypeStruct((flat, hd), BF16),
        jax.ShapeDtypeStruct((flat, hd), BF16),
        jax.ShapeDtypeStruct((rows, hd), F32),
        jax.ShapeDtypeStruct((rows, hd), F32),
    )
    operands = [
        pltpu.SMEM((seq,), jnp.int32),
        pltpu.VMEM((1, seq), jnp.int32),
        pltpu.VMEM((1, seq), jnp.int32),
        pltpu.VMEM((flat, hd), BF16),
        pltpu.VMEM((flat, hd), BF16),
    ]
    if n == 4:
        kernel = functools.partial(pair_kernel, heads, 256)
        scratch = operands + [
            pltpu.VMEM((seq, hd), BF16),
            pltpu.VMEM((seq, hd), BF16),
            pltpu.VMEM((seq, 2 * hd), BF16),
            pltpu.VMEM((flat, 2 * hd), BF16),
            pltpu.VMEM((hd, flat), BF16),
            pltpu.VMEM((hd, flat), BF16),
            pltpu.VMEM((seq, hd), F32),
            pltpu.VMEM((seq, hd), F32),
            pltpu.VMEM((rows, hd), F32),
            pltpu.VMEM((rows, hd), F32),
            pltpu.VMEM((2 * rows, flat), F32),
            pltpu.VMEM((rows, flat), F32),
            pltpu.VMEM((rows, flat), F32),
            pltpu.VMEM((2 * rows, flat), F32),
            pltpu.VMEM((rows, flat), F32),
            pltpu.VMEM((rows, flat), F32),
            pltpu.VMEM((seq, flat), BF16),
            pltpu.VMEM((seq, flat), BF16),
            pltpu.VMEM((16, flat), F32),
            pltpu.VMEM((hd, seq), BF16),
            pltpu.VMEM((hd, seq), BF16),
            pltpu.VMEM((2, hd, rows), F32),
            pltpu.VMEM((6, hd, rows), BF16),
            pltpu.VMEM((6, hd, rows), BF16),
            pltpu.SemaphoreType.DMA((7,)),
            pltpu.SemaphoreType.DMA((12,)),
            pltpu.SemaphoreType.DMA((12,)),
        ]
    else:
        kernel = functools.partial(ring_kernel, n, heads, 128)
        scratch = operands + [
            pltpu.VMEM((rows, hd), BF16),
            pltpu.VMEM((seq, flat), BF16),
            pltpu.VMEM((hd, seq), BF16),
            pltpu.VMEM((rows, hd), F32),
            pltpu.VMEM((rows, hd), F32),
            pltpu.VMEM((flat, 2 * hd), BF16),
            pltpu.VMEM((seq, hd), BF16),
            pltpu.VMEM((seq, hd), BF16),
            pltpu.VMEM((hd, seq), BF16),
            pltpu.VMEM((seq, flat), BF16),
            pltpu.VMEM((seq, rows), BF16),
            pltpu.VMEM((2, n - 1, rows, hd), BF16),
            pltpu.VMEM((2, n - 1, rows, hd), BF16),
            pltpu.VMEM((rows, hd), F32),
            pltpu.SemaphoreType.DMA((7,)),
            pltpu.SemaphoreType.DMA((4, n - 1)),
            pltpu.SemaphoreType.DMA((4, n - 1)),
        ]
    carried = pl.pallas_call(
        kernel,
        out_shape=shapes,
        in_specs=[hbm] * 7,
        out_specs=(vmem,) * 4,
        scratch_shapes=scratch,
        compiler_params=pltpu.CompilerParams(
            collective_id=0, has_side_effects=True, vmem_limit_bytes=(40 if n == 4 else 58) * 1024 * 1024),
    )(*[pltpu.with_memory_space_constraint(operand, pltpu.HBM) for operand in (
        layout, layout.reshape(1, seq), documents.reshape(1, seq),
        queries.reshape(flat, hd), key_heads.reshape(rows, hd), value_heads.reshape(rows, hd),
        out_grad.reshape(flat, hd),
    )])
    out, dq, dk, dv = pl.pallas_call(
        last_kernel,
        out_shape=shapes,
        in_specs=[vmem] * 4,
        out_specs=(hbm,) * 4,
        scratch_shapes=[pltpu.SemaphoreType.DMA((4,))],
        compiler_params=pltpu.CompilerParams(vmem_limit_bytes=8 * 1024 * 1024),
    )(*carried)
    return (out.reshape(rows, heads, hd), dq.reshape(rows, heads, hd), dk, dv)


def solution(mesh):
    return jax.shard_map(
        functools.partial(body, mesh.shape["context"]),
        mesh=mesh,
        in_specs=(
            P(("dp", "context"), "tensor", None),
            P(("dp", "context"), "tensor", None),
            P(("dp", "context"), "tensor", None),
            P(("dp", "context"), "tensor", None),
            P("dp"),
            P("dp"),
        ),
        out_specs=(
            P(("dp", "context"), "tensor", None),
            P(("dp", "context"), "tensor", None),
            P(("dp", "context"), "tensor"),
            P(("dp", "context"), "tensor"),
        ),
        check_vma=False,
    )
```

```python
import functools
import math

import jax
import jax.numpy as jnp
from jax import lax
from jax.experimental import pallas as pl
from jax.experimental.pallas import tpu as pltpu
from jax.sharding import PartitionSpec as P

THETA = 8000000.0
RUN = 64
MASKED = -1e30
MESH = pl.DeviceIdType.MESH
F32 = jnp.float32
BF16 = jnp.bfloat16


def dot(lhs, rhs, rhs_dim=0):
    return lax.dot_general(lhs, rhs, (((1,), (rhs_dim,)), ((), ())), preferred_element_type=F32)


def sine_cosine(x):
    turns = jnp.floor(x * (2.0 / math.pi) + 0.5)
    r = ((x - turns * 1.5703125) - turns * 4.837512969970703125e-4) - turns * 7.54978995489188216e-8
    z = r * r
    s = r + r * z * (-1.6666654611e-1 + z * (8.3321608736e-3 - z * 1.9515295891e-4))
    c = 1.0 - 0.5 * z + z * z * (4.166664568298827e-2 + z * (-1.388731625493765e-3 + z * 2.443315711809948e-5))
    quarter = turns.astype(jnp.int32)
    odd = (quarter & 1) == 1
    sine = jnp.where(odd, c, s)
    cosine = jnp.where(odd, s, c)
    return (jnp.where((quarter & 2) == 2, -sine, sine), jnp.where(((quarter + 1) & 2) == 2, -cosine, cosine))


def per_token(ref, first, tokens, heads):
    return jnp.concatenate([
        jnp.broadcast_to(ref[first + t:first + t + 1, :], (heads, ref.shape[-1])) for t in range(tokens)], axis=0)


def pair_kernel(heads, chunk, layout_h, layout_row_h, docs_h, q_h, k_h, v_h, g_h,
                o_ref, dq_ref, grad_near, recv_buf, cos_mine, sin_mine,
                layout_s, layout_v, docs_v, q_in, g_in, kraw, vall, kb, qe, q_t, g_t, cos_ref, sin_ref,
                w_near, w_across, w_diagonal, dp_near, dp_across, dp_diagonal, p_t, ds_t, stats, k_t, v_t,
                send_buf,
                local_sem, send_sem, recv_sem):
    n = 4
    me = lax.axis_index("context")
    rows, hd = cos_mine.shape
    seq = n * rows
    half = hd // 2
    tokens = chunk // heads
    steps = rows // tokens
    scale = 1.0 / math.sqrt(hd)
    factor = scale * math.log2(math.e)
    chip, core = me // 2, lax.rem(me, 2)
    partner = chip * 2 + (1 - core)
    across = (1 - chip) * 2 + core
    diagonal = (1 - chip) * 2 + (1 - core)
    owners = (me, partner, across, diagonal)

    def block(role, count=1):
        return slice(role * rows, (role + count) * rows)

    def part(at):
        return slice(at * chunk, (at + 1) * chunk)

    near, far = block(0, 2), block(2, 2)

    barrier = pltpu.get_barrier_semaphore()
    for peer in (across, diagonal, partner):
        pl.semaphore_signal(barrier, inc=1, device_id={"context": peer}, device_id_type=MESH)

    k_copy = pltpu.make_async_copy(k_h, kraw.at[block(0)], local_sem.at[2])
    v_copy = pltpu.make_async_copy(v_h, vall.at[block(0)], local_sem.at[4])
    layout_copy = pltpu.make_async_copy(layout_h, layout_s, local_sem.at[0])
    docs_copy = pltpu.make_async_copy(docs_h, docs_v, local_sem.at[1])
    row_copy = pltpu.make_async_copy(layout_row_h, layout_v, local_sem.at[3])
    q_copy = pltpu.make_async_copy(q_h, q_in, local_sem.at[5])
    g_copy = pltpu.make_async_copy(g_h, g_in, local_sem.at[6])
    for copy in (k_copy, v_copy, layout_copy, docs_copy, row_copy, q_copy, g_copy):
        copy.start()

    def transfer(at, source, target, to):
        return pltpu.make_async_remote_copy(
            src_ref=source, dst_ref=target, send_sem=send_sem.at[at], recv_sem=recv_sem.at[at],
            device_id={"context": to}, device_id_type=MESH)

    k_across = transfer(0, kraw.at[block(0)], kraw.at[block(2)], across)
    k_near = transfer(1, kraw.at[block(0)], kraw.at[block(1)], partner)
    k_diagonal = transfer(2, kraw.at[block(0)], kraw.at[block(3)], diagonal)
    v_across = transfer(3, vall.at[block(0)], vall.at[block(2)], across)
    v_near = transfer(4, vall.at[block(0)], vall.at[block(1)], partner)
    v_diagonal = transfer(5, vall.at[block(0)], vall.at[block(3)], diagonal)
    dv_near = transfer(6, send_buf.at[0], recv_buf.at[0], partner)
    dv_across = transfer(7, send_buf.at[1], recv_buf.at[1], across)
    dv_diagonal = transfer(8, send_buf.at[2], recv_buf.at[2], diagonal)
    dk_near = transfer(9, send_buf.at[3], recv_buf.at[3], partner)
    dk_across = transfer(10, send_buf.at[4], recv_buf.at[4], across)
    dk_diagonal = transfer(11, send_buf.at[5], recv_buf.at[5], diagonal)

    for at in range(steps):
        row = lax.broadcasted_iota(jnp.int32, (chunk, hd), 0) // heads + at * tokens
        col = lax.broadcasted_iota(jnp.int32, (chunk, hd), 1)
        qe[part(at), hd:] = jnp.where(row == col, 1.0, 0.0).astype(BF16)

    k_copy.wait()
    v_copy.wait()
    pl.semaphore_wait(barrier, n - 1)
    for copy in (k_across, k_near, k_diagonal, v_near, v_across, v_diagonal):
        copy.start()

    lane = lax.broadcasted_iota(jnp.int32, (1, hd), 1)
    low = lane < half
    freq = jnp.exp(-(2.0 * lax.rem(lane, half).astype(F32) / hd) * math.log(THETA))
    within = lax.broadcasted_iota(jnp.int32, (RUN, 1), 0).astype(F32)
    docs_copy.wait()
    docs = jnp.broadcast_to(docs_v[...], (8, seq))
    lane_at = lax.broadcasted_iota(jnp.int32, (8, seq), 1)
    starts = jnp.where(docs != pltpu.roll(docs, 1, 1), lane_at, 0).astype(F32)[:1]
    layout_copy.wait()

    def places(owner):
        found = []
        for run in range(rows // RUN):
            token = within + layout_s[owner * rows + run * RUN].astype(F32)
            start = jnp.max(jnp.where(starts <= token, starts, 0.0), axis=1, keepdims=True)
            found.append((token, start))
        return found

    def tables(found):
        (token_a, start_a), (token_b, start_b) = found
        sine, cosine = sine_cosine(jnp.where(low, token_a - start_a, token_b - start_b) * freq)
        sine_r, cosine_r = pltpu.roll(sine, half, 1), pltpu.roll(cosine, half, 1)
        c = jnp.concatenate([jnp.where(low, cosine, cosine_r), jnp.where(low, cosine_r, cosine)], axis=0)
        s = jnp.concatenate([jnp.where(low, -sine, sine_r), jnp.where(low, -sine_r, sine)], axis=0)
        return c, s

    def rotate(x, c, s):
        return x * c + pltpu.roll(x, half, 1) * s

    def rotate_keys(role, c, s):
        kb[block(role), :hd] = rotate(kraw[block(role), :].astype(F32), c, s).astype(BF16)

    found = places(me)
    c, s = tables(found)
    cos_mine[...] = c
    sin_mine[...] = s
    rotate_keys(0, c, s)
    token = jnp.concatenate([t for t, _ in found], axis=0)
    start = jnp.concatenate([t for _, t in found], axis=0)
    row_copy.wait()
    for role in range(n):
        keys = layout_v[:, pl.ds(pl.multiple_of(owners[role] * rows, rows), rows)].astype(F32)
        kb[block(role), hd:] = jnp.where((keys >= start) & (keys <= token), 0.0, MASKED).T.astype(BF16)
    q_copy.wait()
    for at in range(steps):
        cosines = per_token(cos_mine, at * tokens, tokens, heads)
        sines = per_token(sin_mine, at * tokens, tokens, heads)
        rotated = rotate(q_in[part(at), :].astype(F32), cosines, sines)
        qe[part(at), :hd] = rotated.astype(BF16)
        q_t[:, part(at)] = rotated.T.astype(BF16)
    g_copy.wait()
    for at in range(steps):
        g_t[:, part(at)] = g_in[part(at), :].astype(F32).T.astype(BF16)
    for role in (1, 2, 3):
        c, s = tables(places(owners[role]))
        cos_ref[block(role), :] = c
        sin_ref[block(role), :] = s

    def score(role, count, w_ref, at, chunk_at):
        here = part(chunk_at)
        scores = dot(kb[block(role, count), :], qe[here, :], 1)
        largest = jnp.max(scores, axis=0, keepdims=True)
        weights = jnp.exp2((scores - largest) * factor)
        w_ref[:, here] = weights
        stats[3 * at:3 * at + 1, here] = largest
        stats[3 * at + 1:3 * at + 2, here] = jnp.sum(weights, axis=0, keepdims=True)

    def back(role, count, w_ref, dp_ref, at, chunk_at):
        here = part(chunk_at)
        dprobs = dot(vall[block(role, count), :], g_in[here, :], 1)
        dp_ref[:, here] = dprobs
        stats[3 * at + 2:3 * at + 3, here] = jnp.sum(w_ref[:, here] * dprobs, axis=0, keepdims=True)

    def arrived(role):
        rotate_keys(role, cos_ref[block(role), :], sin_ref[block(role), :])

    k_near.wait_recv()
    arrived(1)
    v_near.wait_recv()
    for at in range(steps):
        score(0, 2, w_near, 0, at)
        back(0, 2, w_near, dp_near, 0, at)

    k_across.wait_recv()
    arrived(2)
    for at in range(steps):
        score(2, 1, w_across, 1, at)
    k_diagonal.wait_recv()
    arrived(3)
    for at in range(steps):
        here = part(at)
        score(3, 1, w_diagonal, 2, at)
        maxima = [stats[3 * b:3 * b + 1, here] for b in range(3)]
        largest = jnp.maximum(jnp.maximum(maxima[0], maxima[1]), maxima[2])
        shrink = [jnp.exp2((m - largest) * factor) for m in maxima]
        inverse = 1.0 / sum(shrink[b] * stats[3 * b + 1:3 * b + 2, here] for b in range(3))
        weight = [shrink[b] * inverse for b in range(3)]
        stats[9:10, here] = weight[0]
        stats[10:11, here] = weight[0] * stats[2:3, here]
        stats[12:13, here] = weight[2]
        p = w_across[:, here] * weight[1]
        w_across[:, here] = p
        p_t[block(2), here] = p.astype(BF16)
    send_buf[1] = dot(g_t[...], p_t[block(2), :], 1).astype(BF16)
    dv_across.start()
    for at in range(steps):
        here = part(at)
        p = w_diagonal[:, here] * stats[12:13, here]
        w_diagonal[:, here] = p
        p_t[block(3), here] = p.astype(BF16)
    send_buf[2] = dot(g_t[...], p_t[block(3), :], 1).astype(BF16)
    dv_diagonal.start()

    v_across.wait_recv()
    for at in range(steps):
        back(2, 1, w_across, dp_across, 1, at)
    v_diagonal.wait_recv()
    for at in range(steps):
        here = part(at)
        back(3, 1, w_diagonal, dp_diagonal, 2, at)
        delta = stats[10:11, here] + stats[5:6, here] + stats[8:9, here]
        stats[11:12, here] = delta
        ds_t[block(2), here] = (w_across[:, here] * (dp_across[:, here] - delta)).astype(BF16)
    send_buf[4] = dot(q_t[...], ds_t[block(2), :], 1).astype(BF16)
    dk_across.start()
    for at in range(steps):
        here = part(at)
        ds_t[block(3), here] = (w_diagonal[:, here] * (dp_diagonal[:, here] - stats[11:12, here])).astype(BF16)
    send_buf[5] = dot(q_t[...], ds_t[block(3), :], 1).astype(BF16)
    dk_diagonal.start()

    for at in range(steps):
        here = part(at)
        p = w_near[:, here] * stats[9:10, here]
        p_t[near, here] = p.astype(BF16)
        ds_t[near, here] = (p * (dp_near[:, here] - stats[11:12, here])).astype(BF16)
    for kind, left, right in ((0, g_t, p_t), (1, q_t, ds_t)):
        grad = dot(left[...], right[near, :], 1)
        send_buf[3 * kind] = grad[:, rows:].astype(BF16)
        (dv_near, dk_near)[kind].start()
        grad_near[kind] = grad[:, :rows]

    k_t[...] = kb[:, :hd].astype(F32).T.astype(BF16)
    v_t[...] = vall[...].astype(F32).T.astype(BF16)
    for at in range(steps):
        o_ref[part(at), :] = dot(v_t[...], p_t[:, part(at)]).T.astype(BF16)
    cos_mine[...] = cos_mine[...] * scale
    sin_mine[...] = sin_mine[...] * -scale
    for at in range(steps):
        cosines = per_token(cos_mine, at * tokens, tokens, heads)
        sines = per_token(sin_mine, at * tokens, tokens, heads)
        dq_ref[part(at), :] = rotate(dot(k_t[...], ds_t[:, part(at)]).T, cosines, sines).astype(BF16)

    for copy in (dv_near, dk_near, dv_across, dv_diagonal, dk_across, dk_diagonal):
        copy.wait_recv()
    for copy in (k_across, k_near, k_diagonal, v_across, v_near, v_diagonal,
                 dv_near, dv_across, dv_diagonal, dk_near, dk_across, dk_diagonal):
        copy.wait_send()


def loop(count, step):
    if count <= 8:
        for index in range(count):
            step(index)
    else:
        lax.fori_loop(0, count, lambda index, _: (step(index), None)[1], None)


def span(at, size):
    start = at * size
    return pl.ds(start if isinstance(at, int) else pl.multiple_of(start, size), size)


def rotate(x, cosine, sine):
    return x * cosine + pltpu.roll(x, x.shape[-1] // 2, 1) * sine


def spread(ref, at, chunk, heads):
    part = ref[span(at, chunk // heads), :]
    return jnp.broadcast_to(part[:, None, :], (chunk // heads, heads, part.shape[-1])).reshape(chunk, -1)


def ring_kernel(n, heads, chunk, layout_h, layout_row_h, docs_h, q_h, k_h, v_h, g_h,
                o_ref, dq_ref, dk_ref, dv_ref,
                layout_s, layout_v, docs_v, q_in, g_in, k_in, probs, k_t, cos_ref, sin_ref, qe, kall, vall, v_t, p_t, bias_t,
                send_buf, recv_buf, own_dv, local_sem, send_sem, recv_sem):
    me = lax.axis_index("context")
    rows, hd = k_in.shape
    seq = rows * n
    flat = rows * heads
    tokens = chunk // heads
    steps = flat // chunk
    scale = 1.0 / math.sqrt(hd)

    factor = scale * math.log2(math.e)

    def peer(k):
        pair = lax.rem(me // 2 + (k + 1) // 2, n // 2)
        return pair * 2 + lax.rem(me + k + 1, 2)

    barrier = pltpu.get_barrier_semaphore()
    for k in range(n - 1):
        pl.semaphore_signal(barrier, inc=1, device_id={"context": peer(k)}, device_id_type=MESH)

    mine = span(me, rows)
    layout_copy = pltpu.make_async_copy(layout_h, layout_s, local_sem.at[0])
    docs_copy = pltpu.make_async_copy(docs_h, docs_v, local_sem.at[1])
    k_copy = pltpu.make_async_copy(k_h, k_in, local_sem.at[2])
    row_copy = pltpu.make_async_copy(layout_row_h, layout_v, local_sem.at[3])
    v_copy = pltpu.make_async_copy(v_h, vall.at[mine], local_sem.at[4])
    q_copy = pltpu.make_async_copy(q_h, q_in, local_sem.at[5])
    g_copy = pltpu.make_async_copy(g_h, g_in, local_sem.at[6])
    for copy in (layout_copy, docs_copy, k_copy, v_copy, row_copy, q_copy, g_copy):
        copy.start()

    half = hd // 2
    lane = lax.broadcasted_iota(jnp.int32, (1, hd), 1)
    freq = jnp.exp(-(2.0 * lax.rem(lane, half).astype(F32) / hd) * math.log(THETA))
    row_at = lax.broadcasted_iota(jnp.int32, (rows, hd), 0)
    layout_copy.wait()
    first = layout_s[me * rows].astype(F32)
    second = layout_s[me * rows + RUN].astype(F32)
    token = jnp.where(row_at < RUN, row_at.astype(F32) + first, (row_at - RUN).astype(F32) + second)
    token = token[:, :1]
    docs_copy.wait()
    docs = jnp.broadcast_to(docs_v[...], (8, seq))
    lane_at = lax.broadcasted_iota(jnp.int32, (8, seq), 1)
    starts = jnp.where(docs != pltpu.roll(docs, 1, 1), lane_at, 0).astype(F32)[:1]
    start = jnp.max(jnp.where(starts <= token, starts, 0.0), axis=1, keepdims=True)
    angles = (token - start) * freq
    cosine = jnp.cos(angles)
    sine = jnp.where(lane < half, -1.0, 1.0) * jnp.sin(angles)
    cos_ref[...] = cosine
    sin_ref[...] = sine
    k_copy.wait()
    kall[mine] = rotate(k_in[...].astype(F32), cosine, sine).astype(BF16)
    v_copy.wait()

    pl.semaphore_wait(barrier, n - 1)

    def transfer(kind, k, source, target):
        return pltpu.make_async_remote_copy(
            src_ref=source, dst_ref=target,
            send_sem=send_sem.at[kind, k], recv_sem=recv_sem.at[kind, k],
            device_id={"context": peer(k)}, device_id_type=MESH)

    def k_send(k):
        return transfer(0, k, kall.at[mine], kall.at[mine])

    def v_send(k):
        return transfer(1, k, vall.at[mine], vall.at[mine])

    def g_send(kind, k):
        return transfer(2 + kind, k, send_buf.at[kind, k], recv_buf.at[kind, k])

    loop(n - 1, lambda k: k_send(n - 2 - k).start())

    row_copy.wait()
    keys = layout_v[...].astype(F32)
    bias_t[...] = jnp.where((keys >= start) & (keys <= token), 0.0, MASKED).T.astype(BF16)
    q_copy.wait()

    def make_q(at):
        here = span(at, chunk)
        cosines, sines = spread(cos_ref, at, chunk, heads), spread(sin_ref, at, chunk, heads)
        qe[here, :hd] = rotate(q_in[here, :].astype(F32), cosines, sines).astype(BF16)
        row = lax.broadcasted_iota(jnp.int32, (chunk, hd), 0) // heads + at * tokens
        col = lax.broadcasted_iota(jnp.int32, (chunk, hd), 1)
        qe[here, hd:] = (row == col).astype(F32).astype(BF16)

    loop(steps, make_q)

    def make_probs(at):
        here = span(at, chunk)
        scores = dot(jnp.concatenate([kall[...], bias_t[...]], axis=1), qe[here, :], 1)
        largest = jnp.max(scores, axis=0, keepdims=True)
        weights = jnp.exp2((scores - largest) * factor)
        total = jnp.sum(weights, axis=0, keepdims=True)
        p_t[:, here] = (weights * (1.0 / total)).astype(BF16)

    loop(n - 1, lambda k: k_send(k).wait_recv())
    loop(n - 1, lambda k: v_send(k).start())
    loop(steps, make_probs)
    g_copy.wait()

    def v_grads(k):
        send_buf[0, k] = dot(p_t[span(peer(k), rows), :], g_in[...]).astype(BF16)
        g_send(0, k).start()

    loop(n - 1, lambda k: v_grads(n - 2 - k))
    loop(n - 1, lambda k: v_send(k).wait_recv())

    def make_ds(at):
        here = span(at, chunk)
        dprobs = dot(vall[...], g_in[here, :], 1)
        p = p_t[:, here].astype(F32)
        delta = jnp.sum(p * dprobs, axis=0, keepdims=True)
        probs[:, here] = (p * (dprobs - delta)).astype(BF16)

    loop(steps, make_ds)

    def k_grads(k):
        send_buf[1, k] = (dot(probs[span(peer(k), rows), :], qe[:, :hd]) * scale).astype(BF16)
        g_send(1, k).start()

    loop(n - 1, lambda k: k_grads(n - 2 - k))
    own_dk = dot(probs[mine, :], qe[:, :hd]) * scale
    own_dv[...] = dot(p_t[mine, :], g_in[...])
    k_t[...] = kall[...].astype(F32).T.astype(BF16)
    v_t[...] = vall[...].astype(F32).T.astype(BF16)

    def make_o(at):
        here = span(at, chunk)
        o_ref[here, :] = dot(v_t[...], p_t[:, here]).T.astype(BF16)

    def make_dq(at):
        here = span(at, chunk)
        grad = dot(k_t[...], probs[:, here]).T * scale
        cosines, sines = spread(cos_ref, at, chunk, heads), spread(sin_ref, at, chunk, heads)
        dq_ref[here, :] = rotate(grad, cosines, -sines).astype(BF16)

    loop(steps, make_o)
    loop(steps, make_dq)

    def collect(kind, own):
        loop(n - 1, lambda k: g_send(kind, k).wait_recv())
        return own + jnp.sum(recv_buf[kind].astype(F32), axis=0)

    dv_ref[...] = collect(0, own_dv[...])
    dk_ref[...] = rotate(collect(1, own_dk), cos_ref[...], -sin_ref[...])

    def finish(k):
        k_send(k).wait_send()
        v_send(k).wait_send()
        g_send(0, k).wait_send()
        g_send(1, k).wait_send()

    loop(n - 1, finish)


def last_kernel(*refs):
    count = len(refs) // 2
    sem = refs[-1]
    copies = [pltpu.make_async_copy(refs[at], refs[count + at], sem.at[at]) for at in range(count)]
    for copy in copies:
        copy.start()
    for copy in copies:
        copy.wait()


def sum_kernel(o_in, dq_in, grad_near, parts, cosine, sine, o_h, dq_h, dk_h, dv_h, dk, dv, sem):
    copies = [pltpu.make_async_copy(source, target, sem.at[at]) for at, (source, target) in enumerate(
        ((o_in, o_h), (dq_in, dq_h), (dv, dv_h), (dk, dk_h)))]
    copies[0].start()
    copies[1].start()

    def total(kind):
        return (grad_near[kind] + sum(parts[3 * kind + at].astype(F32) for at in range(3))).T

    dv[...] = total(0)
    copies[2].start()
    grad = total(1)
    dk[...] = grad * cosine[...] + pltpu.roll(grad, grad.shape[-1] // 2, 1) * sine[...]
    copies[3].start()
    for copy in copies:
        copy.wait()


def body(n, queries, key_heads, value_heads, out_grad, layout, documents):
    rows, heads, hd = queries.shape
    seq = layout.shape[0]
    flat = rows * heads
    hbm = pl.BlockSpec(memory_space=pltpu.HBM)
    vmem = pl.BlockSpec(memory_space=pltpu.VMEM)
    shapes = (
        jax.ShapeDtypeStruct((flat, hd), BF16),
        jax.ShapeDtypeStruct((flat, hd), BF16),
        jax.ShapeDtypeStruct((rows, hd), F32),
        jax.ShapeDtypeStruct((rows, hd), F32),
    )
    operands = [
        pltpu.SMEM((seq,), jnp.int32),
        pltpu.VMEM((1, seq), jnp.int32),
        pltpu.VMEM((1, seq), jnp.int32),
        pltpu.VMEM((flat, hd), BF16),
        pltpu.VMEM((flat, hd), BF16),
    ]
    if n == 4:
        kernel = functools.partial(pair_kernel, heads, 256)
        scratch = operands + [
            pltpu.VMEM((seq, hd), BF16),
            pltpu.VMEM((seq, hd), BF16),
            pltpu.VMEM((seq, 2 * hd), BF16),
            pltpu.VMEM((flat, 2 * hd), BF16),
            pltpu.VMEM((hd, flat), BF16),
            pltpu.VMEM((hd, flat), BF16),
            pltpu.VMEM((seq, hd), F32),
            pltpu.VMEM((seq, hd), F32),
            pltpu.VMEM((2 * rows, flat), F32),
            pltpu.VMEM((rows, flat), F32),
            pltpu.VMEM((rows, flat), F32),
            pltpu.VMEM((2 * rows, flat), F32),
            pltpu.VMEM((rows, flat), F32),
            pltpu.VMEM((rows, flat), F32),
            pltpu.VMEM((seq, flat), BF16),
            pltpu.VMEM((seq, flat), BF16),
            pltpu.VMEM((16, flat), F32),
            pltpu.VMEM((hd, seq), BF16),
            pltpu.VMEM((hd, seq), BF16),
            pltpu.VMEM((6, hd, rows), BF16),
            pltpu.SemaphoreType.DMA((7,)),
            pltpu.SemaphoreType.DMA((12,)),
            pltpu.SemaphoreType.DMA((12,)),
        ]
    else:
        kernel = functools.partial(ring_kernel, n, heads, 128)
        scratch = operands + [
            pltpu.VMEM((rows, hd), BF16),
            pltpu.VMEM((seq, flat), BF16),
            pltpu.VMEM((hd, seq), BF16),
            pltpu.VMEM((rows, hd), F32),
            pltpu.VMEM((rows, hd), F32),
            pltpu.VMEM((flat, 2 * hd), BF16),
            pltpu.VMEM((seq, hd), BF16),
            pltpu.VMEM((seq, hd), BF16),
            pltpu.VMEM((hd, seq), BF16),
            pltpu.VMEM((seq, flat), BF16),
            pltpu.VMEM((seq, rows), BF16),
            pltpu.VMEM((2, n - 1, rows, hd), BF16),
            pltpu.VMEM((2, n - 1, rows, hd), BF16),
            pltpu.VMEM((rows, hd), F32),
            pltpu.SemaphoreType.DMA((7,)),
            pltpu.SemaphoreType.DMA((4, n - 1)),
            pltpu.SemaphoreType.DMA((4, n - 1)),
        ]
    if n == 4:
        carry = shapes[:2] + (
            jax.ShapeDtypeStruct((2, hd, rows), F32),
            jax.ShapeDtypeStruct((6, hd, rows), BF16),
            jax.ShapeDtypeStruct((rows, hd), F32),
            jax.ShapeDtypeStruct((rows, hd), F32),
        )
        last = sum_kernel
        last_scratch = [pltpu.VMEM((rows, hd), F32), pltpu.VMEM((rows, hd), F32)]
    else:
        carry, last, last_scratch = shapes, last_kernel, []
    carried = pl.pallas_call(
        kernel,
        out_shape=carry,
        in_specs=[hbm] * 7,
        out_specs=(vmem,) * len(carry),
        scratch_shapes=scratch,
        compiler_params=pltpu.CompilerParams(
            collective_id=0, has_side_effects=True, vmem_limit_bytes=(40 if n == 4 else 58) * 1024 * 1024),
    )(*[pltpu.with_memory_space_constraint(operand, pltpu.HBM) for operand in (
        layout, layout.reshape(1, seq), documents.reshape(1, seq),
        queries.reshape(flat, hd), key_heads.reshape(rows, hd), value_heads.reshape(rows, hd),
        out_grad.reshape(flat, hd),
    )])
    out, dq, dk, dv = pl.pallas_call(
        last,
        out_shape=shapes,
        in_specs=[vmem] * len(carry),
        out_specs=(hbm,) * 4,
        scratch_shapes=last_scratch + [pltpu.SemaphoreType.DMA((4,))],
        compiler_params=pltpu.CompilerParams(vmem_limit_bytes=8 * 1024 * 1024),
    )(*carried)
    return (out.reshape(rows, heads, hd), dq.reshape(rows, heads, hd), dk, dv)


def solution(mesh):
    return jax.shard_map(
        functools.partial(body, mesh.shape["context"]),
        mesh=mesh,
        in_specs=(
            P(("dp", "context"), "tensor", None),
            P(("dp", "context"), "tensor", None),
            P(("dp", "context"), "tensor", None),
            P(("dp", "context"), "tensor", None),
            P("dp"),
            P("dp"),
        ),
        out_specs=(
            P(("dp", "context"), "tensor", None),
            P(("dp", "context"), "tensor", None),
            P(("dp", "context"), "tensor"),
            P(("dp", "context"), "tensor"),
        ),
        check_vma=False,
    )
```

```python
import functools
import math

import jax
import jax.numpy as jnp
from jax import lax
from jax.experimental import pallas as pl
from jax.experimental.pallas import tpu as pltpu
from jax.sharding import PartitionSpec as P

THETA = 8000000.0
RUN = 64
MASKED = -1e30
MESH = pl.DeviceIdType.MESH
F32 = jnp.float32
BF16 = jnp.bfloat16


def dot(lhs, rhs, rhs_dim=0):
    return lax.dot_general(lhs, rhs, (((1,), (rhs_dim,)), ((), ())), preferred_element_type=F32)


def sine_cosine(x):
    turns = jnp.floor(x * (2.0 / math.pi) + 0.5)
    r = ((x - turns * 1.5703125) - turns * 4.837512969970703125e-4) - turns * 7.54978995489188216e-8
    z = r * r
    s = r + r * z * (-1.6666654611e-1 + z * (8.3321608736e-3 - z * 1.9515295891e-4))
    c = 1.0 - 0.5 * z + z * z * (4.166664568298827e-2 + z * (-1.388731625493765e-3 + z * 2.443315711809948e-5))
    quarter = turns.astype(jnp.int32)
    odd = (quarter & 1) == 1
    sine = jnp.where(odd, c, s)
    cosine = jnp.where(odd, s, c)
    return (jnp.where((quarter & 2) == 2, -sine, sine), jnp.where(((quarter + 1) & 2) == 2, -cosine, cosine))


def per_token(ref, first, tokens, heads):
    return jnp.concatenate([
        jnp.broadcast_to(ref[first + t:first + t + 1, :], (heads, ref.shape[-1])) for t in range(tokens)], axis=0)


def pair_kernel(heads, chunk, layout_h, layout_row_h, docs_h, q_h, k_h, v_h, g_h,
                o_ref, dq_ref, grad_near, recv_buf, cos_mine, sin_mine,
                layout_s, layout_v, docs_v, q_in, g_in, kraw, vall, kb, q_t, g_t, cos_ref, sin_ref,
                w_near, w_far, dp_near, dp_far, p_t, ds_t, stats, k_t, v_t,
                send_buf,
                local_sem, send_sem, recv_sem):
    n = 4
    me = lax.axis_index("context")
    rows, hd = cos_mine.shape
    seq = n * rows
    half = hd // 2
    tokens = chunk // heads
    steps = rows // tokens
    scale = 1.0 / math.sqrt(hd)
    factor = scale * math.log2(math.e)
    chip, core = me // 2, lax.rem(me, 2)
    partner = chip * 2 + (1 - core)
    far0 = (1 - chip) * 2
    owners = (me, partner, far0, far0 + 1)

    def block(role, count=1):
        return slice(role * rows, (role + count) * rows)

    def part(at):
        return slice(at * chunk, (at + 1) * chunk)

    near, far = block(0, 2), block(2, 2)

    barrier = pltpu.get_barrier_semaphore()
    for peer in (far0, far0 + 1, partner):
        pl.semaphore_signal(barrier, inc=1, device_id={"context": peer}, device_id_type=MESH)

    k_copy = pltpu.make_async_copy(k_h, kraw.at[block(0)], local_sem.at[2])
    v_copy = pltpu.make_async_copy(v_h, vall.at[block(0)], local_sem.at[4])
    layout_copy = pltpu.make_async_copy(layout_h, layout_s, local_sem.at[0])
    docs_copy = pltpu.make_async_copy(docs_h, docs_v, local_sem.at[1])
    row_copy = pltpu.make_async_copy(layout_row_h, layout_v, local_sem.at[3])
    q_copy = pltpu.make_async_copy(q_h, q_in, local_sem.at[5])
    g_copy = pltpu.make_async_copy(g_h, g_in, local_sem.at[6])
    for copy in (k_copy, v_copy, layout_copy, docs_copy, row_copy, q_copy, g_copy):
        copy.start()

    def transfer(at, source, target, to):
        return pltpu.make_async_remote_copy(
            src_ref=source, dst_ref=target, send_sem=send_sem.at[at], recv_sem=recv_sem.at[at],
            device_id={"context": to}, device_id_type=MESH)

    def slot(ref, at):
        return ref.at[pl.ds(pl.multiple_of((2 + at) * rows, rows), rows)]

    def to_far(kind, to, source, target):
        return pltpu.make_async_remote_copy(
            src_ref=source, dst_ref=target, send_sem=send_sem.at[2 * kind + to], recv_sem=recv_sem.at[2 * kind + core],
            device_id={"context": far0 + to}, device_id_type=MESH)

    def from_far(kind, at, target):
        return pltpu.make_async_remote_copy(
            src_ref=target, dst_ref=target, send_sem=send_sem.at[2 * kind], recv_sem=recv_sem.at[2 * kind + at],
            device_id={"context": far0}, device_id_type=MESH)

    k_far = [to_far(0, to, kraw.at[block(0)], slot(kraw, core)) for to in (0, 1)]
    v_far = [to_far(1, to, vall.at[block(0)], slot(vall, core)) for to in (0, 1)]
    dv_far = [to_far(2, to, send_buf.at[1 + to], recv_buf.at[1 + core]) for to in (0, 1)]
    dk_far = [to_far(3, to, send_buf.at[4 + to], recv_buf.at[4 + core]) for to in (0, 1)]
    k_near = transfer(8, kraw.at[block(0)], kraw.at[block(1)], partner)
    v_near = transfer(9, vall.at[block(0)], vall.at[block(1)], partner)
    dv_near = transfer(10, send_buf.at[0], recv_buf.at[0], partner)
    dk_near = transfer(11, send_buf.at[3], recv_buf.at[3], partner)

    for at in range(steps):
        row = lax.broadcasted_iota(jnp.int32, (rows, chunk), 0)
        col = lax.broadcasted_iota(jnp.int32, (rows, chunk), 1) // heads + at * tokens
        q_t[hd:, part(at)] = jnp.where(row == col, 1.0, 0.0).astype(BF16)

    k_copy.wait()
    v_copy.wait()
    pl.semaphore_wait(barrier, n - 1)
    for copy in (k_far[0], k_near, k_far[1], v_near, v_far[0], v_far[1]):
        copy.start()

    lane = lax.broadcasted_iota(jnp.int32, (1, hd), 1)
    low = lane < half
    freq = jnp.exp(-(2.0 * lax.rem(lane, half).astype(F32) / hd) * math.log(THETA))
    within = lax.broadcasted_iota(jnp.int32, (RUN, 1), 0).astype(F32)
    docs_copy.wait()
    docs = jnp.broadcast_to(docs_v[...], (8, seq))
    lane_at = lax.broadcasted_iota(jnp.int32, (8, seq), 1)
    starts = jnp.where(docs != pltpu.roll(docs, 1, 1), lane_at, 0).astype(F32)[:1]
    layout_copy.wait()

    def places(owner):
        found = []
        for run in range(rows // RUN):
            token = within + layout_s[owner * rows + run * RUN].astype(F32)
            start = jnp.max(jnp.where(starts <= token, starts, 0.0), axis=1, keepdims=True)
            found.append((token, start))
        return found

    def tables(found):
        (token_a, start_a), (token_b, start_b) = found
        sine, cosine = sine_cosine(jnp.where(low, token_a - start_a, token_b - start_b) * freq)
        sine_r, cosine_r = pltpu.roll(sine, half, 1), pltpu.roll(cosine, half, 1)
        c = jnp.concatenate([jnp.where(low, cosine, cosine_r), jnp.where(low, cosine_r, cosine)], axis=0)
        s = jnp.concatenate([jnp.where(low, -sine, sine_r), jnp.where(low, -sine_r, sine)], axis=0)
        return c, s

    def rotate(x, c, s):
        return x * c + pltpu.roll(x, half, 1) * s

    def rotate_keys(role, c, s):
        kb[block(role), :hd] = rotate(kraw[block(role), :].astype(F32), c, s).astype(BF16)

    found = places(me)
    c, s = tables(found)
    cos_mine[...] = c
    sin_mine[...] = s
    rotate_keys(0, c, s)
    token = jnp.concatenate([t for t, _ in found], axis=0)
    start = jnp.concatenate([t for _, t in found], axis=0)
    row_copy.wait()
    for role in range(n):
        keys = layout_v[:, pl.ds(pl.multiple_of(owners[role] * rows, rows), rows)].astype(F32)
        kb[block(role), hd:] = jnp.where((keys >= start) & (keys <= token), 0.0, MASKED).T.astype(BF16)
    q_copy.wait()
    for at in range(steps):
        cosines = per_token(cos_mine, at * tokens, tokens, heads)
        sines = per_token(sin_mine, at * tokens, tokens, heads)
        rotated = rotate(q_in[part(at), :].astype(F32), cosines, sines)
        q_t[:hd, part(at)] = rotated.T.astype(BF16)
    g_copy.wait()
    for at in range(steps):
        g_t[:, part(at)] = g_in[part(at), :].astype(F32).T.astype(BF16)
    for role in (1, 2, 3):
        c, s = tables(places(owners[role]))
        cos_ref[block(role), :] = c
        sin_ref[block(role), :] = s

    def score(role, count, w_ref, at, chunk_at):
        here = part(chunk_at)
        scores = dot(kb[block(role, count), :], q_t[:, here])
        largest = jnp.max(scores, axis=0, keepdims=True)
        weights = jnp.exp2((scores - largest) * factor)
        w_ref[:, here] = weights
        stats[3 * at:3 * at + 1, here] = largest
        stats[3 * at + 1:3 * at + 2, here] = jnp.sum(weights, axis=0, keepdims=True)

    def back(role, count, w_ref, dp_ref, at, chunk_at):
        here = part(chunk_at)
        dprobs = dot(vall[block(role, count), :], g_t[:, here])
        dp_ref[:, here] = dprobs
        stats[3 * at + 2:3 * at + 3, here] = jnp.sum(w_ref[:, here] * dprobs, axis=0, keepdims=True)

    def arrived(role):
        rotate_keys(role, cos_ref[block(role), :], sin_ref[block(role), :])

    k_near.wait_recv()
    arrived(1)
    v_near.wait_recv()
    for at in range(steps):
        score(0, 2, w_near, 0, at)
        back(0, 2, w_near, dp_near, 0, at)

    for at in (0, 1):
        from_far(0, at, slot(kraw, at)).wait_recv()
        arrived(2 + at)
    for at in range(steps):
        here = part(at)
        score(2, 2, w_far, 1, at)
        largest = jnp.maximum(stats[0:1, here], stats[3:4, here])
        shrink = [jnp.exp2((stats[b:b + 1, here] - largest) * factor) for b in (0, 3)]
        inverse = 1.0 / (shrink[0] * stats[1:2, here] + shrink[1] * stats[4:5, here])
        weight = shrink[0] * inverse
        stats[9:10, here] = weight
        stats[10:11, here] = weight * stats[2:3, here]
        stats[12:13, here] = shrink[1] * inverse
        p = w_far[:rows, here] * stats[12:13, here]
        w_far[:rows, here] = p
        p_t[block(2), here] = p.astype(BF16)
    send_buf[1] = dot(g_t[...], p_t[block(2), :], 1).astype(BF16)
    dv_far[0].start()
    for at in range(steps):
        here = part(at)
        p = w_far[rows:, here] * stats[12:13, here]
        w_far[rows:, here] = p
        p_t[block(3), here] = p.astype(BF16)
    send_buf[2] = dot(g_t[...], p_t[block(3), :], 1).astype(BF16)
    dv_far[1].start()
    for at in (0, 1):
        from_far(1, at, slot(vall, at)).wait_recv()
    for at in range(steps):
        here = part(at)
        back(2, 2, w_far, dp_far, 1, at)
        stats[11:12, here] = stats[10:11, here] + stats[5:6, here]
        ds_t[block(2), here] = (w_far[:rows, here] * (dp_far[:rows, here] - stats[11:12, here])).astype(BF16)
    send_buf[4] = dot(q_t[:hd, :], ds_t[block(2), :], 1).astype(BF16)
    dk_far[0].start()
    for at in range(steps):
        here = part(at)
        ds_t[block(3), here] = (w_far[rows:, here] * (dp_far[rows:, here] - stats[11:12, here])).astype(BF16)
    send_buf[5] = dot(q_t[:hd, :], ds_t[block(3), :], 1).astype(BF16)
    dk_far[1].start()
    for at in range(steps):
        here = part(at)
        p = w_near[:, here] * stats[9:10, here]
        p_t[near, here] = p.astype(BF16)
        ds_t[near, here] = (p * (dp_near[:, here] - stats[11:12, here])).astype(BF16)
    for kind, left, right in ((0, g_t, p_t), (1, q_t.at[:hd], ds_t)):
        grad = dot(left[...], right[near, :], 1)
        send_buf[3 * kind] = grad[:, rows:].astype(BF16)
        (dv_near, dk_near)[kind].start()
        grad_near[kind] = grad[:, :rows]

    k_t[...] = kb[:, :hd].astype(F32).T.astype(BF16)
    v_t[...] = vall[...].astype(F32).T.astype(BF16)
    for at in range(steps):
        o_ref[part(at), :] = dot(v_t[...], p_t[:, part(at)]).T.astype(BF16)
    cos_mine[...] = cos_mine[...] * scale
    sin_mine[...] = sin_mine[...] * -scale
    for at in range(steps):
        cosines = per_token(cos_mine, at * tokens, tokens, heads)
        sines = per_token(sin_mine, at * tokens, tokens, heads)
        dq_ref[part(at), :] = rotate(dot(k_t[...], ds_t[:, part(at)]).T, cosines, sines).astype(BF16)

    dv_near.wait_recv()
    dk_near.wait_recv()
    for kind in (2, 3):
        for at in (0, 1):
            from_far(kind, at, recv_buf.at[3 * (kind - 2) + 1 + at]).wait_recv()
    for copy in (k_near, v_near, dv_near, dk_near, *k_far, *v_far, *dv_far, *dk_far):
        copy.wait_send()


def loop(count, step):
    if count <= 8:
        for index in range(count):
            step(index)
    else:
        lax.fori_loop(0, count, lambda index, _: (step(index), None)[1], None)


def span(at, size):
    start = at * size
    return pl.ds(start if isinstance(at, int) else pl.multiple_of(start, size), size)


def rotate(x, cosine, sine):
    return x * cosine + pltpu.roll(x, x.shape[-1] // 2, 1) * sine


def spread(ref, at, chunk, heads):
    part = ref[span(at, chunk // heads), :]
    return jnp.broadcast_to(part[:, None, :], (chunk // heads, heads, part.shape[-1])).reshape(chunk, -1)


def ring_kernel(n, heads, chunk, layout_h, layout_row_h, docs_h, q_h, k_h, v_h, g_h,
                o_ref, dq_ref, dk_ref, dv_ref,
                layout_s, layout_v, docs_v, q_in, g_in, k_in, probs, k_t, cos_ref, sin_ref, qe, kall, vall, v_t, p_t, bias_t,
                send_buf, recv_buf, own_dv, local_sem, send_sem, recv_sem):
    me = lax.axis_index("context")
    rows, hd = k_in.shape
    seq = rows * n
    flat = rows * heads
    tokens = chunk // heads
    steps = flat // chunk
    scale = 1.0 / math.sqrt(hd)

    factor = scale * math.log2(math.e)

    def peer(k):
        pair = lax.rem(me // 2 + (k + 1) // 2, n // 2)
        return pair * 2 + lax.rem(me + k + 1, 2)

    barrier = pltpu.get_barrier_semaphore()
    for k in range(n - 1):
        pl.semaphore_signal(barrier, inc=1, device_id={"context": peer(k)}, device_id_type=MESH)

    mine = span(me, rows)
    layout_copy = pltpu.make_async_copy(layout_h, layout_s, local_sem.at[0])
    docs_copy = pltpu.make_async_copy(docs_h, docs_v, local_sem.at[1])
    k_copy = pltpu.make_async_copy(k_h, k_in, local_sem.at[2])
    row_copy = pltpu.make_async_copy(layout_row_h, layout_v, local_sem.at[3])
    v_copy = pltpu.make_async_copy(v_h, vall.at[mine], local_sem.at[4])
    q_copy = pltpu.make_async_copy(q_h, q_in, local_sem.at[5])
    g_copy = pltpu.make_async_copy(g_h, g_in, local_sem.at[6])
    for copy in (layout_copy, docs_copy, k_copy, v_copy, row_copy, q_copy, g_copy):
        copy.start()

    half = hd // 2
    lane = lax.broadcasted_iota(jnp.int32, (1, hd), 1)
    freq = jnp.exp(-(2.0 * lax.rem(lane, half).astype(F32) / hd) * math.log(THETA))
    row_at = lax.broadcasted_iota(jnp.int32, (rows, hd), 0)
    layout_copy.wait()
    first = layout_s[me * rows].astype(F32)
    second = layout_s[me * rows + RUN].astype(F32)
    token = jnp.where(row_at < RUN, row_at.astype(F32) + first, (row_at - RUN).astype(F32) + second)
    token = token[:, :1]
    docs_copy.wait()
    docs = jnp.broadcast_to(docs_v[...], (8, seq))
    lane_at = lax.broadcasted_iota(jnp.int32, (8, seq), 1)
    starts = jnp.where(docs != pltpu.roll(docs, 1, 1), lane_at, 0).astype(F32)[:1]
    start = jnp.max(jnp.where(starts <= token, starts, 0.0), axis=1, keepdims=True)
    angles = (token - start) * freq
    cosine = jnp.cos(angles)
    sine = jnp.where(lane < half, -1.0, 1.0) * jnp.sin(angles)
    cos_ref[...] = cosine
    sin_ref[...] = sine
    k_copy.wait()
    kall[mine] = rotate(k_in[...].astype(F32), cosine, sine).astype(BF16)
    v_copy.wait()

    pl.semaphore_wait(barrier, n - 1)

    def transfer(kind, k, source, target):
        return pltpu.make_async_remote_copy(
            src_ref=source, dst_ref=target,
            send_sem=send_sem.at[kind, k], recv_sem=recv_sem.at[kind, k],
            device_id={"context": peer(k)}, device_id_type=MESH)

    def k_send(k):
        return transfer(0, k, kall.at[mine], kall.at[mine])

    def v_send(k):
        return transfer(1, k, vall.at[mine], vall.at[mine])

    def g_send(kind, k):
        return transfer(2 + kind, k, send_buf.at[kind, k], recv_buf.at[kind, k])

    loop(n - 1, lambda k: k_send(n - 2 - k).start())

    row_copy.wait()
    keys = layout_v[...].astype(F32)
    bias_t[...] = jnp.where((keys >= start) & (keys <= token), 0.0, MASKED).T.astype(BF16)
    q_copy.wait()

    def make_q(at):
        here = span(at, chunk)
        cosines, sines = spread(cos_ref, at, chunk, heads), spread(sin_ref, at, chunk, heads)
        qe[here, :hd] = rotate(q_in[here, :].astype(F32), cosines, sines).astype(BF16)
        row = lax.broadcasted_iota(jnp.int32, (chunk, hd), 0) // heads + at * tokens
        col = lax.broadcasted_iota(jnp.int32, (chunk, hd), 1)
        qe[here, hd:] = (row == col).astype(F32).astype(BF16)

    loop(steps, make_q)

    def make_probs(at):
        here = span(at, chunk)
        scores = dot(jnp.concatenate([kall[...], bias_t[...]], axis=1), qe[here, :], 1)
        largest = jnp.max(scores, axis=0, keepdims=True)
        weights = jnp.exp2((scores - largest) * factor)
        total = jnp.sum(weights, axis=0, keepdims=True)
        p_t[:, here] = (weights * (1.0 / total)).astype(BF16)

    loop(n - 1, lambda k: k_send(k).wait_recv())
    loop(n - 1, lambda k: v_send(k).start())
    loop(steps, make_probs)
    g_copy.wait()

    def v_grads(k):
        send_buf[0, k] = dot(p_t[span(peer(k), rows), :], g_in[...]).astype(BF16)
        g_send(0, k).start()

    loop(n - 1, lambda k: v_grads(n - 2 - k))
    loop(n - 1, lambda k: v_send(k).wait_recv())

    def make_ds(at):
        here = span(at, chunk)
        dprobs = dot(vall[...], g_in[here, :], 1)
        p = p_t[:, here].astype(F32)
        delta = jnp.sum(p * dprobs, axis=0, keepdims=True)
        probs[:, here] = (p * (dprobs - delta)).astype(BF16)

    loop(steps, make_ds)

    def k_grads(k):
        send_buf[1, k] = (dot(probs[span(peer(k), rows), :], qe[:, :hd]) * scale).astype(BF16)
        g_send(1, k).start()

    loop(n - 1, lambda k: k_grads(n - 2 - k))
    own_dk = dot(probs[mine, :], qe[:, :hd]) * scale
    own_dv[...] = dot(p_t[mine, :], g_in[...])
    k_t[...] = kall[...].astype(F32).T.astype(BF16)
    v_t[...] = vall[...].astype(F32).T.astype(BF16)

    def make_o(at):
        here = span(at, chunk)
        o_ref[here, :] = dot(v_t[...], p_t[:, here]).T.astype(BF16)

    def make_dq(at):
        here = span(at, chunk)
        grad = dot(k_t[...], probs[:, here]).T * scale
        cosines, sines = spread(cos_ref, at, chunk, heads), spread(sin_ref, at, chunk, heads)
        dq_ref[here, :] = rotate(grad, cosines, -sines).astype(BF16)

    loop(steps, make_o)
    loop(steps, make_dq)

    def collect(kind, own):
        loop(n - 1, lambda k: g_send(kind, k).wait_recv())
        return own + jnp.sum(recv_buf[kind].astype(F32), axis=0)

    dv_ref[...] = collect(0, own_dv[...])
    dk_ref[...] = rotate(collect(1, own_dk), cos_ref[...], -sin_ref[...])

    def finish(k):
        k_send(k).wait_send()
        v_send(k).wait_send()
        g_send(0, k).wait_send()
        g_send(1, k).wait_send()

    loop(n - 1, finish)


def last_kernel(*refs):
    count = len(refs) // 2
    sem = refs[-1]
    copies = [pltpu.make_async_copy(refs[at], refs[count + at], sem.at[at]) for at in range(count)]
    for copy in copies:
        copy.start()
    for copy in copies:
        copy.wait()


def sum_kernel(o_in, dq_in, grad_near, parts, cosine, sine, o_h, dq_h, dk_h, dv_h, dk, dv, sem):
    copies = [pltpu.make_async_copy(source, target, sem.at[at]) for at, (source, target) in enumerate(
        ((o_in, o_h), (dq_in, dq_h), (dv, dv_h), (dk, dk_h)))]
    copies[0].start()
    copies[1].start()

    def total(kind):
        return (grad_near[kind] + sum(parts[3 * kind + at].astype(F32) for at in range(3))).T

    dv[...] = total(0)
    copies[2].start()
    grad = total(1)
    dk[...] = grad * cosine[...] + pltpu.roll(grad, grad.shape[-1] // 2, 1) * sine[...]
    copies[3].start()
    for copy in copies:
        copy.wait()


def body(n, queries, key_heads, value_heads, out_grad, layout, documents):
    rows, heads, hd = queries.shape
    seq = layout.shape[0]
    flat = rows * heads
    hbm = pl.BlockSpec(memory_space=pltpu.HBM)
    vmem = pl.BlockSpec(memory_space=pltpu.VMEM)
    shapes = (
        jax.ShapeDtypeStruct((flat, hd), BF16),
        jax.ShapeDtypeStruct((flat, hd), BF16),
        jax.ShapeDtypeStruct((rows, hd), F32),
        jax.ShapeDtypeStruct((rows, hd), F32),
    )
    operands = [
        pltpu.SMEM((seq,), jnp.int32),
        pltpu.VMEM((1, seq), jnp.int32),
        pltpu.VMEM((1, seq), jnp.int32),
        pltpu.VMEM((flat, hd), BF16),
        pltpu.VMEM((flat, hd), BF16),
    ]
    if n == 4:
        kernel = functools.partial(pair_kernel, heads, 256)
        scratch = operands + [
            pltpu.VMEM((seq, hd), BF16),
            pltpu.VMEM((seq, hd), BF16),
            pltpu.VMEM((seq, 2 * hd), BF16),
            pltpu.VMEM((hd + rows, flat), BF16),
            pltpu.VMEM((hd, flat), BF16),
            pltpu.VMEM((seq, hd), F32),
            pltpu.VMEM((seq, hd), F32),
            pltpu.VMEM((2 * rows, flat), F32),
            pltpu.VMEM((2 * rows, flat), F32),
            pltpu.VMEM((2 * rows, flat), F32),
            pltpu.VMEM((2 * rows, flat), F32),
            pltpu.VMEM((seq, flat), BF16),
            pltpu.VMEM((seq, flat), BF16),
            pltpu.VMEM((16, flat), F32),
            pltpu.VMEM((hd, seq), BF16),
            pltpu.VMEM((hd, seq), BF16),
            pltpu.VMEM((6, hd, rows), BF16),
            pltpu.SemaphoreType.DMA((7,)),
            pltpu.SemaphoreType.DMA((12,)),
            pltpu.SemaphoreType.DMA((12,)),
        ]
    else:
        kernel = functools.partial(ring_kernel, n, heads, 128)
        scratch = operands + [
            pltpu.VMEM((rows, hd), BF16),
            pltpu.VMEM((seq, flat), BF16),
            pltpu.VMEM((hd, seq), BF16),
            pltpu.VMEM((rows, hd), F32),
            pltpu.VMEM((rows, hd), F32),
            pltpu.VMEM((flat, 2 * hd), BF16),
            pltpu.VMEM((seq, hd), BF16),
            pltpu.VMEM((seq, hd), BF16),
            pltpu.VMEM((hd, seq), BF16),
            pltpu.VMEM((seq, flat), BF16),
            pltpu.VMEM((seq, rows), BF16),
            pltpu.VMEM((2, n - 1, rows, hd), BF16),
            pltpu.VMEM((2, n - 1, rows, hd), BF16),
            pltpu.VMEM((rows, hd), F32),
            pltpu.SemaphoreType.DMA((7,)),
            pltpu.SemaphoreType.DMA((4, n - 1)),
            pltpu.SemaphoreType.DMA((4, n - 1)),
        ]
    if n == 4:
        carry = shapes[:2] + (
            jax.ShapeDtypeStruct((2, hd, rows), F32),
            jax.ShapeDtypeStruct((6, hd, rows), BF16),
            jax.ShapeDtypeStruct((rows, hd), F32),
            jax.ShapeDtypeStruct((rows, hd), F32),
        )
        last = sum_kernel
        last_scratch = [pltpu.VMEM((rows, hd), F32), pltpu.VMEM((rows, hd), F32)]
    else:
        carry, last, last_scratch = shapes, last_kernel, []
    carried = pl.pallas_call(
        kernel,
        out_shape=carry,
        in_specs=[hbm] * 7,
        out_specs=(vmem,) * len(carry),
        scratch_shapes=scratch,
        compiler_params=pltpu.CompilerParams(
            collective_id=0, has_side_effects=True, vmem_limit_bytes=(40 if n == 4 else 58) * 1024 * 1024),
    )(*[pltpu.with_memory_space_constraint(operand, pltpu.HBM) for operand in (
        layout, layout.reshape(1, seq), documents.reshape(1, seq),
        queries.reshape(flat, hd), key_heads.reshape(rows, hd), value_heads.reshape(rows, hd),
        out_grad.reshape(flat, hd),
    )])
    out, dq, dk, dv = pl.pallas_call(
        last,
        out_shape=shapes,
        in_specs=[vmem] * len(carry),
        out_specs=(hbm,) * 4,
        scratch_shapes=last_scratch + [pltpu.SemaphoreType.DMA((4,))],
        compiler_params=pltpu.CompilerParams(vmem_limit_bytes=8 * 1024 * 1024),
    )(*carried)
    return (out.reshape(rows, heads, hd), dq.reshape(rows, heads, hd), dk, dv)


def solution(mesh):
    return jax.shard_map(
        functools.partial(body, mesh.shape["context"]),
        mesh=mesh,
        in_specs=(
            P(("dp", "context"), "tensor", None),
            P(("dp", "context"), "tensor", None),
            P(("dp", "context"), "tensor", None),
            P(("dp", "context"), "tensor", None),
            P("dp"),
            P("dp"),
        ),
        out_specs=(
            P(("dp", "context"), "tensor", None),
            P(("dp", "context"), "tensor", None),
            P(("dp", "context"), "tensor"),
            P(("dp", "context"), "tensor"),
        ),
        check_vma=False,
    )
```

```python
import functools
import math

import jax
import jax.numpy as jnp
from jax import lax
from jax.experimental import pallas as pl
from jax.experimental.pallas import tpu as pltpu
from jax.sharding import PartitionSpec as P

THETA = 8000000.0
RUN = 64
MASKED = -1e30
MESH = pl.DeviceIdType.MESH
F32 = jnp.float32
BF16 = jnp.bfloat16


def dot(lhs, rhs, rhs_dim=0):
    return lax.dot_general(lhs, rhs, (((1,), (rhs_dim,)), ((), ())), preferred_element_type=F32)


def sine_cosine(x):
    turns = jnp.floor(x * (2.0 / math.pi) + 0.5)
    r = ((x - turns * 1.5703125) - turns * 4.837512969970703125e-4) - turns * 7.54978995489188216e-8
    z = r * r
    s = r + r * z * (-1.6666654611e-1 + z * (8.3321608736e-3 - z * 1.9515295891e-4))
    c = 1.0 - 0.5 * z + z * z * (4.166664568298827e-2 + z * (-1.388731625493765e-3 + z * 2.443315711809948e-5))
    quarter = turns.astype(jnp.int32)
    odd = (quarter & 1) == 1
    sine = jnp.where(odd, c, s)
    cosine = jnp.where(odd, s, c)
    return (jnp.where((quarter & 2) == 2, -sine, sine), jnp.where(((quarter + 1) & 2) == 2, -cosine, cosine))


def per_token(ref, first, tokens, heads):
    return jnp.concatenate([
        jnp.broadcast_to(ref[first + t:first + t + 1, :], (heads, ref.shape[-1])) for t in range(tokens)], axis=0)


def pair_kernel(heads, chunk, layout_h, layout_row_h, docs_h, q_h, k_h, v_h, g_h,
                o_ref, dq_ref, grad_near, recv_buf, cos_mine, sin_mine,
                layout_s, layout_v, docs_v, q_in, g_in, kraw, vall, kb, q_t, g_t, cos_ref, sin_ref,
                w_near, w_far, dp_near, dp_far, p_t, ds_t, stats, k_t, v_t,
                send_buf,
                local_sem, send_sem, recv_sem):
    n = 4
    me = lax.axis_index("context")
    rows, hd = cos_mine.shape
    seq = n * rows
    half = hd // 2
    tokens = chunk // heads
    steps = rows // tokens
    scale = 1.0 / math.sqrt(hd)
    factor = scale * math.log2(math.e)
    chip, core = me // 2, lax.rem(me, 2)
    partner = chip * 2 + (1 - core)
    far0 = (1 - chip) * 2
    owners = (me, partner, far0, far0 + 1)

    def block(role, count=1):
        return slice(role * rows, (role + count) * rows)

    def part(at):
        return slice(at * chunk, (at + 1) * chunk)

    near, far = block(0, 2), block(2, 2)

    barrier = pltpu.get_barrier_semaphore()
    for peer in (far0, far0 + 1, partner):
        pl.semaphore_signal(barrier, inc=1, device_id={"context": peer}, device_id_type=MESH)

    k_copy = pltpu.make_async_copy(k_h, kraw.at[block(0)], local_sem.at[2])
    v_copy = pltpu.make_async_copy(v_h, vall.at[block(0)], local_sem.at[4])
    layout_copy = pltpu.make_async_copy(layout_h, layout_s, local_sem.at[0])
    docs_copy = pltpu.make_async_copy(docs_h, docs_v, local_sem.at[1])
    row_copy = pltpu.make_async_copy(layout_row_h, layout_v, local_sem.at[3])
    q_copy = pltpu.make_async_copy(q_h, q_in, local_sem.at[5])
    g_copy = pltpu.make_async_copy(g_h, g_in, local_sem.at[6])
    for copy in (k_copy, v_copy, layout_copy, docs_copy, row_copy, q_copy, g_copy):
        copy.start()

    def transfer(at, source, target, to):
        return pltpu.make_async_remote_copy(
            src_ref=source, dst_ref=target, send_sem=send_sem.at[at], recv_sem=recv_sem.at[at],
            device_id={"context": to}, device_id_type=MESH)

    def slot(ref, at):
        return ref.at[pl.ds(pl.multiple_of((2 + at) * rows, rows), rows)]

    def to_far(kind, to, source, target):
        return pltpu.make_async_remote_copy(
            src_ref=source, dst_ref=target, send_sem=send_sem.at[2 * kind + to], recv_sem=recv_sem.at[2 * kind + core],
            device_id={"context": far0 + to}, device_id_type=MESH)

    def from_far(kind, at, target):
        return pltpu.make_async_remote_copy(
            src_ref=target, dst_ref=target, send_sem=send_sem.at[2 * kind], recv_sem=recv_sem.at[2 * kind + at],
            device_id={"context": far0}, device_id_type=MESH)

    k_far = [to_far(0, to, kraw.at[block(0)], slot(kraw, core)) for to in (0, 1)]
    v_far = [to_far(1, to, vall.at[block(0)], slot(vall, core)) for to in (0, 1)]
    dv_far = [to_far(2, to, send_buf.at[1 + to], recv_buf.at[1 + core]) for to in (0, 1)]
    dk_far = [to_far(3, to, send_buf.at[4 + to], recv_buf.at[4 + core]) for to in (0, 1)]
    k_near = transfer(8, kraw.at[block(0)], kraw.at[block(1)], partner)
    v_near = transfer(9, vall.at[block(0)], vall.at[block(1)], partner)
    dv_near = transfer(10, send_buf.at[0], recv_buf.at[0], partner)
    dk_near = transfer(11, send_buf.at[3], recv_buf.at[3], partner)

    for at in range(steps):
        row = lax.broadcasted_iota(jnp.int32, (rows, chunk), 0)
        col = lax.broadcasted_iota(jnp.int32, (rows, chunk), 1) // heads + at * tokens
        q_t[hd:, part(at)] = jnp.where(row == col, 1.0, 0.0).astype(BF16)

    k_copy.wait()
    v_copy.wait()
    pl.semaphore_wait(barrier, n - 1)
    for copy in (k_far[0], k_near, k_far[1], v_near, v_far[0], v_far[1]):
        copy.start()

    lane = lax.broadcasted_iota(jnp.int32, (1, hd), 1)
    low = lane < half
    freq = jnp.exp(-(2.0 * lax.rem(lane, half).astype(F32) / hd) * math.log(THETA))
    within = lax.broadcasted_iota(jnp.int32, (RUN, 1), 0).astype(F32)
    docs_copy.wait()
    docs = jnp.broadcast_to(docs_v[...], (8, seq))
    lane_at = lax.broadcasted_iota(jnp.int32, (8, seq), 1)
    starts = jnp.where(docs != pltpu.roll(docs, 1, 1), lane_at, 0).astype(F32)[:1]
    layout_copy.wait()

    def places(owner):
        found = []
        for run in range(rows // RUN):
            token = within + layout_s[owner * rows + run * RUN].astype(F32)
            start = jnp.max(jnp.where(starts <= token, starts, 0.0), axis=1, keepdims=True)
            found.append((token, start))
        return found

    def tables(found):
        (token_a, start_a), (token_b, start_b) = found
        sine, cosine = sine_cosine(jnp.where(low, token_a - start_a, token_b - start_b) * freq)
        sine_r, cosine_r = pltpu.roll(sine, half, 1), pltpu.roll(cosine, half, 1)
        c = jnp.concatenate([jnp.where(low, cosine, cosine_r), jnp.where(low, cosine_r, cosine)], axis=0)
        s = jnp.concatenate([jnp.where(low, -sine, sine_r), jnp.where(low, -sine_r, sine)], axis=0)
        return c, s

    def rotate(x, c, s):
        return x * c + pltpu.roll(x, half, 1) * s

    def rotate_keys(role, c, s):
        kb[block(role), :hd] = rotate(kraw[block(role), :].astype(F32), c, s).astype(BF16)

    found = places(me)
    c, s = tables(found)
    cos_mine[...] = c
    sin_mine[...] = s
    rotate_keys(0, c, s)
    token = jnp.concatenate([t for t, _ in found], axis=0)
    start = jnp.concatenate([t for _, t in found], axis=0)
    row_copy.wait()
    for role in range(n):
        keys = layout_v[:, pl.ds(pl.multiple_of(owners[role] * rows, rows), rows)].astype(F32)
        kb[block(role), hd:] = jnp.where((keys >= start) & (keys <= token), 0.0, MASKED).T.astype(BF16)
    q_copy.wait()
    for at in range(steps):
        cosines = per_token(cos_mine, at * tokens, tokens, heads)
        sines = per_token(sin_mine, at * tokens, tokens, heads)
        rotated = rotate(q_in[part(at), :].astype(F32), cosines, sines)
        q_t[:hd, part(at)] = rotated.T.astype(BF16)
    g_copy.wait()
    for at in range(steps):
        g_t[:, part(at)] = g_in[part(at), :].astype(F32).T.astype(BF16)
    for role in (1, 2, 3):
        c, s = tables(places(owners[role]))
        cos_ref[block(role), :] = c
        sin_ref[block(role), :] = s

    def score(role, count, w_ref, at, chunk_at):
        here = part(chunk_at)
        scores = dot(kb[block(role, count), :], q_t[:, here])
        largest = jnp.max(scores, axis=0, keepdims=True)
        weights = jnp.exp2((scores - largest) * factor)
        w_ref[:, here] = weights
        stats[3 * at:3 * at + 1, here] = largest
        stats[3 * at + 1:3 * at + 2, here] = jnp.sum(weights, axis=0, keepdims=True)

    def back(role, count, w_ref, dp_ref, at, chunk_at):
        here = part(chunk_at)
        dprobs = dot(vall[block(role, count), :], g_t[:, here])
        dp_ref[:, here] = dprobs
        stats[3 * at + 2:3 * at + 3, here] = jnp.sum(w_ref[:, here] * dprobs, axis=0, keepdims=True)

    def arrived(role):
        rotate_keys(role, cos_ref[block(role), :], sin_ref[block(role), :])

    k_near.wait_recv()
    arrived(1)
    v_near.wait_recv()
    for at in range(steps):
        score(0, 2, w_near, 0, at)
        back(0, 2, w_near, dp_near, 0, at)

    def far_keys(at):
        from_far(0, at, slot(kraw, at)).wait_recv()
        arrived(2 + at)

    def far_score(at, chunk_at):
        here = part(chunk_at)
        scores = dot(kb[block(2 + at), :], q_t[:, here])
        largest = jnp.max(scores, axis=0, keepdims=True)
        weights = jnp.exp2((scores - largest) * factor)
        w_far[block(at), here] = weights
        stats[3 + 3 * at:4 + 3 * at, here] = largest
        stats[4 + 3 * at:5 + 3 * at, here] = jnp.sum(weights, axis=0, keepdims=True)

    def normalize(at, here):
        p = w_far[block(at), here] * stats[12 + at:13 + at, here]
        w_far[block(at), here] = p
        p_t[block(2 + at), here] = p.astype(BF16)

    far_keys(1)
    for at in range(steps):
        far_score(1, at)
    far_keys(0)
    for at in range(steps):
        here = part(at)
        far_score(0, at)
        maxima = [stats[b:b + 1, here] for b in (0, 3, 6)]
        largest = jnp.maximum(jnp.maximum(maxima[0], maxima[1]), maxima[2])
        shrink = [jnp.exp2((m - largest) * factor) for m in maxima]
        inverse = 1.0 / sum(shrink[b] * stats[3 * b + 1:3 * b + 2, here] for b in range(3))
        weight = shrink[0] * inverse
        stats[9:10, here] = weight
        stats[10:11, here] = weight * stats[2:3, here]
        stats[12:13, here] = shrink[1] * inverse
        stats[13:14, here] = shrink[2] * inverse
        normalize(1, here)
    send_buf[2] = dot(g_t[...], p_t[block(3), :], 1).astype(BF16)
    dv_far[1].start()
    for at in range(steps):
        normalize(0, part(at))
    send_buf[1] = dot(g_t[...], p_t[block(2), :], 1).astype(BF16)
    dv_far[0].start()

    for at in (0, 1):
        from_far(1, at, slot(vall, at)).wait_recv()
    for at in range(steps):
        here = part(at)
        back(2, 2, w_far, dp_far, 1, at)
        stats[11:12, here] = stats[10:11, here] + stats[5:6, here]
        ds_t[block(2), here] = (w_far[:rows, here] * (dp_far[:rows, here] - stats[11:12, here])).astype(BF16)
    send_buf[4] = dot(q_t[:hd, :], ds_t[block(2), :], 1).astype(BF16)
    dk_far[0].start()
    for at in range(steps):
        here = part(at)
        ds_t[block(3), here] = (w_far[rows:, here] * (dp_far[rows:, here] - stats[11:12, here])).astype(BF16)
    send_buf[5] = dot(q_t[:hd, :], ds_t[block(3), :], 1).astype(BF16)
    dk_far[1].start()
    for at in range(steps):
        here = part(at)
        p = w_near[:, here] * stats[9:10, here]
        p_t[near, here] = p.astype(BF16)
        ds_t[near, here] = (p * (dp_near[:, here] - stats[11:12, here])).astype(BF16)
    for kind, left, right in ((0, g_t, p_t), (1, q_t.at[:hd], ds_t)):
        grad = dot(left[...], right[near, :], 1)
        send_buf[3 * kind] = grad[:, rows:].astype(BF16)
        (dv_near, dk_near)[kind].start()
        grad_near[kind] = grad[:, :rows]

    k_t[...] = kb[:, :hd].astype(F32).T.astype(BF16)
    v_t[...] = vall[...].astype(F32).T.astype(BF16)
    for at in range(steps):
        o_ref[part(at), :] = dot(v_t[...], p_t[:, part(at)]).T.astype(BF16)
    cos_mine[...] = cos_mine[...] * scale
    sin_mine[...] = sin_mine[...] * -scale
    for at in range(steps):
        cosines = per_token(cos_mine, at * tokens, tokens, heads)
        sines = per_token(sin_mine, at * tokens, tokens, heads)
        dq_ref[part(at), :] = rotate(dot(k_t[...], ds_t[:, part(at)]).T, cosines, sines).astype(BF16)

    dv_near.wait_recv()
    dk_near.wait_recv()
    for kind in (2, 3):
        for at in (0, 1):
            from_far(kind, at, recv_buf.at[3 * (kind - 2) + 1 + at]).wait_recv()
    for copy in (k_near, v_near, dv_near, dk_near, *k_far, *v_far, *dv_far, *dk_far):
        copy.wait_send()


def loop(count, step):
    if count <= 8:
        for index in range(count):
            step(index)
    else:
        lax.fori_loop(0, count, lambda index, _: (step(index), None)[1], None)


def span(at, size):
    start = at * size
    return pl.ds(start if isinstance(at, int) else pl.multiple_of(start, size), size)


def rotate(x, cosine, sine):
    return x * cosine + pltpu.roll(x, x.shape[-1] // 2, 1) * sine


def spread(ref, at, chunk, heads):
    part = ref[span(at, chunk // heads), :]
    return jnp.broadcast_to(part[:, None, :], (chunk // heads, heads, part.shape[-1])).reshape(chunk, -1)


def ring_kernel(n, heads, chunk, layout_h, layout_row_h, docs_h, q_h, k_h, v_h, g_h,
                o_ref, dq_ref, dk_ref, dv_ref,
                layout_s, layout_v, docs_v, q_in, g_in, k_in, probs, k_t, cos_ref, sin_ref, qe, kall, vall, v_t, p_t, bias_t,
                send_buf, recv_buf, own_dv, local_sem, send_sem, recv_sem):
    me = lax.axis_index("context")
    rows, hd = k_in.shape
    seq = rows * n
    flat = rows * heads
    tokens = chunk // heads
    steps = flat // chunk
    scale = 1.0 / math.sqrt(hd)

    factor = scale * math.log2(math.e)

    def peer(k):
        pair = lax.rem(me // 2 + (k + 1) // 2, n // 2)
        return pair * 2 + lax.rem(me + k + 1, 2)

    barrier = pltpu.get_barrier_semaphore()
    for k in range(n - 1):
        pl.semaphore_signal(barrier, inc=1, device_id={"context": peer(k)}, device_id_type=MESH)

    mine = span(me, rows)
    layout_copy = pltpu.make_async_copy(layout_h, layout_s, local_sem.at[0])
    docs_copy = pltpu.make_async_copy(docs_h, docs_v, local_sem.at[1])
    k_copy = pltpu.make_async_copy(k_h, k_in, local_sem.at[2])
    row_copy = pltpu.make_async_copy(layout_row_h, layout_v, local_sem.at[3])
    v_copy = pltpu.make_async_copy(v_h, vall.at[mine], local_sem.at[4])
    q_copy = pltpu.make_async_copy(q_h, q_in, local_sem.at[5])
    g_copy = pltpu.make_async_copy(g_h, g_in, local_sem.at[6])
    for copy in (layout_copy, docs_copy, k_copy, v_copy, row_copy, q_copy, g_copy):
        copy.start()

    half = hd // 2
    lane = lax.broadcasted_iota(jnp.int32, (1, hd), 1)
    freq = jnp.exp(-(2.0 * lax.rem(lane, half).astype(F32) / hd) * math.log(THETA))
    row_at = lax.broadcasted_iota(jnp.int32, (rows, hd), 0)
    layout_copy.wait()
    first = layout_s[me * rows].astype(F32)
    second = layout_s[me * rows + RUN].astype(F32)
    token = jnp.where(row_at < RUN, row_at.astype(F32) + first, (row_at - RUN).astype(F32) + second)
    token = token[:, :1]
    docs_copy.wait()
    docs = jnp.broadcast_to(docs_v[...], (8, seq))
    lane_at = lax.broadcasted_iota(jnp.int32, (8, seq), 1)
    starts = jnp.where(docs != pltpu.roll(docs, 1, 1), lane_at, 0).astype(F32)[:1]
    start = jnp.max(jnp.where(starts <= token, starts, 0.0), axis=1, keepdims=True)
    angles = (token - start) * freq
    cosine = jnp.cos(angles)
    sine = jnp.where(lane < half, -1.0, 1.0) * jnp.sin(angles)
    cos_ref[...] = cosine
    sin_ref[...] = sine
    k_copy.wait()
    kall[mine] = rotate(k_in[...].astype(F32), cosine, sine).astype(BF16)
    v_copy.wait()

    pl.semaphore_wait(barrier, n - 1)

    def transfer(kind, k, source, target):
        return pltpu.make_async_remote_copy(
            src_ref=source, dst_ref=target,
            send_sem=send_sem.at[kind, k], recv_sem=recv_sem.at[kind, k],
            device_id={"context": peer(k)}, device_id_type=MESH)

    def k_send(k):
        return transfer(0, k, kall.at[mine], kall.at[mine])

    def v_send(k):
        return transfer(1, k, vall.at[mine], vall.at[mine])

    def g_send(kind, k):
        return transfer(2 + kind, k, send_buf.at[kind, k], recv_buf.at[kind, k])

    loop(n - 1, lambda k: k_send(n - 2 - k).start())

    row_copy.wait()
    keys = layout_v[...].astype(F32)
    bias_t[...] = jnp.where((keys >= start) & (keys <= token), 0.0, MASKED).T.astype(BF16)
    q_copy.wait()

    def make_q(at):
        here = span(at, chunk)
        cosines, sines = spread(cos_ref, at, chunk, heads), spread(sin_ref, at, chunk, heads)
        qe[here, :hd] = rotate(q_in[here, :].astype(F32), cosines, sines).astype(BF16)
        row = lax.broadcasted_iota(jnp.int32, (chunk, hd), 0) // heads + at * tokens
        col = lax.broadcasted_iota(jnp.int32, (chunk, hd), 1)
        qe[here, hd:] = (row == col).astype(F32).astype(BF16)

    loop(steps, make_q)

    def make_probs(at):
        here = span(at, chunk)
        scores = dot(jnp.concatenate([kall[...], bias_t[...]], axis=1), qe[here, :], 1)
        largest = jnp.max(scores, axis=0, keepdims=True)
        weights = jnp.exp2((scores - largest) * factor)
        total = jnp.sum(weights, axis=0, keepdims=True)
        p_t[:, here] = (weights * (1.0 / total)).astype(BF16)

    loop(n - 1, lambda k: k_send(k).wait_recv())
    loop(n - 1, lambda k: v_send(k).start())
    loop(steps, make_probs)
    g_copy.wait()

    def v_grads(k):
        send_buf[0, k] = dot(p_t[span(peer(k), rows), :], g_in[...]).astype(BF16)
        g_send(0, k).start()

    loop(n - 1, lambda k: v_grads(n - 2 - k))
    loop(n - 1, lambda k: v_send(k).wait_recv())

    def make_ds(at):
        here = span(at, chunk)
        dprobs = dot(vall[...], g_in[here, :], 1)
        p = p_t[:, here].astype(F32)
        delta = jnp.sum(p * dprobs, axis=0, keepdims=True)
        probs[:, here] = (p * (dprobs - delta)).astype(BF16)

    loop(steps, make_ds)

    def k_grads(k):
        send_buf[1, k] = (dot(probs[span(peer(k), rows), :], qe[:, :hd]) * scale).astype(BF16)
        g_send(1, k).start()

    loop(n - 1, lambda k: k_grads(n - 2 - k))
    own_dk = dot(probs[mine, :], qe[:, :hd]) * scale
    own_dv[...] = dot(p_t[mine, :], g_in[...])
    k_t[...] = kall[...].astype(F32).T.astype(BF16)
    v_t[...] = vall[...].astype(F32).T.astype(BF16)

    def make_o(at):
        here = span(at, chunk)
        o_ref[here, :] = dot(v_t[...], p_t[:, here]).T.astype(BF16)

    def make_dq(at):
        here = span(at, chunk)
        grad = dot(k_t[...], probs[:, here]).T * scale
        cosines, sines = spread(cos_ref, at, chunk, heads), spread(sin_ref, at, chunk, heads)
        dq_ref[here, :] = rotate(grad, cosines, -sines).astype(BF16)

    loop(steps, make_o)
    loop(steps, make_dq)

    def collect(kind, own):
        loop(n - 1, lambda k: g_send(kind, k).wait_recv())
        return own + jnp.sum(recv_buf[kind].astype(F32), axis=0)

    dv_ref[...] = collect(0, own_dv[...])
    dk_ref[...] = rotate(collect(1, own_dk), cos_ref[...], -sin_ref[...])

    def finish(k):
        k_send(k).wait_send()
        v_send(k).wait_send()
        g_send(0, k).wait_send()
        g_send(1, k).wait_send()

    loop(n - 1, finish)


def last_kernel(*refs):
    count = len(refs) // 2
    sem = refs[-1]
    copies = [pltpu.make_async_copy(refs[at], refs[count + at], sem.at[at]) for at in range(count)]
    for copy in copies:
        copy.start()
    for copy in copies:
        copy.wait()


def sum_kernel(o_in, dq_in, grad_near, parts, cosine, sine, o_h, dq_h, dk_h, dv_h, dk, dv, sem):
    copies = [pltpu.make_async_copy(source, target, sem.at[at]) for at, (source, target) in enumerate(
        ((o_in, o_h), (dq_in, dq_h), (dv, dv_h), (dk, dk_h)))]
    copies[0].start()
    copies[1].start()

    def total(kind):
        return (grad_near[kind] + sum(parts[3 * kind + at].astype(F32) for at in range(3))).T

    dv[...] = total(0)
    copies[2].start()
    grad = total(1)
    dk[...] = grad * cosine[...] + pltpu.roll(grad, grad.shape[-1] // 2, 1) * sine[...]
    copies[3].start()
    for copy in copies:
        copy.wait()


def body(n, queries, key_heads, value_heads, out_grad, layout, documents):
    rows, heads, hd = queries.shape
    seq = layout.shape[0]
    flat = rows * heads
    hbm = pl.BlockSpec(memory_space=pltpu.HBM)
    vmem = pl.BlockSpec(memory_space=pltpu.VMEM)
    shapes = (
        jax.ShapeDtypeStruct((flat, hd), BF16),
        jax.ShapeDtypeStruct((flat, hd), BF16),
        jax.ShapeDtypeStruct((rows, hd), F32),
        jax.ShapeDtypeStruct((rows, hd), F32),
    )
    operands = [
        pltpu.SMEM((seq,), jnp.int32),
        pltpu.VMEM((1, seq), jnp.int32),
        pltpu.VMEM((1, seq), jnp.int32),
        pltpu.VMEM((flat, hd), BF16),
        pltpu.VMEM((flat, hd), BF16),
    ]
    if n == 4:
        kernel = functools.partial(pair_kernel, heads, 256)
        scratch = operands + [
            pltpu.VMEM((seq, hd), BF16),
            pltpu.VMEM((seq, hd), BF16),
            pltpu.VMEM((seq, 2 * hd), BF16),
            pltpu.VMEM((hd + rows, flat), BF16),
            pltpu.VMEM((hd, flat), BF16),
            pltpu.VMEM((seq, hd), F32),
            pltpu.VMEM((seq, hd), F32),
            pltpu.VMEM((2 * rows, flat), F32),
            pltpu.VMEM((2 * rows, flat), F32),
            pltpu.VMEM((2 * rows, flat), F32),
            pltpu.VMEM((2 * rows, flat), F32),
            pltpu.VMEM((seq, flat), BF16),
            pltpu.VMEM((seq, flat), BF16),
            pltpu.VMEM((16, flat), F32),
            pltpu.VMEM((hd, seq), BF16),
            pltpu.VMEM((hd, seq), BF16),
            pltpu.VMEM((6, hd, rows), BF16),
            pltpu.SemaphoreType.DMA((7,)),
            pltpu.SemaphoreType.DMA((12,)),
            pltpu.SemaphoreType.DMA((12,)),
        ]
    else:
        kernel = functools.partial(ring_kernel, n, heads, 128)
        scratch = operands + [
            pltpu.VMEM((rows, hd), BF16),
            pltpu.VMEM((seq, flat), BF16),
            pltpu.VMEM((hd, seq), BF16),
            pltpu.VMEM((rows, hd), F32),
            pltpu.VMEM((rows, hd), F32),
            pltpu.VMEM((flat, 2 * hd), BF16),
            pltpu.VMEM((seq, hd), BF16),
            pltpu.VMEM((seq, hd), BF16),
            pltpu.VMEM((hd, seq), BF16),
            pltpu.VMEM((seq, flat), BF16),
            pltpu.VMEM((seq, rows), BF16),
            pltpu.VMEM((2, n - 1, rows, hd), BF16),
            pltpu.VMEM((2, n - 1, rows, hd), BF16),
            pltpu.VMEM((rows, hd), F32),
            pltpu.SemaphoreType.DMA((7,)),
            pltpu.SemaphoreType.DMA((4, n - 1)),
            pltpu.SemaphoreType.DMA((4, n - 1)),
        ]
    if n == 4:
        carry = shapes[:2] + (
            jax.ShapeDtypeStruct((2, hd, rows), F32),
            jax.ShapeDtypeStruct((6, hd, rows), BF16),
            jax.ShapeDtypeStruct((rows, hd), F32),
            jax.ShapeDtypeStruct((rows, hd), F32),
        )
        last = sum_kernel
        last_scratch = [pltpu.VMEM((rows, hd), F32), pltpu.VMEM((rows, hd), F32)]
    else:
        carry, last, last_scratch = shapes, last_kernel, []
    carried = pl.pallas_call(
        kernel,
        out_shape=carry,
        in_specs=[hbm] * 7,
        out_specs=(vmem,) * len(carry),
        scratch_shapes=scratch,
        compiler_params=pltpu.CompilerParams(
            collective_id=0, has_side_effects=True, vmem_limit_bytes=(40 if n == 4 else 58) * 1024 * 1024),
    )(*[pltpu.with_memory_space_constraint(operand, pltpu.HBM) for operand in (
        layout, layout.reshape(1, seq), documents.reshape(1, seq),
        queries.reshape(flat, hd), key_heads.reshape(rows, hd), value_heads.reshape(rows, hd),
        out_grad.reshape(flat, hd),
    )])
    out, dq, dk, dv = pl.pallas_call(
        last,
        out_shape=shapes,
        in_specs=[vmem] * len(carry),
        out_specs=(hbm,) * 4,
        scratch_shapes=last_scratch + [pltpu.SemaphoreType.DMA((4,))],
        compiler_params=pltpu.CompilerParams(vmem_limit_bytes=8 * 1024 * 1024),
    )(*carried)
    return (out.reshape(rows, heads, hd), dq.reshape(rows, heads, hd), dk, dv)


def solution(mesh):
    return jax.shard_map(
        functools.partial(body, mesh.shape["context"]),
        mesh=mesh,
        in_specs=(
            P(("dp", "context"), "tensor", None),
            P(("dp", "context"), "tensor", None),
            P(("dp", "context"), "tensor", None),
            P(("dp", "context"), "tensor", None),
            P("dp"),
            P("dp"),
        ),
        out_specs=(
            P(("dp", "context"), "tensor", None),
            P(("dp", "context"), "tensor", None),
            P(("dp", "context"), "tensor"),
            P(("dp", "context"), "tensor"),
        ),
        check_vma=False,
    )
```

```python
import functools
import math

import jax
import jax.numpy as jnp
from jax import lax
from jax.experimental import pallas as pl
from jax.experimental.pallas import tpu as pltpu
from jax.sharding import PartitionSpec as P

THETA = 8000000.0
RUN = 64
MASKED = -1e30
MESH = pl.DeviceIdType.MESH
F32 = jnp.float32
BF16 = jnp.bfloat16


def dot(lhs, rhs, rhs_dim=0):
    return lax.dot_general(lhs, rhs, (((1,), (rhs_dim,)), ((), ())), preferred_element_type=F32)


def sine_cosine(x):
    turns = jnp.floor(x * (2.0 / math.pi) + 0.5)
    r = ((x - turns * 1.5703125) - turns * 4.837512969970703125e-4) - turns * 7.54978995489188216e-8
    z = r * r
    s = r + r * z * (-1.6666654611e-1 + z * (8.3321608736e-3 - z * 1.9515295891e-4))
    c = 1.0 - 0.5 * z + z * z * (4.166664568298827e-2 + z * (-1.388731625493765e-3 + z * 2.443315711809948e-5))
    quarter = turns.astype(jnp.int32)
    odd = (quarter & 1) == 1
    sine = jnp.where(odd, c, s)
    cosine = jnp.where(odd, s, c)
    return (jnp.where((quarter & 2) == 2, -sine, sine), jnp.where(((quarter + 1) & 2) == 2, -cosine, cosine))


def per_token(ref, first, tokens, heads):
    return jnp.concatenate([
        jnp.broadcast_to(ref[first + t:first + t + 1, :], (heads, ref.shape[-1])) for t in range(tokens)], axis=0)


def pair_kernel(heads, chunk, layout_h, layout_row_h, docs_h, q_h, k_h, v_h, g_h,
                o_ref, dq_ref, grad_near, recv_buf, cos_mine, sin_mine,
                layout_s, layout_v, docs_v, q_in, g_in, kraw, vall, kb, q_t, g_t, cos_ref, sin_ref,
                w_near, w_far, dp_near, dp_far, p_t, ds_t, stats, k_t, v_t,
                send_buf,
                local_sem, send_sem, recv_sem):
    n = 4
    me = lax.axis_index("context")
    rows, hd = cos_mine.shape
    seq = n * rows
    half = hd // 2
    tokens = chunk // heads
    steps = rows // tokens
    scale = 1.0 / math.sqrt(hd)
    factor = scale * math.log2(math.e)
    chip, core = me // 2, lax.rem(me, 2)
    partner = chip * 2 + (1 - core)
    far0 = (1 - chip) * 2
    owners = (me, partner, far0, far0 + 1)

    def block(role, count=1):
        return slice(role * rows, (role + count) * rows)

    def part(at):
        return slice(at * chunk, (at + 1) * chunk)

    near, far = block(0, 2), block(2, 2)

    barrier = pltpu.get_barrier_semaphore()
    for peer in (far0, far0 + 1, partner):
        pl.semaphore_signal(barrier, inc=1, device_id={"context": peer}, device_id_type=MESH)

    k_copy = pltpu.make_async_copy(k_h, kraw.at[block(0)], local_sem.at[2])
    v_copy = pltpu.make_async_copy(v_h, vall.at[block(0)], local_sem.at[4])
    layout_copy = pltpu.make_async_copy(layout_h, layout_s, local_sem.at[0])
    docs_copy = pltpu.make_async_copy(docs_h, docs_v, local_sem.at[1])
    row_copy = pltpu.make_async_copy(layout_row_h, layout_v, local_sem.at[3])
    q_copy = pltpu.make_async_copy(q_h, q_in, local_sem.at[5])
    g_copy = pltpu.make_async_copy(g_h, g_in, local_sem.at[6])
    for copy in (k_copy, v_copy, layout_copy, docs_copy, row_copy, q_copy, g_copy):
        copy.start()

    def transfer(at, source, target, to):
        return pltpu.make_async_remote_copy(
            src_ref=source, dst_ref=target, send_sem=send_sem.at[at], recv_sem=recv_sem.at[at],
            device_id={"context": to}, device_id_type=MESH)

    def slot(ref, at):
        return ref.at[pl.ds(pl.multiple_of((2 + at) * rows, rows), rows)]

    def to_far(kind, to, source, target):
        return pltpu.make_async_remote_copy(
            src_ref=source, dst_ref=target, send_sem=send_sem.at[2 * kind + to], recv_sem=recv_sem.at[2 * kind + core],
            device_id={"context": far0 + to}, device_id_type=MESH)

    def from_far(kind, at, target):
        return pltpu.make_async_remote_copy(
            src_ref=target, dst_ref=target, send_sem=send_sem.at[2 * kind], recv_sem=recv_sem.at[2 * kind + at],
            device_id={"context": far0}, device_id_type=MESH)

    k_far = [to_far(0, to, kraw.at[block(0)], slot(kraw, core)) for to in (0, 1)]
    v_far = [to_far(1, to, vall.at[block(0)], slot(vall, core)) for to in (0, 1)]
    dv_far = [to_far(2, to, send_buf.at[1 + to], recv_buf.at[1 + core]) for to in (0, 1)]
    dk_far = [to_far(3, to, send_buf.at[4 + to], recv_buf.at[4 + core]) for to in (0, 1)]
    k_near = transfer(8, kraw.at[block(0)], kraw.at[block(1)], partner)
    v_near = transfer(9, vall.at[block(0)], vall.at[block(1)], partner)
    dv_near = transfer(10, send_buf.at[0], recv_buf.at[0], partner)
    dk_near = transfer(11, send_buf.at[3], recv_buf.at[3], partner)

    for at in range(steps):
        row = lax.broadcasted_iota(jnp.int32, (rows, chunk), 0)
        col = lax.broadcasted_iota(jnp.int32, (rows, chunk), 1) // heads + at * tokens
        q_t[hd:, part(at)] = jnp.where(row == col, 1.0, 0.0).astype(BF16)

    k_copy.wait()
    v_copy.wait()
    pl.semaphore_wait(barrier, n - 1)
    for copy in (k_far[0], k_near, k_far[1], v_near, v_far[0], v_far[1]):
        copy.start()

    lane = lax.broadcasted_iota(jnp.int32, (1, hd), 1)
    low = lane < half
    freq = jnp.exp(-(2.0 * lax.rem(lane, half).astype(F32) / hd) * math.log(THETA))
    within = lax.broadcasted_iota(jnp.int32, (RUN, 1), 0).astype(F32)
    docs_copy.wait()
    docs = jnp.broadcast_to(docs_v[...], (8, seq))
    lane_at = lax.broadcasted_iota(jnp.int32, (8, seq), 1)
    starts = jnp.where(docs != pltpu.roll(docs, 1, 1), lane_at, 0).astype(F32)[:1]
    layout_copy.wait()

    def places(owner):
        found = []
        for run in range(rows // RUN):
            token = within + layout_s[owner * rows + run * RUN].astype(F32)
            start = jnp.max(jnp.where(starts <= token, starts, 0.0), axis=1, keepdims=True)
            found.append((token, start))
        return found

    def tables(found):
        (token_a, start_a), (token_b, start_b) = found
        sine, cosine = sine_cosine(jnp.where(low, token_a - start_a, token_b - start_b) * freq)
        sine_r, cosine_r = pltpu.roll(sine, half, 1), pltpu.roll(cosine, half, 1)
        c = jnp.concatenate([jnp.where(low, cosine, cosine_r), jnp.where(low, cosine_r, cosine)], axis=0)
        s = jnp.concatenate([jnp.where(low, -sine, sine_r), jnp.where(low, -sine_r, sine)], axis=0)
        return c, s

    def rotate(x, c, s):
        return x * c + pltpu.roll(x, half, 1) * s

    def rotate_keys(role, c, s):
        kb[block(role), :hd] = rotate(kraw[block(role), :].astype(F32), c, s).astype(BF16)

    found = places(me)
    c, s = tables(found)
    cos_mine[...] = c
    sin_mine[...] = s
    rotate_keys(0, c, s)
    token = jnp.concatenate([t for t, _ in found], axis=0)
    start = jnp.concatenate([t for _, t in found], axis=0)
    row_copy.wait()
    for role in range(n):
        keys = layout_v[:, pl.ds(pl.multiple_of(owners[role] * rows, rows), rows)].astype(F32)
        kb[block(role), hd:] = jnp.where((keys >= start) & (keys <= token), 0.0, MASKED).T.astype(BF16)
    q_copy.wait()
    for at in range(steps):
        cosines = per_token(cos_mine, at * tokens, tokens, heads)
        sines = per_token(sin_mine, at * tokens, tokens, heads)
        rotated = rotate(q_in[part(at), :].astype(F32), cosines, sines)
        q_t[:hd, part(at)] = rotated.T.astype(BF16)
    g_copy.wait()
    for at in range(steps):
        g_t[:, part(at)] = g_in[part(at), :].astype(F32).T.astype(BF16)
    for role in (1, 2, 3):
        c, s = tables(places(owners[role]))
        cos_ref[block(role), :] = c
        sin_ref[block(role), :] = s

    def score(role, count, w_ref, at, chunk_at):
        here = part(chunk_at)
        scores = dot(kb[block(role, count), :], q_t[:, here])
        largest = jnp.max(scores, axis=0, keepdims=True)
        weights = jnp.exp2((scores - largest) * factor)
        w_ref[:, here] = weights
        stats[3 * at:3 * at + 1, here] = largest
        stats[3 * at + 1:3 * at + 2, here] = jnp.sum(weights, axis=0, keepdims=True)

    def back(role, count, w_ref, dp_ref, at, chunk_at):
        here = part(chunk_at)
        dprobs = dot(vall[block(role, count), :], g_t[:, here])
        dp_ref[:, here] = dprobs
        stats[3 * at + 2:3 * at + 3, here] = jnp.sum(w_ref[:, here] * dprobs, axis=0, keepdims=True)

    def arrived(role):
        rotate_keys(role, cos_ref[block(role), :], sin_ref[block(role), :])

    k_near.wait_recv()
    arrived(1)
    v_near.wait_recv()
    for at in range(steps):
        score(0, 2, w_near, 0, at)
        back(0, 2, w_near, dp_near, 0, at)

    def far_keys(at):
        from_far(0, at, slot(kraw, at)).wait_recv()
        arrived(2 + at)

    def far_score(at, chunk_at):
        here = part(chunk_at)
        scores = dot(kb[block(2 + at), :], q_t[:, here])
        largest = jnp.max(scores, axis=0, keepdims=True)
        weights = jnp.exp2((scores - largest) * factor)
        w_far[block(at), here] = weights
        stats[3 + 3 * at:4 + 3 * at, here] = largest
        stats[4 + 3 * at:5 + 3 * at, here] = jnp.sum(weights, axis=0, keepdims=True)

    def normalize(at, here):
        p = w_far[block(at), here] * stats[12 + at:13 + at, here]
        w_far[block(at), here] = p
        p_t[block(2 + at), here] = p.astype(BF16)

    far_keys(1)
    for at in range(steps):
        far_score(1, at)
    for at in range(steps):
        here = part(at)
        largest = jnp.maximum(stats[0:1, here], stats[6:7, here])
        shrink = [jnp.exp2((stats[b:b + 1, here] - largest) * factor) for b in (0, 6)]
        stats[0:1, here] = largest
        stats[1:2, here] = shrink[0] * stats[1:2, here] + shrink[1] * stats[7:8, here]
        stats[9:10, here] = shrink[0]
        stats[13:14, here] = shrink[1]
    far_keys(0)
    for at in range(steps):
        here = part(at)
        scores = dot(kb[block(2), :], q_t[:, here])
        last = jnp.max(scores, axis=0, keepdims=True)
        weights = jnp.exp2((scores - last) * factor)
        largest = jnp.maximum(stats[0:1, here], last)
        before, after = jnp.exp2((stats[0:1, here] - largest) * factor), jnp.exp2((last - largest) * factor)
        inverse = 1.0 / (before * stats[1:2, here] + after * jnp.sum(weights, axis=0, keepdims=True))
        before = before * inverse
        weight = stats[9:10, here] * before
        stats[9:10, here] = weight
        stats[10:11, here] = weight * stats[2:3, here]
        stats[13:14, here] = stats[13:14, here] * before
        p = weights * (after * inverse)
        w_far[block(0), here] = p
        p_t[block(2), here] = p.astype(BF16)
    send_buf[1] = dot(g_t[...], p_t[block(2), :], 1).astype(BF16)
    dv_far[0].start()
    for at in range(steps):
        normalize(1, part(at))
    send_buf[2] = dot(g_t[...], p_t[block(3), :], 1).astype(BF16)
    dv_far[1].start()

    def far_back(at, here):
        dprobs = dot(vall[block(2 + at), :], g_t[:, here])
        dp_far[block(at), here] = dprobs
        return jnp.sum(w_far[block(at), here] * dprobs, axis=0, keepdims=True)

    from_far(1, 1, slot(vall, 1)).wait_recv()
    for at in range(steps):
        here = part(at)
        stats[10:11, here] = stats[10:11, here] + far_back(1, here)
    from_far(1, 0, slot(vall, 0)).wait_recv()
    for at in range(steps):
        here = part(at)
        stats[11:12, here] = stats[10:11, here] + far_back(0, here)
        ds_t[block(2), here] = (w_far[:rows, here] * (dp_far[:rows, here] - stats[11:12, here])).astype(BF16)
    send_buf[4] = dot(q_t[:hd, :], ds_t[block(2), :], 1).astype(BF16)
    dk_far[0].start()
    for at in range(steps):
        here = part(at)
        ds_t[block(3), here] = (w_far[rows:, here] * (dp_far[rows:, here] - stats[11:12, here])).astype(BF16)
    send_buf[5] = dot(q_t[:hd, :], ds_t[block(3), :], 1).astype(BF16)
    dk_far[1].start()
    for at in range(steps):
        here = part(at)
        p = w_near[:, here] * stats[9:10, here]
        p_t[near, here] = p.astype(BF16)
        ds_t[near, here] = (p * (dp_near[:, here] - stats[11:12, here])).astype(BF16)
    for kind, left, right in ((0, g_t, p_t), (1, q_t.at[:hd], ds_t)):
        grad = dot(left[...], right[near, :], 1)
        send_buf[3 * kind] = grad[:, rows:].astype(BF16)
        (dv_near, dk_near)[kind].start()
        grad_near[kind] = grad[:, :rows]

    k_t[...] = kb[:, :hd].astype(F32).T.astype(BF16)
    v_t[...] = vall[...].astype(F32).T.astype(BF16)
    for at in range(steps):
        o_ref[part(at), :] = dot(v_t[...], p_t[:, part(at)]).T.astype(BF16)
    cos_mine[...] = cos_mine[...] * scale
    sin_mine[...] = sin_mine[...] * -scale
    for at in range(steps):
        cosines = per_token(cos_mine, at * tokens, tokens, heads)
        sines = per_token(sin_mine, at * tokens, tokens, heads)
        dq_ref[part(at), :] = rotate(dot(k_t[...], ds_t[:, part(at)]).T, cosines, sines).astype(BF16)

    dv_near.wait_recv()
    dk_near.wait_recv()
    for kind in (2, 3):
        for at in (0, 1):
            from_far(kind, at, recv_buf.at[3 * (kind - 2) + 1 + at]).wait_recv()
    for copy in (k_near, v_near, dv_near, dk_near, *k_far, *v_far, *dv_far, *dk_far):
        copy.wait_send()


def loop(count, step):
    if count <= 8:
        for index in range(count):
            step(index)
    else:
        lax.fori_loop(0, count, lambda index, _: (step(index), None)[1], None)


def span(at, size):
    start = at * size
    return pl.ds(start if isinstance(at, int) else pl.multiple_of(start, size), size)


def rotate(x, cosine, sine):
    return x * cosine + pltpu.roll(x, x.shape[-1] // 2, 1) * sine


def spread(ref, at, chunk, heads):
    part = ref[span(at, chunk // heads), :]
    return jnp.broadcast_to(part[:, None, :], (chunk // heads, heads, part.shape[-1])).reshape(chunk, -1)


def ring_kernel(n, heads, chunk, layout_h, layout_row_h, docs_h, q_h, k_h, v_h, g_h,
                o_ref, dq_ref, dk_ref, dv_ref,
                layout_s, layout_v, docs_v, q_in, g_in, k_in, probs, k_t, cos_ref, sin_ref, qe, kall, vall, v_t, p_t, bias_t,
                send_buf, recv_buf, own_dv, local_sem, send_sem, recv_sem):
    me = lax.axis_index("context")
    rows, hd = k_in.shape
    seq = rows * n
    flat = rows * heads
    tokens = chunk // heads
    steps = flat // chunk
    scale = 1.0 / math.sqrt(hd)

    factor = scale * math.log2(math.e)

    def peer(k):
        pair = lax.rem(me // 2 + (k + 1) // 2, n // 2)
        return pair * 2 + lax.rem(me + k + 1, 2)

    barrier = pltpu.get_barrier_semaphore()
    for k in range(n - 1):
        pl.semaphore_signal(barrier, inc=1, device_id={"context": peer(k)}, device_id_type=MESH)

    mine = span(me, rows)
    layout_copy = pltpu.make_async_copy(layout_h, layout_s, local_sem.at[0])
    docs_copy = pltpu.make_async_copy(docs_h, docs_v, local_sem.at[1])
    k_copy = pltpu.make_async_copy(k_h, k_in, local_sem.at[2])
    row_copy = pltpu.make_async_copy(layout_row_h, layout_v, local_sem.at[3])
    v_copy = pltpu.make_async_copy(v_h, vall.at[mine], local_sem.at[4])
    q_copy = pltpu.make_async_copy(q_h, q_in, local_sem.at[5])
    g_copy = pltpu.make_async_copy(g_h, g_in, local_sem.at[6])
    for copy in (layout_copy, docs_copy, k_copy, v_copy, row_copy, q_copy, g_copy):
        copy.start()

    half = hd // 2
    lane = lax.broadcasted_iota(jnp.int32, (1, hd), 1)
    freq = jnp.exp(-(2.0 * lax.rem(lane, half).astype(F32) / hd) * math.log(THETA))
    row_at = lax.broadcasted_iota(jnp.int32, (rows, hd), 0)
    layout_copy.wait()
    first = layout_s[me * rows].astype(F32)
    second = layout_s[me * rows + RUN].astype(F32)
    token = jnp.where(row_at < RUN, row_at.astype(F32) + first, (row_at - RUN).astype(F32) + second)
    token = token[:, :1]
    docs_copy.wait()
    docs = jnp.broadcast_to(docs_v[...], (8, seq))
    lane_at = lax.broadcasted_iota(jnp.int32, (8, seq), 1)
    starts = jnp.where(docs != pltpu.roll(docs, 1, 1), lane_at, 0).astype(F32)[:1]
    start = jnp.max(jnp.where(starts <= token, starts, 0.0), axis=1, keepdims=True)
    angles = (token - start) * freq
    cosine = jnp.cos(angles)
    sine = jnp.where(lane < half, -1.0, 1.0) * jnp.sin(angles)
    cos_ref[...] = cosine
    sin_ref[...] = sine
    k_copy.wait()
    kall[mine] = rotate(k_in[...].astype(F32), cosine, sine).astype(BF16)
    v_copy.wait()

    pl.semaphore_wait(barrier, n - 1)

    def transfer(kind, k, source, target):
        return pltpu.make_async_remote_copy(
            src_ref=source, dst_ref=target,
            send_sem=send_sem.at[kind, k], recv_sem=recv_sem.at[kind, k],
            device_id={"context": peer(k)}, device_id_type=MESH)

    def k_send(k):
        return transfer(0, k, kall.at[mine], kall.at[mine])

    def v_send(k):
        return transfer(1, k, vall.at[mine], vall.at[mine])

    def g_send(kind, k):
        return transfer(2 + kind, k, send_buf.at[kind, k], recv_buf.at[kind, k])

    loop(n - 1, lambda k: k_send(n - 2 - k).start())

    row_copy.wait()
    keys = layout_v[...].astype(F32)
    bias_t[...] = jnp.where((keys >= start) & (keys <= token), 0.0, MASKED).T.astype(BF16)
    q_copy.wait()

    def make_q(at):
        here = span(at, chunk)
        cosines, sines = spread(cos_ref, at, chunk, heads), spread(sin_ref, at, chunk, heads)
        qe[here, :hd] = rotate(q_in[here, :].astype(F32), cosines, sines).astype(BF16)
        row = lax.broadcasted_iota(jnp.int32, (chunk, hd), 0) // heads + at * tokens
        col = lax.broadcasted_iota(jnp.int32, (chunk, hd), 1)
        qe[here, hd:] = (row == col).astype(F32).astype(BF16)

    loop(steps, make_q)

    def make_probs(at):
        here = span(at, chunk)
        scores = dot(jnp.concatenate([kall[...], bias_t[...]], axis=1), qe[here, :], 1)
        largest = jnp.max(scores, axis=0, keepdims=True)
        weights = jnp.exp2((scores - largest) * factor)
        total = jnp.sum(weights, axis=0, keepdims=True)
        p_t[:, here] = (weights * (1.0 / total)).astype(BF16)

    loop(n - 1, lambda k: k_send(k).wait_recv())
    loop(n - 1, lambda k: v_send(k).start())
    loop(steps, make_probs)
    g_copy.wait()

    def v_grads(k):
        send_buf[0, k] = dot(p_t[span(peer(k), rows), :], g_in[...]).astype(BF16)
        g_send(0, k).start()

    loop(n - 1, lambda k: v_grads(n - 2 - k))
    loop(n - 1, lambda k: v_send(k).wait_recv())

    def make_ds(at):
        here = span(at, chunk)
        dprobs = dot(vall[...], g_in[here, :], 1)
        p = p_t[:, here].astype(F32)
        delta = jnp.sum(p * dprobs, axis=0, keepdims=True)
        probs[:, here] = (p * (dprobs - delta)).astype(BF16)

    loop(steps, make_ds)

    def k_grads(k):
        send_buf[1, k] = (dot(probs[span(peer(k), rows), :], qe[:, :hd]) * scale).astype(BF16)
        g_send(1, k).start()

    loop(n - 1, lambda k: k_grads(n - 2 - k))
    own_dk = dot(probs[mine, :], qe[:, :hd]) * scale
    own_dv[...] = dot(p_t[mine, :], g_in[...])
    k_t[...] = kall[...].astype(F32).T.astype(BF16)
    v_t[...] = vall[...].astype(F32).T.astype(BF16)

    def make_o(at):
        here = span(at, chunk)
        o_ref[here, :] = dot(v_t[...], p_t[:, here]).T.astype(BF16)

    def make_dq(at):
        here = span(at, chunk)
        grad = dot(k_t[...], probs[:, here]).T * scale
        cosines, sines = spread(cos_ref, at, chunk, heads), spread(sin_ref, at, chunk, heads)
        dq_ref[here, :] = rotate(grad, cosines, -sines).astype(BF16)

    loop(steps, make_o)
    loop(steps, make_dq)

    def collect(kind, own):
        loop(n - 1, lambda k: g_send(kind, k).wait_recv())
        return own + jnp.sum(recv_buf[kind].astype(F32), axis=0)

    dv_ref[...] = collect(0, own_dv[...])
    dk_ref[...] = rotate(collect(1, own_dk), cos_ref[...], -sin_ref[...])

    def finish(k):
        k_send(k).wait_send()
        v_send(k).wait_send()
        g_send(0, k).wait_send()
        g_send(1, k).wait_send()

    loop(n - 1, finish)


def last_kernel(*refs):
    count = len(refs) // 2
    sem = refs[-1]
    copies = [pltpu.make_async_copy(refs[at], refs[count + at], sem.at[at]) for at in range(count)]
    for copy in copies:
        copy.start()
    for copy in copies:
        copy.wait()


def sum_kernel(o_in, dq_in, grad_near, parts, cosine, sine, o_h, dq_h, dk_h, dv_h, dk, dv, sem):
    copies = [pltpu.make_async_copy(source, target, sem.at[at]) for at, (source, target) in enumerate(
        ((o_in, o_h), (dq_in, dq_h), (dv, dv_h), (dk, dk_h)))]
    copies[0].start()
    copies[1].start()

    def total(kind):
        return (grad_near[kind] + sum(parts[3 * kind + at].astype(F32) for at in range(3))).T

    dv[...] = total(0)
    copies[2].start()
    grad = total(1)
    dk[...] = grad * cosine[...] + pltpu.roll(grad, grad.shape[-1] // 2, 1) * sine[...]
    copies[3].start()
    for copy in copies:
        copy.wait()


def body(n, queries, key_heads, value_heads, out_grad, layout, documents):
    rows, heads, hd = queries.shape
    seq = layout.shape[0]
    flat = rows * heads
    hbm = pl.BlockSpec(memory_space=pltpu.HBM)
    vmem = pl.BlockSpec(memory_space=pltpu.VMEM)
    shapes = (
        jax.ShapeDtypeStruct((flat, hd), BF16),
        jax.ShapeDtypeStruct((flat, hd), BF16),
        jax.ShapeDtypeStruct((rows, hd), F32),
        jax.ShapeDtypeStruct((rows, hd), F32),
    )
    operands = [
        pltpu.SMEM((seq,), jnp.int32),
        pltpu.VMEM((1, seq), jnp.int32),
        pltpu.VMEM((1, seq), jnp.int32),
        pltpu.VMEM((flat, hd), BF16),
        pltpu.VMEM((flat, hd), BF16),
    ]
    if n == 4:
        kernel = functools.partial(pair_kernel, heads, 256)
        scratch = operands + [
            pltpu.VMEM((seq, hd), BF16),
            pltpu.VMEM((seq, hd), BF16),
            pltpu.VMEM((seq, 2 * hd), BF16),
            pltpu.VMEM((hd + rows, flat), BF16),
            pltpu.VMEM((hd, flat), BF16),
            pltpu.VMEM((seq, hd), F32),
            pltpu.VMEM((seq, hd), F32),
            pltpu.VMEM((2 * rows, flat), F32),
            pltpu.VMEM((2 * rows, flat), F32),
            pltpu.VMEM((2 * rows, flat), F32),
            pltpu.VMEM((2 * rows, flat), F32),
            pltpu.VMEM((seq, flat), BF16),
            pltpu.VMEM((seq, flat), BF16),
            pltpu.VMEM((16, flat), F32),
            pltpu.VMEM((hd, seq), BF16),
            pltpu.VMEM((hd, seq), BF16),
            pltpu.VMEM((6, hd, rows), BF16),
            pltpu.SemaphoreType.DMA((7,)),
            pltpu.SemaphoreType.DMA((12,)),
            pltpu.SemaphoreType.DMA((12,)),
        ]
    else:
        kernel = functools.partial(ring_kernel, n, heads, 128)
        scratch = operands + [
            pltpu.VMEM((rows, hd), BF16),
            pltpu.VMEM((seq, flat), BF16),
            pltpu.VMEM((hd, seq), BF16),
            pltpu.VMEM((rows, hd), F32),
            pltpu.VMEM((rows, hd), F32),
            pltpu.VMEM((flat, 2 * hd), BF16),
            pltpu.VMEM((seq, hd), BF16),
            pltpu.VMEM((seq, hd), BF16),
            pltpu.VMEM((hd, seq), BF16),
            pltpu.VMEM((seq, flat), BF16),
            pltpu.VMEM((seq, rows), BF16),
            pltpu.VMEM((2, n - 1, rows, hd), BF16),
            pltpu.VMEM((2, n - 1, rows, hd), BF16),
            pltpu.VMEM((rows, hd), F32),
            pltpu.SemaphoreType.DMA((7,)),
            pltpu.SemaphoreType.DMA((4, n - 1)),
            pltpu.SemaphoreType.DMA((4, n - 1)),
        ]
    if n == 4:
        carry = shapes[:2] + (
            jax.ShapeDtypeStruct((2, hd, rows), F32),
            jax.ShapeDtypeStruct((6, hd, rows), BF16),
            jax.ShapeDtypeStruct((rows, hd), F32),
            jax.ShapeDtypeStruct((rows, hd), F32),
        )
        last = sum_kernel
        last_scratch = [pltpu.VMEM((rows, hd), F32), pltpu.VMEM((rows, hd), F32)]
    else:
        carry, last, last_scratch = shapes, last_kernel, []
    carried = pl.pallas_call(
        kernel,
        out_shape=carry,
        in_specs=[hbm] * 7,
        out_specs=(vmem,) * len(carry),
        scratch_shapes=scratch,
        compiler_params=pltpu.CompilerParams(
            collective_id=0, has_side_effects=True, vmem_limit_bytes=(40 if n == 4 else 58) * 1024 * 1024),
    )(*[pltpu.with_memory_space_constraint(operand, pltpu.HBM) for operand in (
        layout, layout.reshape(1, seq), documents.reshape(1, seq),
        queries.reshape(flat, hd), key_heads.reshape(rows, hd), value_heads.reshape(rows, hd),
        out_grad.reshape(flat, hd),
    )])
    out, dq, dk, dv = pl.pallas_call(
        last,
        out_shape=shapes,
        in_specs=[vmem] * len(carry),
        out_specs=(hbm,) * 4,
        scratch_shapes=last_scratch + [pltpu.SemaphoreType.DMA((4,))],
        compiler_params=pltpu.CompilerParams(vmem_limit_bytes=8 * 1024 * 1024),
    )(*carried)
    return (out.reshape(rows, heads, hd), dq.reshape(rows, heads, hd), dk, dv)


def solution(mesh):
    return jax.shard_map(
        functools.partial(body, mesh.shape["context"]),
        mesh=mesh,
        in_specs=(
            P(("dp", "context"), "tensor", None),
            P(("dp", "context"), "tensor", None),
            P(("dp", "context"), "tensor", None),
            P(("dp", "context"), "tensor", None),
            P("dp"),
            P("dp"),
        ),
        out_specs=(
            P(("dp", "context"), "tensor", None),
            P(("dp", "context"), "tensor", None),
            P(("dp", "context"), "tensor"),
            P(("dp", "context"), "tensor"),
        ),
        check_vma=False,
    )
```

```python
import functools
import math

import jax
import jax.numpy as jnp
from jax import lax
from jax.experimental import pallas as pl
from jax.experimental.pallas import tpu as pltpu
from jax.sharding import PartitionSpec as P

THETA = 8000000.0
RUN = 64
MASKED = -1e30
MESH = pl.DeviceIdType.MESH
F32 = jnp.float32
BF16 = jnp.bfloat16


def dot(lhs, rhs, rhs_dim=0):
    return lax.dot_general(lhs, rhs, (((1,), (rhs_dim,)), ((), ())), preferred_element_type=F32)


def sine_cosine(x):
    turns = jnp.floor(x * (2.0 / math.pi) + 0.5)
    r = ((x - turns * 1.5703125) - turns * 4.837512969970703125e-4) - turns * 7.54978995489188216e-8
    z = r * r
    s = r + r * z * (-1.6666654611e-1 + z * (8.3321608736e-3 - z * 1.9515295891e-4))
    c = 1.0 - 0.5 * z + z * z * (4.166664568298827e-2 + z * (-1.388731625493765e-3 + z * 2.443315711809948e-5))
    quarter = turns.astype(jnp.int32)
    odd = (quarter & 1) == 1
    sine = jnp.where(odd, c, s)
    cosine = jnp.where(odd, s, c)
    return (jnp.where((quarter & 2) == 2, -sine, sine), jnp.where(((quarter + 1) & 2) == 2, -cosine, cosine))


def per_token(ref, first, tokens, heads):
    return jnp.concatenate([
        jnp.broadcast_to(ref[first + t:first + t + 1, :], (heads, ref.shape[-1])) for t in range(tokens)], axis=0)


def pair_kernel(heads, chunk, layout_h, layout_row_h, docs_h, q_h, k_h, v_h, g_h,
                o_ref, dq_ref, grad_near, recv_buf, cos_mine, sin_mine,
                layout_s, layout_v, docs_v, q_in, g_in, kraw, vall, kb, q_t, g_t, cos_ref, sin_ref,
                w_near, w_far, dp_near, dp_far, p_t, ds_t, stats, k_t, v_t,
                send_buf,
                local_sem, send_sem, recv_sem):
    n = 4
    me = lax.axis_index("context")
    rows, hd = cos_mine.shape
    seq = n * rows
    half = hd // 2
    tokens = chunk // heads
    steps = rows // tokens
    scale = 1.0 / math.sqrt(hd)
    factor = scale * math.log2(math.e)
    chip, core = me // 2, lax.rem(me, 2)
    partner = chip * 2 + (1 - core)
    far0 = (1 - chip) * 2
    owners = (me, partner, far0, far0 + 1)

    def block(role, count=1):
        return slice(role * rows, (role + count) * rows)

    def part(at):
        return slice(at * chunk, (at + 1) * chunk)

    near, far = block(0, 2), block(2, 2)

    barrier = pltpu.get_barrier_semaphore()
    for peer in (far0, far0 + 1, partner):
        pl.semaphore_signal(barrier, inc=1, device_id={"context": peer}, device_id_type=MESH)

    k_copy = pltpu.make_async_copy(k_h, kraw.at[block(0)], local_sem.at[2])
    v_copy = pltpu.make_async_copy(v_h, vall.at[block(0)], local_sem.at[4])
    layout_copy = pltpu.make_async_copy(layout_h, layout_s, local_sem.at[0])
    docs_copy = pltpu.make_async_copy(docs_h, docs_v, local_sem.at[1])
    row_copy = pltpu.make_async_copy(layout_row_h, layout_v, local_sem.at[3])
    q_copy = pltpu.make_async_copy(q_h, q_in, local_sem.at[5])
    g_copy = pltpu.make_async_copy(g_h, g_in, local_sem.at[6])
    for copy in (k_copy, v_copy, layout_copy, docs_copy, row_copy, q_copy, g_copy):
        copy.start()

    def transfer(at, source, target, to):
        return pltpu.make_async_remote_copy(
            src_ref=source, dst_ref=target, send_sem=send_sem.at[at], recv_sem=recv_sem.at[at],
            device_id={"context": to}, device_id_type=MESH)

    def slot(ref, at):
        return ref.at[pl.ds(pl.multiple_of((2 + at) * rows, rows), rows)]

    def to_far(kind, to, source, target):
        return pltpu.make_async_remote_copy(
            src_ref=source, dst_ref=target, send_sem=send_sem.at[2 * kind + to], recv_sem=recv_sem.at[2 * kind + core],
            device_id={"context": far0 + to}, device_id_type=MESH)

    def from_far(kind, at, target):
        return pltpu.make_async_remote_copy(
            src_ref=target, dst_ref=target, send_sem=send_sem.at[2 * kind], recv_sem=recv_sem.at[2 * kind + at],
            device_id={"context": far0}, device_id_type=MESH)

    k_far = [to_far(0, to, kraw.at[block(0)], slot(kraw, core)) for to in (0, 1)]
    v_far = [to_far(1, to, vall.at[block(0)], slot(vall, core)) for to in (0, 1)]
    dv_far = [to_far(2, to, send_buf.at[1 + to], recv_buf.at[1 + core]) for to in (0, 1)]
    dk_far = [to_far(3, to, send_buf.at[4 + to], recv_buf.at[4 + core]) for to in (0, 1)]
    k_near = transfer(8, kraw.at[block(0)], kraw.at[block(1)], partner)
    v_near = transfer(9, vall.at[block(0)], vall.at[block(1)], partner)
    dv_near = transfer(10, send_buf.at[0], recv_buf.at[0], partner)
    dk_near = transfer(11, send_buf.at[3], recv_buf.at[3], partner)

    for at in range(steps):
        row = lax.broadcasted_iota(jnp.int32, (rows, chunk), 0)
        col = lax.broadcasted_iota(jnp.int32, (rows, chunk), 1) // heads + at * tokens
        q_t[hd:, part(at)] = jnp.where(row == col, 1.0, 0.0).astype(BF16)

    k_copy.wait()
    v_copy.wait()
    pl.semaphore_wait(barrier, n - 1)
    for copy in (k_far[0], k_far[1], k_near, v_near, v_far[0], v_far[1]):
        copy.start()

    lane = lax.broadcasted_iota(jnp.int32, (1, hd), 1)
    low = lane < half
    freq = jnp.exp(-(2.0 * lax.rem(lane, half).astype(F32) / hd) * math.log(THETA))
    within = lax.broadcasted_iota(jnp.int32, (RUN, 1), 0).astype(F32)
    docs_copy.wait()
    docs = jnp.broadcast_to(docs_v[...], (8, seq))
    lane_at = lax.broadcasted_iota(jnp.int32, (8, seq), 1)
    starts = jnp.where(docs != pltpu.roll(docs, 1, 1), lane_at, 0).astype(F32)[:1]
    layout_copy.wait()

    def places(owner):
        found = []
        for run in range(rows // RUN):
            token = within + layout_s[owner * rows + run * RUN].astype(F32)
            start = jnp.max(jnp.where(starts <= token, starts, 0.0), axis=1, keepdims=True)
            found.append((token, start))
        return found

    def tables(found):
        (token_a, start_a), (token_b, start_b) = found
        sine, cosine = sine_cosine(jnp.where(low, token_a - start_a, token_b - start_b) * freq)
        sine_r, cosine_r = pltpu.roll(sine, half, 1), pltpu.roll(cosine, half, 1)
        c = jnp.concatenate([jnp.where(low, cosine, cosine_r), jnp.where(low, cosine_r, cosine)], axis=0)
        s = jnp.concatenate([jnp.where(low, -sine, sine_r), jnp.where(low, -sine_r, sine)], axis=0)
        return c, s

    def rotate(x, c, s):
        return x * c + pltpu.roll(x, half, 1) * s

    def rotate_keys(role, c, s):
        kb[block(role), :hd] = rotate(kraw[block(role), :].astype(F32), c, s).astype(BF16)

    found = places(me)
    c, s = tables(found)
    cos_mine[...] = c
    sin_mine[...] = s
    rotate_keys(0, c, s)
    token = jnp.concatenate([t for t, _ in found], axis=0)
    start = jnp.concatenate([t for _, t in found], axis=0)
    row_copy.wait()
    for role in range(n):
        keys = layout_v[:, pl.ds(pl.multiple_of(owners[role] * rows, rows), rows)].astype(F32)
        kb[block(role), hd:] = jnp.where((keys >= start) & (keys <= token), 0.0, MASKED).T.astype(BF16)
    q_copy.wait()
    for at in range(steps):
        cosines = per_token(cos_mine, at * tokens, tokens, heads)
        sines = per_token(sin_mine, at * tokens, tokens, heads)
        rotated = rotate(q_in[part(at), :].astype(F32), cosines, sines)
        q_t[:hd, part(at)] = rotated.T.astype(BF16)
    g_copy.wait()
    for at in range(steps):
        g_t[:, part(at)] = g_in[part(at), :].astype(F32).T.astype(BF16)
    for role in (1, 2, 3):
        c, s = tables(places(owners[role]))
        cos_ref[block(role), :] = c
        sin_ref[block(role), :] = s

    def score(role, count, w_ref, at, chunk_at):
        here = part(chunk_at)
        scores = dot(kb[block(role, count), :], q_t[:, here])
        largest = jnp.max(scores, axis=0, keepdims=True)
        weights = jnp.exp2((scores - largest) * factor)
        w_ref[:, here] = weights
        stats[3 * at:3 * at + 1, here] = largest
        stats[3 * at + 1:3 * at + 2, here] = jnp.sum(weights, axis=0, keepdims=True)

    def back(role, count, w_ref, dp_ref, at, chunk_at):
        here = part(chunk_at)
        dprobs = dot(vall[block(role, count), :], g_t[:, here])
        dp_ref[:, here] = dprobs
        stats[3 * at + 2:3 * at + 3, here] = jnp.sum(w_ref[:, here] * dprobs, axis=0, keepdims=True)

    def arrived(role):
        rotate_keys(role, cos_ref[block(role), :], sin_ref[block(role), :])

    k_near.wait_recv()
    arrived(1)
    v_near.wait_recv()
    for at in range(steps):
        score(0, 2, w_near, 0, at)
        back(0, 2, w_near, dp_near, 0, at)

    def far_keys(at):
        from_far(0, at, slot(kraw, at)).wait_recv()
        arrived(2 + at)

    def far_score(at, chunk_at):
        here = part(chunk_at)
        scores = dot(kb[block(2 + at), :], q_t[:, here])
        largest = jnp.max(scores, axis=0, keepdims=True)
        weights = jnp.exp2((scores - largest) * factor)
        w_far[block(at), here] = weights
        stats[3 + 3 * at:4 + 3 * at, here] = largest
        stats[4 + 3 * at:5 + 3 * at, here] = jnp.sum(weights, axis=0, keepdims=True)

    def normalize(at, here):
        p = w_far[block(at), here] * stats[12 + at:13 + at, here]
        w_far[block(at), here] = p
        p_t[block(2 + at), here] = p.astype(BF16)

    far_keys(1)
    for at in range(steps):
        far_score(1, at)
    for at in range(steps):
        here = part(at)
        largest = jnp.maximum(stats[0:1, here], stats[6:7, here])
        shrink = [jnp.exp2((stats[b:b + 1, here] - largest) * factor) for b in (0, 6)]
        stats[0:1, here] = largest
        stats[1:2, here] = shrink[0] * stats[1:2, here] + shrink[1] * stats[7:8, here]
        stats[9:10, here] = shrink[0]
        stats[13:14, here] = shrink[1]
    far_keys(0)
    for at in range(steps):
        here = part(at)
        scores = dot(kb[block(2), :], q_t[:, here])
        last = jnp.max(scores, axis=0, keepdims=True)
        weights = jnp.exp2((scores - last) * factor)
        largest = jnp.maximum(stats[0:1, here], last)
        before, after = jnp.exp2((stats[0:1, here] - largest) * factor), jnp.exp2((last - largest) * factor)
        inverse = 1.0 / (before * stats[1:2, here] + after * jnp.sum(weights, axis=0, keepdims=True))
        before = before * inverse
        weight = stats[9:10, here] * before
        stats[9:10, here] = weight
        stats[10:11, here] = weight * stats[2:3, here]
        stats[13:14, here] = stats[13:14, here] * before
        p = weights * (after * inverse)
        w_far[block(0), here] = p
        p_t[block(2), here] = p.astype(BF16)
    send_buf[1] = dot(g_t[...], p_t[block(2), :], 1).astype(BF16)
    dv_far[0].start()
    for at in range(steps):
        normalize(1, part(at))
    send_buf[2] = dot(g_t[...], p_t[block(3), :], 1).astype(BF16)
    dv_far[1].start()

    def far_back(at, here):
        dprobs = dot(vall[block(2 + at), :], g_t[:, here])
        dp_far[block(at), here] = dprobs
        return jnp.sum(w_far[block(at), here] * dprobs, axis=0, keepdims=True)

    from_far(1, 1, slot(vall, 1)).wait_recv()
    for at in range(steps):
        here = part(at)
        stats[10:11, here] = stats[10:11, here] + far_back(1, here)
    from_far(1, 0, slot(vall, 0)).wait_recv()
    for at in range(steps):
        here = part(at)
        stats[11:12, here] = stats[10:11, here] + far_back(0, here)
        ds_t[block(2), here] = (w_far[:rows, here] * (dp_far[:rows, here] - stats[11:12, here])).astype(BF16)
    send_buf[4] = dot(q_t[:hd, :], ds_t[block(2), :], 1).astype(BF16)
    dk_far[0].start()
    for at in range(steps):
        here = part(at)
        ds_t[block(3), here] = (w_far[rows:, here] * (dp_far[rows:, here] - stats[11:12, here])).astype(BF16)
    send_buf[5] = dot(q_t[:hd, :], ds_t[block(3), :], 1).astype(BF16)
    dk_far[1].start()
    for at in range(steps):
        here = part(at)
        p = w_near[:, here] * stats[9:10, here]
        p_t[near, here] = p.astype(BF16)
        ds_t[near, here] = (p * (dp_near[:, here] - stats[11:12, here])).astype(BF16)
    for kind, left, right in ((0, g_t, p_t), (1, q_t.at[:hd], ds_t)):
        grad = dot(left[...], right[near, :], 1)
        send_buf[3 * kind] = grad[:, rows:].astype(BF16)
        (dv_near, dk_near)[kind].start()
        grad_near[kind] = grad[:, :rows]

    k_t[...] = kb[:, :hd].astype(F32).T.astype(BF16)
    v_t[...] = vall[...].astype(F32).T.astype(BF16)
    for at in range(steps):
        o_ref[part(at), :] = dot(v_t[...], p_t[:, part(at)]).T.astype(BF16)
    cos_mine[...] = cos_mine[...] * scale
    sin_mine[...] = sin_mine[...] * -scale
    for at in range(steps):
        cosines = per_token(cos_mine, at * tokens, tokens, heads)
        sines = per_token(sin_mine, at * tokens, tokens, heads)
        dq_ref[part(at), :] = rotate(dot(k_t[...], ds_t[:, part(at)]).T, cosines, sines).astype(BF16)

    dv_near.wait_recv()
    dk_near.wait_recv()
    for kind in (2, 3):
        for at in (0, 1):
            from_far(kind, at, recv_buf.at[3 * (kind - 2) + 1 + at]).wait_recv()
    for copy in (k_near, v_near, dv_near, dk_near, *k_far, *v_far, *dv_far, *dk_far):
        copy.wait_send()


def loop(count, step):
    if count <= 8:
        for index in range(count):
            step(index)
    else:
        lax.fori_loop(0, count, lambda index, _: (step(index), None)[1], None)


def span(at, size):
    start = at * size
    return pl.ds(start if isinstance(at, int) else pl.multiple_of(start, size), size)


def rotate(x, cosine, sine):
    return x * cosine + pltpu.roll(x, x.shape[-1] // 2, 1) * sine


def spread(ref, at, chunk, heads):
    part = ref[span(at, chunk // heads), :]
    return jnp.broadcast_to(part[:, None, :], (chunk // heads, heads, part.shape[-1])).reshape(chunk, -1)


def ring_kernel(n, heads, chunk, layout_h, layout_row_h, docs_h, q_h, k_h, v_h, g_h,
                o_ref, dq_ref, dk_ref, dv_ref,
                layout_s, layout_v, docs_v, q_in, g_in, k_in, probs, k_t, cos_ref, sin_ref, qe, kall, vall, v_t, p_t, bias_t,
                send_buf, recv_buf, own_dv, local_sem, send_sem, recv_sem):
    me = lax.axis_index("context")
    rows, hd = k_in.shape
    seq = rows * n
    flat = rows * heads
    tokens = chunk // heads
    steps = flat // chunk
    scale = 1.0 / math.sqrt(hd)

    factor = scale * math.log2(math.e)

    def peer(k):
        pair = lax.rem(me // 2 + (k + 1) // 2, n // 2)
        return pair * 2 + lax.rem(me + k + 1, 2)

    barrier = pltpu.get_barrier_semaphore()
    for k in range(n - 1):
        pl.semaphore_signal(barrier, inc=1, device_id={"context": peer(k)}, device_id_type=MESH)

    mine = span(me, rows)
    layout_copy = pltpu.make_async_copy(layout_h, layout_s, local_sem.at[0])
    docs_copy = pltpu.make_async_copy(docs_h, docs_v, local_sem.at[1])
    k_copy = pltpu.make_async_copy(k_h, k_in, local_sem.at[2])
    row_copy = pltpu.make_async_copy(layout_row_h, layout_v, local_sem.at[3])
    v_copy = pltpu.make_async_copy(v_h, vall.at[mine], local_sem.at[4])
    q_copy = pltpu.make_async_copy(q_h, q_in, local_sem.at[5])
    g_copy = pltpu.make_async_copy(g_h, g_in, local_sem.at[6])
    for copy in (layout_copy, docs_copy, k_copy, v_copy, row_copy, q_copy, g_copy):
        copy.start()

    half = hd // 2
    lane = lax.broadcasted_iota(jnp.int32, (1, hd), 1)
    freq = jnp.exp(-(2.0 * lax.rem(lane, half).astype(F32) / hd) * math.log(THETA))
    row_at = lax.broadcasted_iota(jnp.int32, (rows, hd), 0)
    layout_copy.wait()
    first = layout_s[me * rows].astype(F32)
    second = layout_s[me * rows + RUN].astype(F32)
    token = jnp.where(row_at < RUN, row_at.astype(F32) + first, (row_at - RUN).astype(F32) + second)
    token = token[:, :1]
    docs_copy.wait()
    docs = jnp.broadcast_to(docs_v[...], (8, seq))
    lane_at = lax.broadcasted_iota(jnp.int32, (8, seq), 1)
    starts = jnp.where(docs != pltpu.roll(docs, 1, 1), lane_at, 0).astype(F32)[:1]
    start = jnp.max(jnp.where(starts <= token, starts, 0.0), axis=1, keepdims=True)
    angles = (token - start) * freq
    cosine = jnp.cos(angles)
    sine = jnp.where(lane < half, -1.0, 1.0) * jnp.sin(angles)
    cos_ref[...] = cosine
    sin_ref[...] = sine
    k_copy.wait()
    kall[mine] = rotate(k_in[...].astype(F32), cosine, sine).astype(BF16)
    v_copy.wait()

    pl.semaphore_wait(barrier, n - 1)

    def transfer(kind, k, source, target):
        return pltpu.make_async_remote_copy(
            src_ref=source, dst_ref=target,
            send_sem=send_sem.at[kind, k], recv_sem=recv_sem.at[kind, k],
            device_id={"context": peer(k)}, device_id_type=MESH)

    def k_send(k):
        return transfer(0, k, kall.at[mine], kall.at[mine])

    def v_send(k):
        return transfer(1, k, vall.at[mine], vall.at[mine])

    def g_send(kind, k):
        return transfer(2 + kind, k, send_buf.at[kind, k], recv_buf.at[kind, k])

    loop(n - 1, lambda k: k_send(n - 2 - k).start())

    row_copy.wait()
    keys = layout_v[...].astype(F32)
    bias_t[...] = jnp.where((keys >= start) & (keys <= token), 0.0, MASKED).T.astype(BF16)
    q_copy.wait()

    def make_q(at):
        here = span(at, chunk)
        cosines, sines = spread(cos_ref, at, chunk, heads), spread(sin_ref, at, chunk, heads)
        qe[here, :hd] = rotate(q_in[here, :].astype(F32), cosines, sines).astype(BF16)
        row = lax.broadcasted_iota(jnp.int32, (chunk, hd), 0) // heads + at * tokens
        col = lax.broadcasted_iota(jnp.int32, (chunk, hd), 1)
        qe[here, hd:] = (row == col).astype(F32).astype(BF16)

    loop(steps, make_q)

    def make_probs(at):
        here = span(at, chunk)
        scores = dot(jnp.concatenate([kall[...], bias_t[...]], axis=1), qe[here, :], 1)
        largest = jnp.max(scores, axis=0, keepdims=True)
        weights = jnp.exp2((scores - largest) * factor)
        total = jnp.sum(weights, axis=0, keepdims=True)
        p_t[:, here] = (weights * (1.0 / total)).astype(BF16)

    loop(n - 1, lambda k: k_send(k).wait_recv())
    loop(n - 1, lambda k: v_send(k).start())
    loop(steps, make_probs)
    g_copy.wait()

    def v_grads(k):
        send_buf[0, k] = dot(p_t[span(peer(k), rows), :], g_in[...]).astype(BF16)
        g_send(0, k).start()

    loop(n - 1, lambda k: v_grads(n - 2 - k))
    loop(n - 1, lambda k: v_send(k).wait_recv())

    def make_ds(at):
        here = span(at, chunk)
        dprobs = dot(vall[...], g_in[here, :], 1)
        p = p_t[:, here].astype(F32)
        delta = jnp.sum(p * dprobs, axis=0, keepdims=True)
        probs[:, here] = (p * (dprobs - delta)).astype(BF16)

    loop(steps, make_ds)

    def k_grads(k):
        send_buf[1, k] = (dot(probs[span(peer(k), rows), :], qe[:, :hd]) * scale).astype(BF16)
        g_send(1, k).start()

    loop(n - 1, lambda k: k_grads(n - 2 - k))
    own_dk = dot(probs[mine, :], qe[:, :hd]) * scale
    own_dv[...] = dot(p_t[mine, :], g_in[...])
    k_t[...] = kall[...].astype(F32).T.astype(BF16)
    v_t[...] = vall[...].astype(F32).T.astype(BF16)

    def make_o(at):
        here = span(at, chunk)
        o_ref[here, :] = dot(v_t[...], p_t[:, here]).T.astype(BF16)

    def make_dq(at):
        here = span(at, chunk)
        grad = dot(k_t[...], probs[:, here]).T * scale
        cosines, sines = spread(cos_ref, at, chunk, heads), spread(sin_ref, at, chunk, heads)
        dq_ref[here, :] = rotate(grad, cosines, -sines).astype(BF16)

    loop(steps, make_o)
    loop(steps, make_dq)

    def collect(kind, own):
        loop(n - 1, lambda k: g_send(kind, k).wait_recv())
        return own + jnp.sum(recv_buf[kind].astype(F32), axis=0)

    dv_ref[...] = collect(0, own_dv[...])
    dk_ref[...] = rotate(collect(1, own_dk), cos_ref[...], -sin_ref[...])

    def finish(k):
        k_send(k).wait_send()
        v_send(k).wait_send()
        g_send(0, k).wait_send()
        g_send(1, k).wait_send()

    loop(n - 1, finish)


def last_kernel(*refs):
    count = len(refs) // 2
    sem = refs[-1]
    copies = [pltpu.make_async_copy(refs[at], refs[count + at], sem.at[at]) for at in range(count)]
    for copy in copies:
        copy.start()
    for copy in copies:
        copy.wait()


def sum_kernel(o_in, dq_in, grad_near, parts, cosine, sine, o_h, dq_h, dk_h, dv_h, dk, dv, sem):
    copies = [pltpu.make_async_copy(source, target, sem.at[at]) for at, (source, target) in enumerate(
        ((o_in, o_h), (dq_in, dq_h), (dv, dv_h), (dk, dk_h)))]
    copies[0].start()
    copies[1].start()

    def total(kind):
        return (grad_near[kind] + sum(parts[3 * kind + at].astype(F32) for at in range(3))).T

    dv[...] = total(0)
    copies[2].start()
    grad = total(1)
    dk[...] = grad * cosine[...] + pltpu.roll(grad, grad.shape[-1] // 2, 1) * sine[...]
    copies[3].start()
    for copy in copies:
        copy.wait()


def body(n, queries, key_heads, value_heads, out_grad, layout, documents):
    rows, heads, hd = queries.shape
    seq = layout.shape[0]
    flat = rows * heads
    hbm = pl.BlockSpec(memory_space=pltpu.HBM)
    vmem = pl.BlockSpec(memory_space=pltpu.VMEM)
    shapes = (
        jax.ShapeDtypeStruct((flat, hd), BF16),
        jax.ShapeDtypeStruct((flat, hd), BF16),
        jax.ShapeDtypeStruct((rows, hd), F32),
        jax.ShapeDtypeStruct((rows, hd), F32),
    )
    operands = [
        pltpu.SMEM((seq,), jnp.int32),
        pltpu.VMEM((1, seq), jnp.int32),
        pltpu.VMEM((1, seq), jnp.int32),
        pltpu.VMEM((flat, hd), BF16),
        pltpu.VMEM((flat, hd), BF16),
    ]
    if n == 4:
        kernel = functools.partial(pair_kernel, heads, 256)
        scratch = operands + [
            pltpu.VMEM((seq, hd), BF16),
            pltpu.VMEM((seq, hd), BF16),
            pltpu.VMEM((seq, 2 * hd), BF16),
            pltpu.VMEM((hd + rows, flat), BF16),
            pltpu.VMEM((hd, flat), BF16),
            pltpu.VMEM((seq, hd), F32),
            pltpu.VMEM((seq, hd), F32),
            pltpu.VMEM((2 * rows, flat), F32),
            pltpu.VMEM((2 * rows, flat), F32),
            pltpu.VMEM((2 * rows, flat), F32),
            pltpu.VMEM((2 * rows, flat), F32),
            pltpu.VMEM((seq, flat), BF16),
            pltpu.VMEM((seq, flat), BF16),
            pltpu.VMEM((16, flat), F32),
            pltpu.VMEM((hd, seq), BF16),
            pltpu.VMEM((hd, seq), BF16),
            pltpu.VMEM((6, hd, rows), BF16),
            pltpu.SemaphoreType.DMA((7,)),
            pltpu.SemaphoreType.DMA((12,)),
            pltpu.SemaphoreType.DMA((12,)),
        ]
    else:
        kernel = functools.partial(ring_kernel, n, heads, 128)
        scratch = operands + [
            pltpu.VMEM((rows, hd), BF16),
            pltpu.VMEM((seq, flat), BF16),
            pltpu.VMEM((hd, seq), BF16),
            pltpu.VMEM((rows, hd), F32),
            pltpu.VMEM((rows, hd), F32),
            pltpu.VMEM((flat, 2 * hd), BF16),
            pltpu.VMEM((seq, hd), BF16),
            pltpu.VMEM((seq, hd), BF16),
            pltpu.VMEM((hd, seq), BF16),
            pltpu.VMEM((seq, flat), BF16),
            pltpu.VMEM((seq, rows), BF16),
            pltpu.VMEM((2, n - 1, rows, hd), BF16),
            pltpu.VMEM((2, n - 1, rows, hd), BF16),
            pltpu.VMEM((rows, hd), F32),
            pltpu.SemaphoreType.DMA((7,)),
            pltpu.SemaphoreType.DMA((4, n - 1)),
            pltpu.SemaphoreType.DMA((4, n - 1)),
        ]
    if n == 4:
        carry = shapes[:2] + (
            jax.ShapeDtypeStruct((2, hd, rows), F32),
            jax.ShapeDtypeStruct((6, hd, rows), BF16),
            jax.ShapeDtypeStruct((rows, hd), F32),
            jax.ShapeDtypeStruct((rows, hd), F32),
        )
        last = sum_kernel
        last_scratch = [pltpu.VMEM((rows, hd), F32), pltpu.VMEM((rows, hd), F32)]
    else:
        carry, last, last_scratch = shapes, last_kernel, []
    carried = pl.pallas_call(
        kernel,
        out_shape=carry,
        in_specs=[hbm] * 7,
        out_specs=(vmem,) * len(carry),
        scratch_shapes=scratch,
        compiler_params=pltpu.CompilerParams(
            collective_id=0, has_side_effects=True, vmem_limit_bytes=(40 if n == 4 else 58) * 1024 * 1024),
    )(*[pltpu.with_memory_space_constraint(operand, pltpu.HBM) for operand in (
        layout, layout.reshape(1, seq), documents.reshape(1, seq),
        queries.reshape(flat, hd), key_heads.reshape(rows, hd), value_heads.reshape(rows, hd),
        out_grad.reshape(flat, hd),
    )])
    out, dq, dk, dv = pl.pallas_call(
        last,
        out_shape=shapes,
        in_specs=[vmem] * len(carry),
        out_specs=(hbm,) * 4,
        scratch_shapes=last_scratch + [pltpu.SemaphoreType.DMA((4,))],
        compiler_params=pltpu.CompilerParams(vmem_limit_bytes=8 * 1024 * 1024),
    )(*carried)
    return (out.reshape(rows, heads, hd), dq.reshape(rows, heads, hd), dk, dv)


def solution(mesh):
    return jax.shard_map(
        functools.partial(body, mesh.shape["context"]),
        mesh=mesh,
        in_specs=(
            P(("dp", "context"), "tensor", None),
            P(("dp", "context"), "tensor", None),
            P(("dp", "context"), "tensor", None),
            P(("dp", "context"), "tensor", None),
            P("dp"),
            P("dp"),
        ),
        out_specs=(
            P(("dp", "context"), "tensor", None),
            P(("dp", "context"), "tensor", None),
            P(("dp", "context"), "tensor"),
            P(("dp", "context"), "tensor"),
        ),
        check_vma=False,
    )
```

```python
import functools
import math

import jax
import jax.numpy as jnp
from jax import lax
from jax.experimental import pallas as pl
from jax.experimental.pallas import tpu as pltpu
from jax.sharding import PartitionSpec as P

THETA = 8000000.0
RUN = 64
MASKED = -1e30
MESH = pl.DeviceIdType.MESH
F32 = jnp.float32
BF16 = jnp.bfloat16


def dot(lhs, rhs, rhs_dim=0):
    return lax.dot_general(lhs, rhs, (((1,), (rhs_dim,)), ((), ())), preferred_element_type=F32)


def sine_cosine(x):
    turns = jnp.floor(x * (2.0 / math.pi) + 0.5)
    r = ((x - turns * 1.5703125) - turns * 4.837512969970703125e-4) - turns * 7.54978995489188216e-8
    z = r * r
    s = r + r * z * (-1.6666654611e-1 + z * (8.3321608736e-3 - z * 1.9515295891e-4))
    c = 1.0 - 0.5 * z + z * z * (4.166664568298827e-2 + z * (-1.388731625493765e-3 + z * 2.443315711809948e-5))
    quarter = turns.astype(jnp.int32)
    odd = (quarter & 1) == 1
    sine = jnp.where(odd, c, s)
    cosine = jnp.where(odd, s, c)
    return (jnp.where((quarter & 2) == 2, -sine, sine), jnp.where(((quarter + 1) & 2) == 2, -cosine, cosine))


def per_token(ref, first, tokens, heads):
    return jnp.concatenate([
        jnp.broadcast_to(ref[first + t:first + t + 1, :], (heads, ref.shape[-1])) for t in range(tokens)], axis=0)


def pair_kernel(heads, chunk, layout_h, layout_row_h, docs_h, q_h, k_h, v_h, g_h,
                o_ref, dq_ref, grad_near, recv_buf, cos_mine, sin_mine,
                layout_s, layout_v, docs_v, q_in, g_in, kraw, vall, kb, q_t, g_t, cos_ref, sin_ref,
                w_near, w_far, dp_near, dp_far, p_t, ds_t, stats, k_t, v_t,
                send_buf,
                local_sem, send_sem, recv_sem):
    n = 4
    me = lax.axis_index("context")
    rows, hd = cos_mine.shape
    seq = n * rows
    half = hd // 2
    tokens = chunk // heads
    steps = rows // tokens
    scale = 1.0 / math.sqrt(hd)
    factor = scale * math.log2(math.e)
    chip, core = me // 2, lax.rem(me, 2)
    partner = chip * 2 + (1 - core)
    far0 = (1 - chip) * 2
    owners = (me, partner, far0, far0 + 1)

    def block(role, count=1):
        return slice(role * rows, (role + count) * rows)

    def part(at):
        return slice(at * chunk, (at + 1) * chunk)

    near, far = block(0, 2), block(2, 2)

    barrier = pltpu.get_barrier_semaphore()
    for peer in (far0, far0 + 1, partner):
        pl.semaphore_signal(barrier, inc=1, device_id={"context": peer}, device_id_type=MESH)

    k_copy = pltpu.make_async_copy(k_h, kraw.at[block(0)], local_sem.at[2])
    v_copy = pltpu.make_async_copy(v_h, vall.at[block(0)], local_sem.at[4])
    layout_copy = pltpu.make_async_copy(layout_h, layout_s, local_sem.at[0])
    docs_copy = pltpu.make_async_copy(docs_h, docs_v, local_sem.at[1])
    row_copy = pltpu.make_async_copy(layout_row_h, layout_v, local_sem.at[3])
    q_copy = pltpu.make_async_copy(q_h, q_in, local_sem.at[5])
    g_copy = pltpu.make_async_copy(g_h, g_in, local_sem.at[6])
    for copy in (k_copy, v_copy, layout_copy, docs_copy, row_copy, q_copy, g_copy):
        copy.start()

    def transfer(at, source, target, to):
        return pltpu.make_async_remote_copy(
            src_ref=source, dst_ref=target, send_sem=send_sem.at[at], recv_sem=recv_sem.at[at],
            device_id={"context": to}, device_id_type=MESH)

    def slot(ref, at):
        return ref.at[pl.ds(pl.multiple_of((2 + at) * rows, rows), rows)]

    def to_far(kind, to, source, target):
        return pltpu.make_async_remote_copy(
            src_ref=source, dst_ref=target, send_sem=send_sem.at[2 * kind + to], recv_sem=recv_sem.at[2 * kind + core],
            device_id={"context": far0 + to}, device_id_type=MESH)

    def from_far(kind, at, target):
        return pltpu.make_async_remote_copy(
            src_ref=target, dst_ref=target, send_sem=send_sem.at[2 * kind], recv_sem=recv_sem.at[2 * kind + at],
            device_id={"context": far0}, device_id_type=MESH)

    k_far = [to_far(0, to, kraw.at[block(0)], slot(kraw, core)) for to in (0, 1)]
    v_far = [to_far(1, to, vall.at[block(0)], slot(vall, core)) for to in (0, 1)]
    dv_far = [to_far(2, to, send_buf.at[1 + to], recv_buf.at[1 + core]) for to in (0, 1)]
    dk_far = [to_far(3, to, send_buf.at[4 + to], recv_buf.at[4 + core]) for to in (0, 1)]
    k_near = transfer(8, kraw.at[block(0)], kraw.at[block(1)], partner)
    v_near = transfer(9, vall.at[block(0)], vall.at[block(1)], partner)
    dv_near = transfer(10, send_buf.at[0], recv_buf.at[0], partner)
    dk_near = transfer(11, send_buf.at[3], recv_buf.at[3], partner)

    for at in range(steps):
        row = lax.broadcasted_iota(jnp.int32, (rows, chunk), 0)
        col = lax.broadcasted_iota(jnp.int32, (rows, chunk), 1) // heads + at * tokens
        q_t[hd:, part(at)] = jnp.where(row == col, 1.0, 0.0).astype(BF16)

    k_copy.wait()
    v_copy.wait()
    pl.semaphore_wait(barrier, n - 1)
    for copy in (k_far[0], k_far[1], k_near, v_near, v_far[0], v_far[1]):
        copy.start()

    lane = lax.broadcasted_iota(jnp.int32, (1, hd), 1)
    low = lane < half
    freq = jnp.exp(-(2.0 * lax.rem(lane, half).astype(F32) / hd) * math.log(THETA))
    within = lax.broadcasted_iota(jnp.int32, (RUN, 1), 0).astype(F32)
    docs_copy.wait()
    docs = jnp.broadcast_to(docs_v[...], (8, seq))
    lane_at = lax.broadcasted_iota(jnp.int32, (8, seq), 1)
    starts = jnp.where(docs != pltpu.roll(docs, 1, 1), lane_at, 0).astype(F32)[:1]
    layout_copy.wait()

    def places(owner):
        found = []
        for run in range(rows // RUN):
            token = within + layout_s[owner * rows + run * RUN].astype(F32)
            start = jnp.max(jnp.where(starts <= token, starts, 0.0), axis=1, keepdims=True)
            found.append((token, start))
        return found

    def tables(found):
        (token_a, start_a), (token_b, start_b) = found
        sine, cosine = sine_cosine(jnp.where(low, token_a - start_a, token_b - start_b) * freq)
        sine_r, cosine_r = pltpu.roll(sine, half, 1), pltpu.roll(cosine, half, 1)
        c = jnp.concatenate([jnp.where(low, cosine, cosine_r), jnp.where(low, cosine_r, cosine)], axis=0)
        s = jnp.concatenate([jnp.where(low, -sine, sine_r), jnp.where(low, -sine_r, sine)], axis=0)
        return c, s

    def rotate(x, c, s):
        return x * c + pltpu.roll(x, half, 1) * s

    def rotate_keys(role, c, s):
        kb[block(role), :hd] = rotate(kraw[block(role), :].astype(F32), c, s).astype(BF16)

    found = places(me)
    c, s = tables(found)
    cos_mine[...] = c
    sin_mine[...] = s
    rotate_keys(0, c, s)
    token = jnp.concatenate([t for t, _ in found], axis=0)
    start = jnp.concatenate([t for _, t in found], axis=0)
    row_copy.wait()
    for role in range(n):
        keys = layout_v[:, pl.ds(pl.multiple_of(owners[role] * rows, rows), rows)].astype(F32)
        kb[block(role), hd:] = jnp.where((keys >= start) & (keys <= token), 0.0, MASKED).T.astype(BF16)
    q_copy.wait()
    for at in range(steps):
        cosines = per_token(cos_mine, at * tokens, tokens, heads)
        sines = per_token(sin_mine, at * tokens, tokens, heads)
        rotated = rotate(q_in[part(at), :].astype(F32), cosines, sines)
        q_t[:hd, part(at)] = rotated.T.astype(BF16)
    g_copy.wait()
    for at in range(steps):
        g_t[:, part(at)] = g_in[part(at), :].astype(F32).T.astype(BF16)
    for role in (1, 2, 3):
        c, s = tables(places(owners[role]))
        cos_ref[block(role), :] = c
        sin_ref[block(role), :] = s

    def score(role, count, w_ref, at, chunk_at):
        here = part(chunk_at)
        scores = dot(kb[block(role, count), :], q_t[:, here])
        largest = jnp.max(scores, axis=0, keepdims=True)
        weights = jnp.exp2((scores - largest) * factor)
        w_ref[:, here] = weights
        stats[3 * at:3 * at + 1, here] = largest
        stats[3 * at + 1:3 * at + 2, here] = jnp.sum(weights, axis=0, keepdims=True)

    def back(role, count, w_ref, dp_ref, at, chunk_at):
        here = part(chunk_at)
        dprobs = dot(vall[block(role, count), :], g_t[:, here])
        dp_ref[:, here] = dprobs
        stats[3 * at + 2:3 * at + 3, here] = jnp.sum(w_ref[:, here] * dprobs, axis=0, keepdims=True)

    def arrived(role):
        rotate_keys(role, cos_ref[block(role), :], sin_ref[block(role), :])

    k_near.wait_recv()
    arrived(1)
    v_near.wait_recv()
    for at in range(steps):
        score(0, 2, w_near, 0, at)
        back(0, 2, w_near, dp_near, 0, at)

    def far_keys(at):
        from_far(0, at, slot(kraw, at)).wait_recv()
        arrived(2 + at)

    def far_score(at, chunk_at):
        here = part(chunk_at)
        scores = dot(kb[block(2 + at), :], q_t[:, here])
        largest = jnp.max(scores, axis=0, keepdims=True)
        weights = jnp.exp2((scores - largest) * factor)
        w_far[block(at), here] = weights
        stats[3 + 3 * at:4 + 3 * at, here] = largest
        stats[4 + 3 * at:5 + 3 * at, here] = jnp.sum(weights, axis=0, keepdims=True)

    def normalize(at, here):
        p = w_far[block(at), here] * stats[12 + at:13 + at, here]
        w_far[block(at), here] = p
        p_t[block(2 + at), here] = p.astype(BF16)

    far_keys(1)
    for at in range(steps):
        far_score(1, at)
    for at in range(steps):
        here = part(at)
        largest = jnp.maximum(stats[0:1, here], stats[6:7, here])
        shrink = [jnp.exp2((stats[b:b + 1, here] - largest) * factor) for b in (0, 6)]
        stats[0:1, here] = largest
        stats[1:2, here] = shrink[0] * stats[1:2, here] + shrink[1] * stats[7:8, here]
        stats[9:10, here] = shrink[0]
        stats[13:14, here] = shrink[1]
    far_keys(0)
    for at in range(steps):
        here = part(at)
        scores = dot(kb[block(2), :], q_t[:, here])
        last = jnp.max(scores, axis=0, keepdims=True)
        weights = jnp.exp2((scores - last) * factor)
        largest = jnp.maximum(stats[0:1, here], last)
        before, after = jnp.exp2((stats[0:1, here] - largest) * factor), jnp.exp2((last - largest) * factor)
        inverse = 1.0 / (before * stats[1:2, here] + after * jnp.sum(weights, axis=0, keepdims=True))
        before = before * inverse
        weight = stats[9:10, here] * before
        stats[9:10, here] = weight
        stats[10:11, here] = weight * stats[2:3, here]
        stats[13:14, here] = stats[13:14, here] * before
        p = weights * (after * inverse)
        w_far[block(0), here] = p
        p_t[block(2), here] = p.astype(BF16)
    send_buf[1] = dot(g_t[...], p_t[block(2), :], 1).astype(BF16)
    dv_far[0].start()
    for at in range(steps):
        normalize(1, part(at))
    send_buf[2] = dot(g_t[...], p_t[block(3), :], 1).astype(BF16)
    dv_far[1].start()

    def far_back(at, here):
        dprobs = dot(vall[block(2 + at), :], g_t[:, here])
        dp_far[block(at), here] = dprobs
        return jnp.sum(w_far[block(at), here] * dprobs, axis=0, keepdims=True)

    from_far(1, 1, slot(vall, 1)).wait_recv()
    for at in range(steps):
        here = part(at)
        stats[10:11, here] = stats[10:11, here] + far_back(1, here)
    from_far(1, 0, slot(vall, 0)).wait_recv()
    for at in range(steps):
        here = part(at)
        stats[11:12, here] = stats[10:11, here] + far_back(0, here)
        ds_t[block(2), here] = (w_far[:rows, here] * (dp_far[:rows, here] - stats[11:12, here])).astype(BF16)
    send_buf[4] = dot(q_t[:hd, :], ds_t[block(2), :], 1).astype(BF16)
    dk_far[0].start()
    for at in range(steps):
        here = part(at)
        ds_t[block(3), here] = (w_far[rows:, here] * (dp_far[rows:, here] - stats[11:12, here])).astype(BF16)
    send_buf[5] = dot(q_t[:hd, :], ds_t[block(3), :], 1).astype(BF16)
    dk_far[1].start()
    for at in range(steps):
        here = part(at)
        p = w_near[:, here] * stats[9:10, here]
        p_t[near, here] = p.astype(BF16)
        ds_t[near, here] = (p * (dp_near[:, here] - stats[11:12, here])).astype(BF16)
    for kind, left, right in ((0, g_t, p_t), (1, q_t.at[:hd], ds_t)):
        grad = dot(left[...], right[near, :], 1)
        send_buf[3 * kind] = grad[:, rows:].astype(BF16)
        (dv_near, dk_near)[kind].start()
        grad_near[kind] = grad[:, :rows]

    for copy in (k_near, v_near, *k_far, *v_far):
        copy.wait_send()
    k_t[...] = kb[:, :hd].astype(F32).T.astype(BF16)
    v_t[...] = vall[...].astype(F32).T.astype(BF16)
    for at in range(steps):
        o_ref[part(at), :] = dot(v_t[...], p_t[:, part(at)]).T.astype(BF16)
    cos_mine[...] = cos_mine[...] * scale
    sin_mine[...] = sin_mine[...] * -scale
    for at in range(steps):
        cosines = per_token(cos_mine, at * tokens, tokens, heads)
        sines = per_token(sin_mine, at * tokens, tokens, heads)
        dq_ref[part(at), :] = rotate(dot(k_t[...], ds_t[:, part(at)]).T, cosines, sines).astype(BF16)

    dv_near.wait_recv()
    dk_near.wait_recv()
    for kind in (2, 3):
        for at in (0, 1):
            from_far(kind, at, recv_buf.at[3 * (kind - 2) + 1 + at]).wait_recv()
    for copy in (dv_near, dk_near, *dv_far, *dk_far):
        copy.wait_send()


def loop(count, step):
    if count <= 8:
        for index in range(count):
            step(index)
    else:
        lax.fori_loop(0, count, lambda index, _: (step(index), None)[1], None)


def span(at, size):
    start = at * size
    return pl.ds(start if isinstance(at, int) else pl.multiple_of(start, size), size)


def rotate(x, cosine, sine):
    return x * cosine + pltpu.roll(x, x.shape[-1] // 2, 1) * sine


def spread(ref, at, chunk, heads):
    part = ref[span(at, chunk // heads), :]
    return jnp.broadcast_to(part[:, None, :], (chunk // heads, heads, part.shape[-1])).reshape(chunk, -1)


def ring_kernel(n, heads, chunk, layout_h, layout_row_h, docs_h, q_h, k_h, v_h, g_h,
                o_ref, dq_ref, dk_ref, dv_ref,
                layout_s, layout_v, docs_v, q_in, g_in, k_in, probs, k_t, cos_ref, sin_ref, qe, kall, vall, v_t, p_t, bias_t,
                send_buf, recv_buf, own_dv, local_sem, send_sem, recv_sem):
    me = lax.axis_index("context")
    rows, hd = k_in.shape
    seq = rows * n
    flat = rows * heads
    tokens = chunk // heads
    steps = flat // chunk
    scale = 1.0 / math.sqrt(hd)

    factor = scale * math.log2(math.e)

    def peer(k):
        pair = lax.rem(me // 2 + (k + 1) // 2, n // 2)
        return pair * 2 + lax.rem(me + k + 1, 2)

    barrier = pltpu.get_barrier_semaphore()
    for k in range(n - 1):
        pl.semaphore_signal(barrier, inc=1, device_id={"context": peer(k)}, device_id_type=MESH)

    mine = span(me, rows)
    layout_copy = pltpu.make_async_copy(layout_h, layout_s, local_sem.at[0])
    docs_copy = pltpu.make_async_copy(docs_h, docs_v, local_sem.at[1])
    k_copy = pltpu.make_async_copy(k_h, k_in, local_sem.at[2])
    row_copy = pltpu.make_async_copy(layout_row_h, layout_v, local_sem.at[3])
    v_copy = pltpu.make_async_copy(v_h, vall.at[mine], local_sem.at[4])
    q_copy = pltpu.make_async_copy(q_h, q_in, local_sem.at[5])
    g_copy = pltpu.make_async_copy(g_h, g_in, local_sem.at[6])
    for copy in (layout_copy, docs_copy, k_copy, v_copy, row_copy, q_copy, g_copy):
        copy.start()

    half = hd // 2
    lane = lax.broadcasted_iota(jnp.int32, (1, hd), 1)
    freq = jnp.exp(-(2.0 * lax.rem(lane, half).astype(F32) / hd) * math.log(THETA))
    row_at = lax.broadcasted_iota(jnp.int32, (rows, hd), 0)
    layout_copy.wait()
    first = layout_s[me * rows].astype(F32)
    second = layout_s[me * rows + RUN].astype(F32)
    token = jnp.where(row_at < RUN, row_at.astype(F32) + first, (row_at - RUN).astype(F32) + second)
    token = token[:, :1]
    docs_copy.wait()
    docs = jnp.broadcast_to(docs_v[...], (8, seq))
    lane_at = lax.broadcasted_iota(jnp.int32, (8, seq), 1)
    starts = jnp.where(docs != pltpu.roll(docs, 1, 1), lane_at, 0).astype(F32)[:1]
    start = jnp.max(jnp.where(starts <= token, starts, 0.0), axis=1, keepdims=True)
    angles = (token - start) * freq
    cosine = jnp.cos(angles)
    sine = jnp.where(lane < half, -1.0, 1.0) * jnp.sin(angles)
    cos_ref[...] = cosine
    sin_ref[...] = sine
    k_copy.wait()
    kall[mine] = rotate(k_in[...].astype(F32), cosine, sine).astype(BF16)
    v_copy.wait()

    pl.semaphore_wait(barrier, n - 1)

    def transfer(kind, k, source, target):
        return pltpu.make_async_remote_copy(
            src_ref=source, dst_ref=target,
            send_sem=send_sem.at[kind, k], recv_sem=recv_sem.at[kind, k],
            device_id={"context": peer(k)}, device_id_type=MESH)

    def k_send(k):
        return transfer(0, k, kall.at[mine], kall.at[mine])

    def v_send(k):
        return transfer(1, k, vall.at[mine], vall.at[mine])

    def g_send(kind, k):
        return transfer(2 + kind, k, send_buf.at[kind, k], recv_buf.at[kind, k])

    loop(n - 1, lambda k: k_send(n - 2 - k).start())

    row_copy.wait()
    keys = layout_v[...].astype(F32)
    bias_t[...] = jnp.where((keys >= start) & (keys <= token), 0.0, MASKED).T.astype(BF16)
    q_copy.wait()

    def make_q(at):
        here = span(at, chunk)
        cosines, sines = spread(cos_ref, at, chunk, heads), spread(sin_ref, at, chunk, heads)
        qe[here, :hd] = rotate(q_in[here, :].astype(F32), cosines, sines).astype(BF16)
        row = lax.broadcasted_iota(jnp.int32, (chunk, hd), 0) // heads + at * tokens
        col = lax.broadcasted_iota(jnp.int32, (chunk, hd), 1)
        qe[here, hd:] = (row == col).astype(F32).astype(BF16)

    loop(steps, make_q)

    def make_probs(at):
        here = span(at, chunk)
        scores = dot(jnp.concatenate([kall[...], bias_t[...]], axis=1), qe[here, :], 1)
        largest = jnp.max(scores, axis=0, keepdims=True)
        weights = jnp.exp2((scores - largest) * factor)
        total = jnp.sum(weights, axis=0, keepdims=True)
        p_t[:, here] = (weights * (1.0 / total)).astype(BF16)

    loop(n - 1, lambda k: k_send(k).wait_recv())
    loop(n - 1, lambda k: v_send(k).start())
    loop(steps, make_probs)
    g_copy.wait()

    def v_grads(k):
        send_buf[0, k] = dot(p_t[span(peer(k), rows), :], g_in[...]).astype(BF16)
        g_send(0, k).start()

    loop(n - 1, lambda k: v_grads(n - 2 - k))
    loop(n - 1, lambda k: v_send(k).wait_recv())

    def make_ds(at):
        here = span(at, chunk)
        dprobs = dot(vall[...], g_in[here, :], 1)
        p = p_t[:, here].astype(F32)
        delta = jnp.sum(p * dprobs, axis=0, keepdims=True)
        probs[:, here] = (p * (dprobs - delta)).astype(BF16)

    loop(steps, make_ds)

    def k_grads(k):
        send_buf[1, k] = (dot(probs[span(peer(k), rows), :], qe[:, :hd]) * scale).astype(BF16)
        g_send(1, k).start()

    loop(n - 1, lambda k: k_grads(n - 2 - k))
    own_dk = dot(probs[mine, :], qe[:, :hd]) * scale
    own_dv[...] = dot(p_t[mine, :], g_in[...])
    k_t[...] = kall[...].astype(F32).T.astype(BF16)
    v_t[...] = vall[...].astype(F32).T.astype(BF16)

    def make_o(at):
        here = span(at, chunk)
        o_ref[here, :] = dot(v_t[...], p_t[:, here]).T.astype(BF16)

    def make_dq(at):
        here = span(at, chunk)
        grad = dot(k_t[...], probs[:, here]).T * scale
        cosines, sines = spread(cos_ref, at, chunk, heads), spread(sin_ref, at, chunk, heads)
        dq_ref[here, :] = rotate(grad, cosines, -sines).astype(BF16)

    loop(steps, make_o)
    loop(steps, make_dq)

    def collect(kind, own):
        loop(n - 1, lambda k: g_send(kind, k).wait_recv())
        return own + jnp.sum(recv_buf[kind].astype(F32), axis=0)

    dv_ref[...] = collect(0, own_dv[...])
    dk_ref[...] = rotate(collect(1, own_dk), cos_ref[...], -sin_ref[...])

    def finish(k):
        k_send(k).wait_send()
        v_send(k).wait_send()
        g_send(0, k).wait_send()
        g_send(1, k).wait_send()

    loop(n - 1, finish)


def last_kernel(*refs):
    count = len(refs) // 2
    sem = refs[-1]
    copies = [pltpu.make_async_copy(refs[at], refs[count + at], sem.at[at]) for at in range(count)]
    for copy in copies:
        copy.start()
    for copy in copies:
        copy.wait()


def sum_kernel(o_in, dq_in, grad_near, parts, cosine, sine, o_h, dq_h, dk_h, dv_h, dk, dv, sem):
    copies = [pltpu.make_async_copy(source, target, sem.at[at]) for at, (source, target) in enumerate(
        ((o_in, o_h), (dq_in, dq_h), (dv, dv_h), (dk, dk_h)))]
    copies[0].start()
    copies[1].start()

    def total(kind):
        return (grad_near[kind] + sum(parts[3 * kind + at].astype(F32) for at in range(3))).T

    dv[...] = total(0)
    copies[2].start()
    grad = total(1)
    dk[...] = grad * cosine[...] + pltpu.roll(grad, grad.shape[-1] // 2, 1) * sine[...]
    copies[3].start()
    for copy in copies:
        copy.wait()


def body(n, queries, key_heads, value_heads, out_grad, layout, documents):
    rows, heads, hd = queries.shape
    seq = layout.shape[0]
    flat = rows * heads
    hbm = pl.BlockSpec(memory_space=pltpu.HBM)
    vmem = pl.BlockSpec(memory_space=pltpu.VMEM)
    shapes = (
        jax.ShapeDtypeStruct((flat, hd), BF16),
        jax.ShapeDtypeStruct((flat, hd), BF16),
        jax.ShapeDtypeStruct((rows, hd), F32),
        jax.ShapeDtypeStruct((rows, hd), F32),
    )
    operands = [
        pltpu.SMEM((seq,), jnp.int32),
        pltpu.VMEM((1, seq), jnp.int32),
        pltpu.VMEM((1, seq), jnp.int32),
        pltpu.VMEM((flat, hd), BF16),
        pltpu.VMEM((flat, hd), BF16),
    ]
    if n == 4:
        kernel = functools.partial(pair_kernel, heads, 256)
        scratch = operands + [
            pltpu.VMEM((seq, hd), BF16),
            pltpu.VMEM((seq, hd), BF16),
            pltpu.VMEM((seq, 2 * hd), BF16),
            pltpu.VMEM((hd + rows, flat), BF16),
            pltpu.VMEM((hd, flat), BF16),
            pltpu.VMEM((seq, hd), F32),
            pltpu.VMEM((seq, hd), F32),
            pltpu.VMEM((2 * rows, flat), F32),
            pltpu.VMEM((2 * rows, flat), F32),
            pltpu.VMEM((2 * rows, flat), F32),
            pltpu.VMEM((2 * rows, flat), F32),
            pltpu.VMEM((seq, flat), BF16),
            pltpu.VMEM((seq, flat), BF16),
            pltpu.VMEM((16, flat), F32),
            pltpu.VMEM((hd, seq), BF16),
            pltpu.VMEM((hd, seq), BF16),
            pltpu.VMEM((6, hd, rows), BF16),
            pltpu.SemaphoreType.DMA((7,)),
            pltpu.SemaphoreType.DMA((12,)),
            pltpu.SemaphoreType.DMA((12,)),
        ]
    else:
        kernel = functools.partial(ring_kernel, n, heads, 128)
        scratch = operands + [
            pltpu.VMEM((rows, hd), BF16),
            pltpu.VMEM((seq, flat), BF16),
            pltpu.VMEM((hd, seq), BF16),
            pltpu.VMEM((rows, hd), F32),
            pltpu.VMEM((rows, hd), F32),
            pltpu.VMEM((flat, 2 * hd), BF16),
            pltpu.VMEM((seq, hd), BF16),
            pltpu.VMEM((seq, hd), BF16),
            pltpu.VMEM((hd, seq), BF16),
            pltpu.VMEM((seq, flat), BF16),
            pltpu.VMEM((seq, rows), BF16),
            pltpu.VMEM((2, n - 1, rows, hd), BF16),
            pltpu.VMEM((2, n - 1, rows, hd), BF16),
            pltpu.VMEM((rows, hd), F32),
            pltpu.SemaphoreType.DMA((7,)),
            pltpu.SemaphoreType.DMA((4, n - 1)),
            pltpu.SemaphoreType.DMA((4, n - 1)),
        ]
    if n == 4:
        carry = shapes[:2] + (
            jax.ShapeDtypeStruct((2, hd, rows), F32),
            jax.ShapeDtypeStruct((6, hd, rows), BF16),
            jax.ShapeDtypeStruct((rows, hd), F32),
            jax.ShapeDtypeStruct((rows, hd), F32),
        )
        last = sum_kernel
        last_scratch = [pltpu.VMEM((rows, hd), F32), pltpu.VMEM((rows, hd), F32)]
    else:
        carry, last, last_scratch = shapes, last_kernel, []
    carried = pl.pallas_call(
        kernel,
        out_shape=carry,
        in_specs=[hbm] * 7,
        out_specs=(vmem,) * len(carry),
        scratch_shapes=scratch,
        compiler_params=pltpu.CompilerParams(
            collective_id=0, has_side_effects=True, vmem_limit_bytes=(40 if n == 4 else 58) * 1024 * 1024),
    )(*[pltpu.with_memory_space_constraint(operand, pltpu.HBM) for operand in (
        layout, layout.reshape(1, seq), documents.reshape(1, seq),
        queries.reshape(flat, hd), key_heads.reshape(rows, hd), value_heads.reshape(rows, hd),
        out_grad.reshape(flat, hd),
    )])
    out, dq, dk, dv = pl.pallas_call(
        last,
        out_shape=shapes,
        in_specs=[vmem] * len(carry),
        out_specs=(hbm,) * 4,
        scratch_shapes=last_scratch + [pltpu.SemaphoreType.DMA((4,))],
        compiler_params=pltpu.CompilerParams(vmem_limit_bytes=8 * 1024 * 1024),
    )(*carried)
    return (out.reshape(rows, heads, hd), dq.reshape(rows, heads, hd), dk, dv)


def solution(mesh):
    return jax.shard_map(
        functools.partial(body, mesh.shape["context"]),
        mesh=mesh,
        in_specs=(
            P(("dp", "context"), "tensor", None),
            P(("dp", "context"), "tensor", None),
            P(("dp", "context"), "tensor", None),
            P(("dp", "context"), "tensor", None),
            P("dp"),
            P("dp"),
        ),
        out_specs=(
            P(("dp", "context"), "tensor", None),
            P(("dp", "context"), "tensor", None),
            P(("dp", "context"), "tensor"),
            P(("dp", "context"), "tensor"),
        ),
        check_vma=False,
    )
```
